128 devices in a mesh: row: 8 (over x_lo, z), col: 16 (over x_hi, y, core).
Axes of the slice: x: 4 (x_hi: 2, x_lo: 2; x = x_hi * 2 + x_lo), y: 4, z: 4, core: 2. Of those that a mesh axis runs over, the one named last changes fastest.
Arguments:
- tokens: bfloat16 [2048, 4096], P('row', 'col'), may hold values from -6 to 6
- norm_gain: float32 [4096], replicated, may hold values from 0.1 to 1.9
- expert_ids: int32 [2048, 2], P('row'), may hold values from 0 to 7, all different within a row; in each aligned block of 256 rows (0 to 255, 256 to 511, ...) at most 128 rows name the same one
- gate_weights: float32 [2048, 2], P('row'), may hold values from 0.1 to 1
- w_gate: bfloat16 [8, 4096, 14336], P('row', None, 'col'), may hold values from -0.09375 to 0.09375
- w_up: bfloat16 [8, 4096, 14336], P('row', None, 'col'), may hold values from -0.09375 to 0.09375
- w_down: bfloat16 [8, 14336, 4096], P('row', 'col'), may hold values from -0.046875 to 0.046875
Outputs:
- layer_output: bfloat16 [2048, 4096], P('row', 'col')
The draws below stay inside these ranges and needn't reach their ends.
Inputs may be any that keep to these rules, and one draw needn't show every extreme that they name: `expert_ids`: the 2 experts of a token differ. In each aligned block of 256 tokens no expert is chosen by more than 128 tokens, a bound that some block reaches.
All inputs are finite; a program needn't handle non-finite values.
Results may differ from the reference program's by a relative error of at most 0.0043.
Values may be sent and summed in bfloat16 or wider, within the bound.
A program may use at most 128 MiB of HBM per device.

```python
import math
import jax
import jax.numpy as jnp
import numpy as np
from jax import lax

D = 4096
FF = 14336
EXPERTS = 8
TOP = 2
TOK_ROW = 256
CAP = 128
TOKENS = 2048


def level_of(key, dims, shards, low, top_value):
    level = 1.0
    for dim, blocks in shards:
        draws = jax.random.uniform(jax.random.fold_in(jax.random.fold_in(key, 6), dim), (blocks,), jnp.float32, low / len(shards), top_value / len(shards))
        level = level * jnp.repeat(jnp.exp(draws), dims[dim] // blocks).reshape((-1,) + (1,) * (len(dims) - 1 - dim))
    return level


def deal_out(rng, own, number, rows, number_of, top, most, skew):
    sequence = jax.random.permutation(rng, number_of)
    packed, common = load_shares(number_of, rows * top, most, skew, True), load_shares(number_of, rows * top, most, skew, False)
    places = jnp.arange(number_of)

    def named(lengths, offset_by):
        used = int((lengths > 0).sum())
        fixed = max(1, used // 4)
        moved = fixed + (places - fixed + offset_by * (used - fixed)) % max(1, number_of - fixed)
        return jnp.zeros((number_of,), jnp.int32).at[sequence[jnp.where(places < fixed, places, moved)]].set(jnp.asarray(lengths, jnp.int32))

    lengths = jnp.where(number % 4 == 0, named(packed, number // 4), named(common, number - number // 4 - 1))
    mixed = jax.random.permutation(jax.random.fold_in(own, 3), number_of)
    donor, sink = mixed[0:number_of // 2 * 2:2], mixed[1:number_of // 2 * 2:2]
    room = jnp.minimum(lengths[donor] - 1, most - lengths[sink]) // 2
    room = jnp.where((donor == sequence[0]) | (sink == sequence[0]) | (lengths[sink] == 0), 0, jnp.maximum(room, 0))
    moved = jax.random.randint(jax.random.fold_in(own, 4), (number_of // 2,), 0, 1 << 20) % (room + 1)
    lengths = lengths.at[donor].add(-moved).at[sink].add(moved)
    items = jnp.searchsorted(jnp.cumsum(lengths), jnp.arange(rows * top), side="right").astype(jnp.int32)
    grid = items.reshape(top, rows).T
    grid = grid[jax.random.permutation(jax.random.fold_in(own, 1), rows)]
    offset_by = jax.random.randint(jax.random.fold_in(own, 2), (rows, 1), 0, top)
    return jnp.take_along_axis(grid, (jnp.arange(top)[None, :] + offset_by) % top, axis=1)


def load_shares(amount, total, bound, lean, full):
    loads = [(1 << 20) // math.isqrt(grade ** lean) + 1 for grade in range(1, amount + 1)]
    largest = bound if full else min(bound, max(-(-total // amount), total * loads[0] // sum(loads)))
    least = 1 if total - largest >= amount - 1 else 0
    holding, rest = [largest] + [least] * (amount - 1), total - largest - least * (amount - 1)
    while rest > 0:
        candidates = [i for i in range(1, amount) if holding[i] < largest] or [i for i in range(1, amount) if holding[i] < bound]
        mass, budget = sum([loads[i] for i in candidates]), rest
        for i in candidates:
            extra = min(bound - holding[i], max(1, budget * loads[i] // mass), rest)
            holding[i] = holding[i] + extra
            rest = rest - extra
    return np.array(holding)


def scatter_about(stream_key, dims, deviation, bound, cuts=(), kind=jnp.bfloat16):
    gain = level_of(stream_key, dims, cuts, -0.22, 0.18) if cuts else 1.0
    array = jax.random.normal(stream_key, dims, jnp.float32) * deviation * gain
    return jnp.minimum(jnp.maximum(array, -bound), bound).astype(kind)


def setup_inputs(seed: int = 0) -> dict:
    splits = jax.random.split(jax.random.key(seed), 8)
    tokens = scatter_about(splits[0], (TOKENS, D), 1.0, 6.0, ((0, 8), (1, 16)))
    norm_gain = jnp.clip(1.0 + 0.18 * jax.random.normal(splits[1], (D,), jnp.float32), 0.1, 1.9)
    expert_ids_keys = jax.random.split(jax.random.fold_in(splits[2], 1), TOKENS // TOK_ROW)
    expert_ids_turns = jax.random.permutation(jax.random.fold_in(splits[2], 3), TOKENS // TOK_ROW)
    expert_ids = jax.vmap(lambda own, number: deal_out(jax.random.fold_in(splits[2], 2), own, number, TOK_ROW, EXPERTS, TOP, CAP, 2))(expert_ids_keys, expert_ids_turns).reshape((TOKENS, TOP))
    gate_weights = jnp.clip(0.1 + 0.9 * jax.random.uniform(splits[3], (TOKENS, TOP), jnp.float32) ** level_of(splits[3], (TOKENS, TOP), ((0, 8),), -0.2, 0.2), 0.1, 1.0)
    w_gate = scatter_about(splits[4], (EXPERTS, D, FF), D ** -0.5, 0.09375, ((0, 8), (2, 16)))
    w_up = scatter_about(splits[5], (EXPERTS, D, FF), D ** -0.5, 0.09375, ((0, 8), (2, 16)))
    w_down = scatter_about(splits[6], (EXPERTS, FF, D), FF ** -0.5, 0.046875, ((0, 8), (1, 16)))
    return {"tokens": tokens, "norm_gain": norm_gain, "expert_ids": expert_ids, "gate_weights": gate_weights, "w_gate": w_gate, "w_up": w_up, "w_down": w_down}


def normalize(rows, norm_gain):
    values = rows.astype(jnp.float32)
    inverse_norm = lax.rsqrt(lax.optimization_barrier(jnp.mean(values * values, axis=-1, keepdims=True)) + 1e-05)
    return (values * inverse_norm * norm_gain.astype(jnp.float32)).astype(jnp.bfloat16)

def reference(tokens, norm_gain, expert_ids, gate_weights, w_gate, w_up, w_down):
    normed = normalize(tokens, norm_gain)
    flat_ids = expert_ids.reshape(-1).astype(jnp.int32)
    flat_gates = gate_weights.reshape(-1).astype(jnp.float32)
    token_count = tokens.shape[0]
    limit = TOKENS // 2
    owner_ids = (jnp.arange(flat_ids.shape[0], dtype=jnp.int32) // TOP).astype(jnp.int32)

    def one_expert(index, total):
        expert_hits = (flat_ids == index).astype(jnp.int32)
        ranks = (jnp.cumsum(expert_hits) - expert_hits).astype(jnp.int32)
        targets = jnp.where(expert_hits > 0, ranks, limit).astype(jnp.int32)
        owners = jnp.zeros((limit,), jnp.int32).at[targets].set(owner_ids, mode='drop')
        gathered = normed[owners]
        gate_part = jnp.dot(gathered, w_gate[index], preferred_element_type=jnp.float32)
        up_part = jnp.dot(gathered, w_up[index], preferred_element_type=jnp.float32)
        hidden = (jax.nn.silu(gate_part) * up_part).astype(jnp.bfloat16)
        outputs = jnp.dot(hidden, w_down[index], preferred_element_type=jnp.float32)
        picked = outputs[jnp.minimum(ranks, limit - 1)]
        scaled = picked * (flat_gates * expert_hits.astype(jnp.float32))[:, None]
        return total + lax.optimization_barrier(jnp.sum(scaled.reshape(token_count, TOP, -1), axis=1))
    mixed = lax.fori_loop(0, EXPERTS, one_expert, jnp.zeros(tokens.shape, jnp.float32))
    return (tokens.astype(jnp.float32) + mixed).astype(jnp.bfloat16)
```

```python
import jax
import jax.numpy as jnp
from jax import lax
from jax.sharding import Mesh
from jax.sharding import PartitionSpec as P

EXPERTS = 8
CAP = 128
COL = ("chip", "core")


def route_tables(expert_ids, expert_count, capacity):
    token_count = expert_ids.shape[0]
    flat_ids = expert_ids.reshape(-1)
    expert_range = jnp.arange(expert_count, dtype=jnp.int32)
    expert_hits = (flat_ids[:, None] == expert_range[None, :]).astype(jnp.int32)
    earlier = jnp.cumsum(expert_hits, axis=0) - expert_hits
    ranks = jnp.sum(earlier * expert_hits, axis=1)
    slot_index = (flat_ids * capacity + ranks).reshape(token_count, -1)
    slot_ids = jnp.arange(expert_count * capacity, dtype=jnp.int32)
    matches = (slot_index[:, :, None] == slot_ids[None, None, :]).astype(jnp.float32)
    picker = jnp.sum(matches, axis=1)
    return (picker.astype(jnp.bfloat16), slot_index)


def combine_rows(slot_rows, slot_index, gate_weights):
    picked = slot_rows[slot_index]
    return jnp.sum(picked * gate_weights[:, :, None], axis=1)


def swap_cores(value):
    return lax.ppermute(value, "core", perm=[(0, 1), (1, 0)])


def body(tokens, norm_gain, expert_ids, gate_weights, w_gate, w_up, w_down):
    chips = lax.psum(1, "chip")
    width = tokens.shape[1]
    core = lax.axis_index("core")
    block = lax.axis_index("chip") * 2 + core

    values = tokens.astype(jnp.float32)
    squares = lax.psum(jnp.sum(values * values, axis=-1, keepdims=True), COL)
    inverse_norm = lax.rsqrt(squares / (width * chips * 2) + 1e-05)
    gain = lax.dynamic_slice_in_dim(norm_gain, block * width, width)
    normed = (values * inverse_norm * gain).astype(jnp.bfloat16)

    picker, slot_index = route_tables(expert_ids, EXPERTS, CAP)
    packed = jnp.einsum("ts,td->sd", picker, normed, preferred_element_type=jnp.float32).astype(
        jnp.bfloat16
    )
    packed = packed.reshape(EXPERTS, CAP, width)
    arrived = lax.all_to_all(packed, "row", split_axis=0, concat_axis=0, tiled=True)
    arrived = arrived.reshape(EXPERTS * CAP, width)

    mine = lax.all_gather(arrived, "chip", axis=0, tiled=False)
    other = swap_cores(mine)
    pair = jnp.where(core == 0, jnp.stack([mine, other], 1), jnp.stack([other, mine], 1))
    slots = arrived.shape[0]
    widened = jnp.transpose(pair, (2, 0, 1, 3)).reshape(slots, chips * 2 * width)

    gate_part = jnp.dot(widened, w_gate[0], preferred_element_type=jnp.float32)
    up_part = jnp.dot(widened, w_up[0], preferred_element_type=jnp.float32)
    hidden = (jax.nn.silu(gate_part) * up_part).astype(jnp.bfloat16)
    outputs = jnp.dot(hidden, w_down[0], preferred_element_type=jnp.float32)

    split = outputs.reshape(slots, chips, 2, width)
    keep = jnp.where(core == 0, split[:, :, 0], split[:, :, 1])
    give = jnp.where(core == 0, split[:, :, 1], split[:, :, 0])
    summed = keep + swap_cores(give)
    shares = lax.psum_scatter(summed, "chip", scatter_dimension=1, tiled=True)
    shares = shares.reshape(EXPERTS, CAP, width)
    returned = lax.all_to_all(shares, "row", split_axis=0, concat_axis=0, tiled=True)
    mixed = combine_rows(returned.reshape(-1, width), slot_index, gate_weights)
    return (tokens.astype(jnp.float32) + mixed).astype(jnp.bfloat16)


def solution(mesh):
    rows, cols = mesh.devices.shape
    split_mesh = Mesh(mesh.devices.reshape(rows, cols // 2, 2), ("row", "chip", "core"))
    placed = (
        P("row", COL),
        P(),
        P("row", None),
        P("row", None),
        P("row", None, COL),
        P("row", None, COL),
        P("row", COL, None),
    )
    return jax.shard_map(
        body, mesh=split_mesh, in_specs=placed, out_specs=P("row", COL), check_vma=False
    )
```

```python
import functools

import jax
import jax.numpy as jnp
from jax import lax
from jax.experimental import pallas as pl
from jax.experimental.pallas import tpu as pltpu
from jax.sharding import Mesh
from jax.sharding import PartitionSpec as P

EXPERTS = 8
CAP = 128
COL = ("chip", "core")
MESH = pl.DeviceIdType.MESH


def normalize(rows, norm_gain):
    values = rows.astype(jnp.float32)
    inverse_norm = lax.rsqrt(jnp.mean(values * values, axis=-1, keepdims=True) + 1e-05)
    return (values * inverse_norm * norm_gain).astype(jnp.bfloat16)


def route_tables(expert_ids, expert_count, capacity):
    token_count = expert_ids.shape[0]
    flat_ids = expert_ids.reshape(-1)
    expert_range = jnp.arange(expert_count, dtype=jnp.int32)
    expert_hits = (flat_ids[:, None] == expert_range[None, :]).astype(jnp.int32)
    earlier = jnp.cumsum(expert_hits, axis=0) - expert_hits
    ranks = jnp.sum(earlier * expert_hits, axis=1)
    slot_index = (flat_ids * capacity + ranks).reshape(token_count, -1)
    slot_ids = jnp.arange(expert_count * capacity, dtype=jnp.int32)
    matches = (slot_index[:, :, None] == slot_ids[None, None, :]).astype(jnp.float32)
    picker = jnp.sum(matches, axis=1)
    return (picker.astype(jnp.bfloat16), slot_index)


def combine_rows(slot_rows, slot_index, gate_weights):
    picked = slot_rows[slot_index]
    return jnp.sum(picked * gate_weights[:, :, None], axis=1)


def entry_barrier(chips, row, me, core):
    barrier = pltpu.get_barrier_semaphore()
    for d in range(1, chips):
        peer = lax.rem(me + d, chips)
        pl.semaphore_signal(barrier, inc=1, device_id=(row, peer, core), device_id_type=MESH)
    pl.semaphore_signal(barrier, inc=1, device_id=(row, me, 1 - core), device_id_type=MESH)
    pl.semaphore_wait(barrier, chips)


def gather_kernel(chips, width, src, out, send_sem, recv_sem, fwd_send, fwd_recv, local_sem):
    row, me, core = lax.axis_index("row"), lax.axis_index("chip"), lax.axis_index("core")
    entry_barrier(chips, row, me, core)

    def window(chip, half):
        start = pl.multiple_of((chip * 2 + half) * width, width)
        return out.at[:, pl.ds(start, width)]

    local = pltpu.make_async_copy(src, window(me, core), local_sem)
    local.start()
    copies = []
    for d in range(1, chips):
        peer = lax.rem(me + d, chips)
        copy = pltpu.make_async_remote_copy(
            src_ref=src, dst_ref=window(me, core), send_sem=send_sem.at[d],
            recv_sem=recv_sem.at[d], device_id=(row, peer, core), device_id_type=MESH,
        )
        copy.start()
        copies.append(copy)
    forwards = []
    for d in range(chips):
        source = lax.rem(me - d + chips, chips)
        if d == 0:
            local.wait()
        else:
            copies[d - 1].wait_recv()
        fwd = pltpu.make_async_remote_copy(
            src_ref=window(source, core), dst_ref=window(source, core), send_sem=fwd_send.at[d],
            recv_sem=fwd_recv.at[d], device_id=(row, me, 1 - core), device_id_type=MESH,
        )
        fwd.start()
        forwards.append(fwd)
    for copy in copies:
        copy.wait_send()
    for fwd in forwards:
        fwd.wait()


def gather_cols(block, chips):
    slots, width = block.shape
    return pl.pallas_call(
        functools.partial(gather_kernel, chips, width),
        out_shape=jax.ShapeDtypeStruct((slots, chips * 2 * width), block.dtype),
        in_specs=[pl.BlockSpec(memory_space=pl.ANY)],
        out_specs=pl.BlockSpec(memory_space=pl.ANY),
        scratch_shapes=[
            pltpu.SemaphoreType.DMA((chips,)),
            pltpu.SemaphoreType.DMA((chips,)),
            pltpu.SemaphoreType.DMA((chips,)),
            pltpu.SemaphoreType.DMA((chips,)),
            pltpu.SemaphoreType.DMA(()),
        ],
        compiler_params=pltpu.CompilerParams(collective_id=0, has_side_effects=True),
    )(block)


def scatter_kernel(chips, src, out, send_sem, recv_sem, local_sem):
    row, me, core = lax.axis_index("row"), lax.axis_index("chip"), lax.axis_index("core")
    barrier = pltpu.get_barrier_semaphore()
    for d in range(1, chips):
        peer = lax.rem(me + d, chips)
        pl.semaphore_signal(barrier, inc=1, device_id=(row, peer, core), device_id_type=MESH)
    pl.semaphore_wait(barrier, chips - 1)
    local = pltpu.make_async_copy(src.at[me], out.at[me], local_sem)
    local.start()
    copies = []
    for d in range(1, chips):
        peer = lax.rem(me + d, chips)
        copy = pltpu.make_async_remote_copy(
            src_ref=src.at[peer], dst_ref=out.at[me], send_sem=send_sem.at[d],
            recv_sem=recv_sem.at[d], device_id=(row, peer, core), device_id_type=MESH,
        )
        copy.start()
        copies.append(copy)
    for copy in copies:
        copy.wait()
    local.wait()


def scatter_chips(parts):
    chips = parts.shape[0]
    return pl.pallas_call(
        functools.partial(scatter_kernel, chips),
        out_shape=jax.ShapeDtypeStruct(parts.shape, parts.dtype),
        in_specs=[pl.BlockSpec(memory_space=pl.ANY)],
        out_specs=pl.BlockSpec(memory_space=pl.ANY),
        scratch_shapes=[
            pltpu.SemaphoreType.DMA((chips,)),
            pltpu.SemaphoreType.DMA((chips,)),
            pltpu.SemaphoreType.DMA(()),
        ],
        compiler_params=pltpu.CompilerParams(collective_id=1, has_side_effects=True),
    )(parts)


def body(tokens, norm_gain, expert_ids, gate_weights, w_gate, w_up, w_down):
    chips = lax.psum(1, "chip")
    width = tokens.shape[1]
    core = lax.axis_index("core")

    picker, slot_index = route_tables(expert_ids, EXPERTS, CAP)
    packed = jnp.einsum("ts,td->sd", picker, tokens, preferred_element_type=jnp.float32).astype(
        jnp.bfloat16
    )
    packed = packed.reshape(EXPERTS, CAP, width)
    arrived = lax.all_to_all(packed, "row", split_axis=0, concat_axis=0, tiled=True)
    arrived = arrived.reshape(EXPERTS * CAP, width)
    slots = arrived.shape[0]

    widened = gather_cols(arrived, chips)
    normed = normalize(widened, norm_gain)
    gate_part = jnp.dot(normed, w_gate[0], preferred_element_type=jnp.float32)
    up_part = jnp.dot(normed, w_up[0], preferred_element_type=jnp.float32)
    hidden = (jax.nn.silu(gate_part) * up_part).astype(jnp.bfloat16)
    down = w_down[0].reshape(w_down.shape[1], chips, 2, width)
    split = jnp.einsum("sf,fkjw->jksw", hidden, down, preferred_element_type=jnp.float32)

    keep = lax.dynamic_index_in_dim(split, core, 0, keepdims=False)
    give = lax.dynamic_index_in_dim(split, 1 - core, 0, keepdims=False)
    summed = keep + lax.ppermute(give, "core", perm=[(0, 1), (1, 0)])
    arrived_parts = scatter_chips(summed.astype(jnp.bfloat16))
    shares = jnp.sum(arrived_parts.astype(jnp.float32), axis=0)
    shares = shares.reshape(EXPERTS, CAP, width)
    returned = lax.all_to_all(shares, "row", split_axis=0, concat_axis=0, tiled=True)
    mixed = combine_rows(returned.reshape(-1, width), slot_index, gate_weights)
    return (tokens.astype(jnp.float32) + mixed).astype(jnp.bfloat16)


def solution(mesh):
    rows, cols = mesh.devices.shape
    split_mesh = Mesh(mesh.devices.reshape(rows, cols // 2, 2), ("row", "chip", "core"))
    placed = (
        P("row", COL),
        P(),
        P("row", None),
        P("row", None),
        P("row", None, COL),
        P("row", None, COL),
        P("row", COL, None),
    )
    return jax.shard_map(
        body, mesh=split_mesh, in_specs=placed, out_specs=P("row", COL), check_vma=False
    )
```

```python
import functools

import jax
import jax.numpy as jnp
from jax import lax
from jax.experimental import pallas as pl
from jax.experimental.pallas import tpu as pltpu
from jax.sharding import Mesh
from jax.sharding import PartitionSpec as P

EXPERTS = 8
CAP = 128
COL = ("chip", "core")
MESH = pl.DeviceIdType.MESH


def normalize(rows, norm_gain):
    values = rows.astype(jnp.float32)
    inverse_norm = lax.rsqrt(jnp.mean(values * values, axis=-1, keepdims=True) + 1e-05)
    return (values * inverse_norm * norm_gain).astype(jnp.bfloat16)


def route_tables(expert_ids, expert_count, capacity):
    token_count = expert_ids.shape[0]
    flat_ids = expert_ids.reshape(-1)
    expert_range = jnp.arange(expert_count, dtype=jnp.int32)
    expert_hits = (flat_ids[:, None] == expert_range[None, :]).astype(jnp.int32)
    earlier = jnp.cumsum(expert_hits, axis=0) - expert_hits
    ranks = jnp.sum(earlier * expert_hits, axis=1)
    slot_index = (flat_ids * capacity + ranks).reshape(token_count, -1)
    slot_ids = jnp.arange(expert_count * capacity, dtype=jnp.int32)
    matches = (slot_index[:, :, None] == slot_ids[None, None, :]).astype(jnp.float32)
    picker = jnp.sum(matches, axis=1)
    return (picker.astype(jnp.bfloat16), slot_index)


def combine_rows(slot_rows, slot_index, gate_weights):
    picked = slot_rows[slot_index]
    return jnp.sum(picked * gate_weights[:, :, None], axis=1)


def gather_kernel(width, src, out, send_sem, recv_sem, local_sem):
    row, me, core = lax.axis_index("row"), lax.axis_index("chip"), lax.axis_index("core")
    side, y = me // 4, me % 4
    partner = lax.rem(me + 4, 8)
    up = side * 4 + lax.rem(y + 1, 4)
    down = side * 4 + lax.rem(y + 3, 4)
    across = side * 4 + lax.rem(y + 2, 4)
    sister = 1 - core

    barrier = pltpu.get_barrier_semaphore()
    for chip, half in ((partner, core), (up, core), (down, core), (me, sister)):
        pl.semaphore_signal(barrier, inc=1, device_id=(row, chip, half), device_id_type=MESH)
    pl.semaphore_wait(barrier, 4)

    def window(chip):
        start = pl.multiple_of((chip * 2 + core) * width, width)
        return out.at[:, pl.ds(start, width)]

    def send(tag, origin, chip, half, source=None):
        copy = pltpu.make_async_remote_copy(
            src_ref=window(origin) if source is None else source, dst_ref=window(origin),
            send_sem=send_sem.at[tag], recv_sem=recv_sem.at[tag],
            device_id=(row, chip, half), device_id_type=MESH,
        )
        copy.start()
        return copy

    sent = [
        send(0, me, partner, core, src),
        send(1, me, up, core, src),
        send(2, me, down, core, src),
        send(7, me, me, sister, src),
    ]
    local = pltpu.make_async_copy(src, window(me), local_sem)
    local.start()

    def arrive(tag, origin):
        pltpu.make_async_remote_copy(
            src_ref=window(origin), dst_ref=window(origin), send_sem=send_sem.at[tag],
            recv_sem=recv_sem.at[tag], device_id=(row, me, sister), device_id_type=MESH,
        ).wait_recv()

    other = lax.rem(partner, 8)
    arrive(0, other)
    sent += [send(3, other, up, core), send(4, other, down, core), send(8, other, me, sister)]
    arrive(1, down)
    sent += [send(5, down, up, core), send(9, down, me, sister)]
    arrive(2, up)
    sent.append(send(10, up, me, sister))
    arrive(3, lax.rem(down + 4, 8))
    sent.append(send(11, lax.rem(down + 4, 8), me, sister))
    arrive(4, lax.rem(up + 4, 8))
    sent += [send(6, lax.rem(up + 4, 8), down, core), send(12, lax.rem(up + 4, 8), me, sister)]
    arrive(5, across)
    sent.append(send(13, across, me, sister))
    arrive(6, lax.rem(across + 4, 8))
    sent.append(send(14, lax.rem(across + 4, 8), me, sister))
    local.wait()

    def sister_window(origin):
        start = pl.multiple_of((origin * 2 + sister) * width, width)
        return out.at[:, pl.ds(start, width)]

    for tag, origin in ((7, me), (8, partner), (9, down), (10, up), (11, lax.rem(down + 4, 8)),
                        (12, lax.rem(up + 4, 8)), (13, across), (14, lax.rem(across + 4, 8))):
        pltpu.make_async_remote_copy(
            src_ref=sister_window(origin), dst_ref=sister_window(origin),
            send_sem=send_sem.at[tag], recv_sem=recv_sem.at[tag],
            device_id=(row, me, sister), device_id_type=MESH,
        ).wait_recv()
    for copy in sent:
        copy.wait_send()


def gather_cols(block, chips):
    slots, width = block.shape
    return pl.pallas_call(
        functools.partial(gather_kernel, width),
        out_shape=jax.ShapeDtypeStruct((slots, chips * 2 * width), block.dtype),
        in_specs=[pl.BlockSpec(memory_space=pl.ANY)],
        out_specs=pl.BlockSpec(memory_space=pl.ANY),
        scratch_shapes=[
            pltpu.SemaphoreType.DMA((15,)),
            pltpu.SemaphoreType.DMA((15,)),
            pltpu.SemaphoreType.DMA(()),
        ],
        compiler_params=pltpu.CompilerParams(collective_id=0, has_side_effects=True),
    )(block)


def scatter_kernel(chips, src, out, send_sem, recv_sem, local_sem):
    row, me, core = lax.axis_index("row"), lax.axis_index("chip"), lax.axis_index("core")
    barrier = pltpu.get_barrier_semaphore()
    for d in range(1, chips):
        peer = lax.rem(me + d, chips)
        pl.semaphore_signal(barrier, inc=1, device_id=(row, peer, core), device_id_type=MESH)
    pl.semaphore_wait(barrier, chips - 1)
    local = pltpu.make_async_copy(src.at[me], out.at[me], local_sem)
    local.start()
    copies = []
    for d in range(1, chips):
        peer = lax.rem(me + d, chips)
        copy = pltpu.make_async_remote_copy(
            src_ref=src.at[peer], dst_ref=out.at[me], send_sem=send_sem.at[d],
            recv_sem=recv_sem.at[d], device_id=(row, peer, core), device_id_type=MESH,
        )
        copy.start()
        copies.append(copy)
    for copy in copies:
        copy.wait()
    local.wait()


def scatter_chips(parts):
    chips = parts.shape[0]
    return pl.pallas_call(
        functools.partial(scatter_kernel, chips),
        out_shape=jax.ShapeDtypeStruct(parts.shape, parts.dtype),
        in_specs=[pl.BlockSpec(memory_space=pl.ANY)],
        out_specs=pl.BlockSpec(memory_space=pl.ANY),
        scratch_shapes=[
            pltpu.SemaphoreType.DMA((chips,)),
            pltpu.SemaphoreType.DMA((chips,)),
            pltpu.SemaphoreType.DMA(()),
        ],
        compiler_params=pltpu.CompilerParams(collective_id=1, has_side_effects=True),
    )(parts)


def body(tokens, norm_gain, expert_ids, gate_weights, w_gate, w_up, w_down):
    chips = lax.psum(1, "chip")
    width = tokens.shape[1]
    core = lax.axis_index("core")

    picker, slot_index = route_tables(expert_ids, EXPERTS, CAP)
    packed = jnp.einsum("ts,td->sd", picker, tokens, preferred_element_type=jnp.float32).astype(
        jnp.bfloat16
    )
    packed = packed.reshape(EXPERTS, CAP, width)
    arrived = lax.all_to_all(packed, "row", split_axis=0, concat_axis=0, tiled=True)
    arrived = arrived.reshape(EXPERTS * CAP, width)
    slots = arrived.shape[0]

    widened = gather_cols(arrived, chips)
    normed = normalize(widened, norm_gain)
    gate_part = jnp.dot(normed, w_gate[0], preferred_element_type=jnp.float32)
    up_part = jnp.dot(normed, w_up[0], preferred_element_type=jnp.float32)
    hidden = (jax.nn.silu(gate_part) * up_part).astype(jnp.bfloat16)
    down = w_down[0].reshape(w_down.shape[1], chips, 2, width)
    split = jnp.einsum("sf,fkjw->jksw", hidden, down, preferred_element_type=jnp.float32)

    keep = lax.dynamic_index_in_dim(split, core, 0, keepdims=False)
    give = lax.dynamic_index_in_dim(split, 1 - core, 0, keepdims=False)
    summed = keep + lax.ppermute(give, "core", perm=[(0, 1), (1, 0)])
    arrived_parts = scatter_chips(summed.astype(jnp.bfloat16))
    shares = jnp.sum(arrived_parts.astype(jnp.float32), axis=0)
    shares = shares.reshape(EXPERTS, CAP, width)
    returned = lax.all_to_all(shares, "row", split_axis=0, concat_axis=0, tiled=True)
    mixed = combine_rows(returned.reshape(-1, width), slot_index, gate_weights)
    return (tokens.astype(jnp.float32) + mixed).astype(jnp.bfloat16)


def solution(mesh):
    rows, cols = mesh.devices.shape
    split_mesh = Mesh(mesh.devices.reshape(rows, cols // 2, 2), ("row", "chip", "core"))
    placed = (
        P("row", COL),
        P(),
        P("row", None),
        P("row", None),
        P("row", None, COL),
        P("row", None, COL),
        P("row", COL, None),
    )
    return jax.shard_map(
        body, mesh=split_mesh, in_specs=placed, out_specs=P("row", COL), check_vma=False
    )
```

```python
import functools

import jax
import jax.numpy as jnp
from jax import lax
from jax.experimental import pallas as pl
from jax.experimental.pallas import tpu as pltpu
from jax.sharding import Mesh
from jax.sharding import PartitionSpec as P

EXPERTS = 8
CAP = 128
COL = ("chip", "core")
MESH = pl.DeviceIdType.MESH


def normalize(rows, norm_gain):
    values = rows.astype(jnp.float32)
    inverse_norm = lax.rsqrt(jnp.mean(values * values, axis=-1, keepdims=True) + 1e-05)
    return (values * inverse_norm * norm_gain).astype(jnp.bfloat16)


def route_tables(expert_ids, expert_count, capacity):
    token_count = expert_ids.shape[0]
    flat_ids = expert_ids.reshape(-1)
    expert_range = jnp.arange(expert_count, dtype=jnp.int32)
    expert_hits = (flat_ids[:, None] == expert_range[None, :]).astype(jnp.int32)
    earlier = jnp.cumsum(expert_hits, axis=0) - expert_hits
    ranks = jnp.sum(earlier * expert_hits, axis=1)
    slot_index = (flat_ids * capacity + ranks).reshape(token_count, -1)
    slot_ids = jnp.arange(expert_count * capacity, dtype=jnp.int32)
    matches = (slot_index[:, :, None] == slot_ids[None, None, :]).astype(jnp.float32)
    picker = jnp.sum(matches, axis=1)
    return (picker.astype(jnp.bfloat16), slot_index)


def combine_rows(slot_rows, slot_index, gate_weights):
    picked = slot_rows[slot_index]
    return jnp.sum(picked * gate_weights[:, :, None], axis=1)


def gather_kernel(width, src, out, send_sem, recv_sem, local_sem):
    row, me, core = lax.axis_index("row"), lax.axis_index("chip"), lax.axis_index("core")
    side, y = me // 4, me % 4
    partner = lax.rem(me + 4, 8)
    up = side * 4 + lax.rem(y + 1, 4)
    down = side * 4 + lax.rem(y + 3, 4)
    across = side * 4 + lax.rem(y + 2, 4)
    sister = 1 - core

    barrier = pltpu.get_barrier_semaphore()
    for chip, half in ((partner, core), (up, core), (down, core), (me, sister)):
        pl.semaphore_signal(barrier, inc=1, device_id=(row, chip, half), device_id_type=MESH)
    pl.semaphore_wait(barrier, 4)

    def window(chip):
        start = pl.multiple_of((chip * 2 + core) * width, width)
        return out.at[:, pl.ds(start, width)]

    def send(tag, origin, chip, half, source=None):
        copy = pltpu.make_async_remote_copy(
            src_ref=window(origin) if source is None else source, dst_ref=window(origin),
            send_sem=send_sem.at[tag], recv_sem=recv_sem.at[tag],
            device_id=(row, chip, half), device_id_type=MESH,
        )
        copy.start()
        return copy

    sent = [
        send(0, me, partner, core, src),
        send(1, me, up, core, src),
        send(2, me, down, core, src),
        send(7, me, me, sister, src),
    ]
    local = pltpu.make_async_copy(src, window(me), local_sem)
    local.start()

    def arrive(tag, origin):
        pltpu.make_async_remote_copy(
            src_ref=window(origin), dst_ref=window(origin), send_sem=send_sem.at[tag],
            recv_sem=recv_sem.at[tag], device_id=(row, me, sister), device_id_type=MESH,
        ).wait_recv()

    other = lax.rem(partner, 8)
    arrive(0, other)
    sent += [send(3, other, up, core), send(4, other, down, core), send(8, other, me, sister)]
    arrive(1, down)
    sent += [send(5, down, up, core), send(9, down, me, sister)]
    arrive(2, up)
    sent.append(send(10, up, me, sister))
    arrive(3, lax.rem(down + 4, 8))
    sent.append(send(11, lax.rem(down + 4, 8), me, sister))
    arrive(4, lax.rem(up + 4, 8))
    sent += [send(6, lax.rem(up + 4, 8), down, core), send(12, lax.rem(up + 4, 8), me, sister)]
    arrive(5, across)
    sent.append(send(13, across, me, sister))
    arrive(6, lax.rem(across + 4, 8))
    sent.append(send(14, lax.rem(across + 4, 8), me, sister))
    local.wait()

    def sister_window(origin):
        start = pl.multiple_of((origin * 2 + sister) * width, width)
        return out.at[:, pl.ds(start, width)]

    for tag, origin in ((7, me), (8, partner), (9, down), (10, up), (11, lax.rem(down + 4, 8)),
                        (12, lax.rem(up + 4, 8)), (13, across), (14, lax.rem(across + 4, 8))):
        pltpu.make_async_remote_copy(
            src_ref=sister_window(origin), dst_ref=sister_window(origin),
            send_sem=send_sem.at[tag], recv_sem=recv_sem.at[tag],
            device_id=(row, me, sister), device_id_type=MESH,
        ).wait_recv()
    for copy in sent:
        copy.wait_send()


def gather_cols(block, chips):
    slots, width = block.shape
    return pl.pallas_call(
        functools.partial(gather_kernel, width),
        out_shape=jax.ShapeDtypeStruct((slots, chips * 2 * width), block.dtype),
        in_specs=[pl.BlockSpec(memory_space=pl.ANY)],
        out_specs=pl.BlockSpec(memory_space=pl.ANY),
        scratch_shapes=[
            pltpu.SemaphoreType.DMA((15,)),
            pltpu.SemaphoreType.DMA((15,)),
            pltpu.SemaphoreType.DMA(()),
        ],
        compiler_params=pltpu.CompilerParams(collective_id=0, has_side_effects=True),
    )(block)


def add_blocks(dst, *sources):
    rows = dst.shape[0]
    step = 128

    def one(i, carry):
        part = pl.ds(pl.multiple_of(i * step, step), step)
        total = sources[0][part, :].astype(jnp.float32)
        for source in sources[1:]:
            total = total + source[part, :].astype(jnp.float32)
        dst[part, :] = total.astype(dst.dtype)
        return carry

    lax.fori_loop(0, rows // step, one, 0)


def scatter_kernel(parts, out, sending, landed, send_sem, recv_sem):
    row, me, core = lax.axis_index("row"), lax.axis_index("chip"), lax.axis_index("core")
    side, y = me // 4, me % 4
    partner = lax.rem(me + 4, 8)
    up = side * 4 + lax.rem(y + 1, 4)
    down = side * 4 + lax.rem(y + 3, 4)
    across = side * 4 + lax.rem(y + 2, 4)

    def far(chip):
        return lax.rem(chip + 4, 8)

    barrier = pltpu.get_barrier_semaphore()
    for chip in (partner, up, down):
        pl.semaphore_signal(barrier, inc=1, device_id=(row, chip, core), device_id_type=MESH)
    pl.semaphore_wait(barrier, 3)

    def send(tag, chip):
        copy = pltpu.make_async_remote_copy(
            src_ref=sending.at[tag], dst_ref=landed.at[tag], send_sem=send_sem.at[tag],
            recv_sem=recv_sem.at[tag], device_id=(row, chip, core), device_id_type=MESH,
        )
        copy.start()
        return copy

    def arrive(tag):
        pltpu.make_async_remote_copy(
            src_ref=sending.at[tag], dst_ref=landed.at[tag], send_sem=send_sem.at[tag],
            recv_sem=recv_sem.at[tag], device_id=(row, me, core), device_id_type=MESH,
        ).wait_recv()

    sent = []
    for tag, chip, target in ((0, down, far(down)), (1, down, across), (2, up, up),
                              (3, up, far(across))):
        add_blocks(sending.at[tag], parts.at[target])
        sent.append(send(tag, chip))
    arrive(1)
    add_blocks(sending.at[4], parts.at[down], landed.at[1])
    sent.append(send(4, down))
    arrive(3)
    add_blocks(sending.at[5], parts.at[far(up)], landed.at[3])
    sent.append(send(5, up))
    arrive(0)
    arrive(5)
    add_blocks(sending.at[6], parts.at[partner], landed.at[0], landed.at[5])
    sent.append(send(6, partner))
    arrive(2)
    arrive(4)
    add_blocks(out, parts.at[me], landed.at[2], landed.at[4])
    arrive(6)
    add_blocks(out, out, landed.at[6])
    for copy in sent:
        copy.wait_send()


def scatter_chips(parts):
    chips, slots, width = parts.shape
    return pl.pallas_call(
        scatter_kernel,
        out_shape=jax.ShapeDtypeStruct((slots, width), jnp.float32),
        in_specs=[pl.BlockSpec(memory_space=pltpu.VMEM)],
        out_specs=pl.BlockSpec(memory_space=pltpu.VMEM),
        scratch_shapes=[
            pltpu.VMEM((7, slots, width), jnp.bfloat16),
            pltpu.VMEM((7, slots, width), jnp.bfloat16),
            pltpu.SemaphoreType.DMA((7,)),
            pltpu.SemaphoreType.DMA((7,)),
        ],
        compiler_params=pltpu.CompilerParams(
            collective_id=1, has_side_effects=True, vmem_limit_bytes=48 * 1024 * 1024
        ),
    )(parts)


def body(tokens, norm_gain, expert_ids, gate_weights, w_gate, w_up, w_down):
    chips = lax.psum(1, "chip")
    width = tokens.shape[1]
    core = lax.axis_index("core")

    picker, slot_index = route_tables(expert_ids, EXPERTS, CAP)
    packed = jnp.einsum("ts,td->sd", picker, tokens, preferred_element_type=jnp.float32).astype(
        jnp.bfloat16
    )
    packed = packed.reshape(EXPERTS, CAP, width)
    arrived = lax.all_to_all(packed, "row", split_axis=0, concat_axis=0, tiled=True)
    arrived = arrived.reshape(EXPERTS * CAP, width)
    slots = arrived.shape[0]

    widened = gather_cols(arrived, chips)
    normed = normalize(widened, norm_gain)
    gate_part = jnp.dot(normed, w_gate[0], preferred_element_type=jnp.float32)
    up_part = jnp.dot(normed, w_up[0], preferred_element_type=jnp.float32)
    hidden = (jax.nn.silu(gate_part) * up_part).astype(jnp.bfloat16)
    down = w_down[0].reshape(w_down.shape[1], chips, 2, width)
    split = jnp.einsum("sf,fkjw->jksw", hidden, down, preferred_element_type=jnp.float32)

    keep = lax.dynamic_index_in_dim(split, core, 0, keepdims=False)
    give = lax.dynamic_index_in_dim(split, 1 - core, 0, keepdims=False)
    summed = keep + lax.ppermute(give, "core", perm=[(0, 1), (1, 0)])
    shares = scatter_chips(summed)
    shares = shares.reshape(EXPERTS, CAP, width)
    returned = lax.all_to_all(shares, "row", split_axis=0, concat_axis=0, tiled=True)
    mixed = combine_rows(returned.reshape(-1, width), slot_index, gate_weights)
    return (tokens.astype(jnp.float32) + mixed).astype(jnp.bfloat16)


def solution(mesh):
    rows, cols = mesh.devices.shape
    split_mesh = Mesh(mesh.devices.reshape(rows, cols // 2, 2), ("row", "chip", "core"))
    placed = (
        P("row", COL),
        P(),
        P("row", None),
        P("row", None),
        P("row", None, COL),
        P("row", None, COL),
        P("row", COL, None),
    )
    return jax.shard_map(
        body, mesh=split_mesh, in_specs=placed, out_specs=P("row", COL), check_vma=False
    )
```

```python
import functools

import jax
import jax.numpy as jnp
from jax import lax
from jax.experimental import pallas as pl
from jax.experimental.pallas import tpu as pltpu
from jax.sharding import Mesh
from jax.sharding import PartitionSpec as P

EXPERTS = 8
CAP = 128
COL = ("chip", "core")
MESH = pl.DeviceIdType.MESH


def normalize(rows, norm_gain):
    values = rows.astype(jnp.float32)
    inverse_norm = lax.rsqrt(jnp.mean(values * values, axis=-1, keepdims=True) + 1e-05)
    return (values * inverse_norm * norm_gain).astype(jnp.bfloat16)


def route_tables(expert_ids, expert_count, capacity):
    token_count = expert_ids.shape[0]
    flat_ids = expert_ids.reshape(-1)
    expert_range = jnp.arange(expert_count, dtype=jnp.int32)
    expert_hits = (flat_ids[:, None] == expert_range[None, :]).astype(jnp.int32)
    earlier = jnp.cumsum(expert_hits, axis=0) - expert_hits
    ranks = jnp.sum(earlier * expert_hits, axis=1)
    slot_index = (flat_ids * capacity + ranks).reshape(token_count, -1)
    slot_ids = jnp.arange(expert_count * capacity, dtype=jnp.int32)
    matches = (slot_index[:, :, None] == slot_ids[None, None, :]).astype(jnp.float32)
    picker = jnp.sum(matches, axis=1)
    return (picker.astype(jnp.bfloat16), slot_index)


def combine_rows(slot_rows, slot_index, gate_weights):
    picked = slot_rows[slot_index]
    return jnp.sum(picked * gate_weights[:, :, None], axis=1)


def gather_kernel(width, src, out, send_sem, recv_sem, local_sem):
    row, me, core = lax.axis_index("row"), lax.axis_index("chip"), lax.axis_index("core")
    side, y = me // 4, me % 4
    partner = lax.rem(me + 4, 8)
    up = side * 4 + lax.rem(y + 1, 4)
    down = side * 4 + lax.rem(y + 3, 4)
    across = side * 4 + lax.rem(y + 2, 4)
    sister = 1 - core

    barrier = pltpu.get_barrier_semaphore()
    for chip, half in ((partner, core), (up, core), (down, core), (me, sister)):
        pl.semaphore_signal(barrier, inc=1, device_id=(row, chip, half), device_id_type=MESH)
    pl.semaphore_wait(barrier, 4)

    def window(chip):
        start = pl.multiple_of((chip * 2 + core) * width, width)
        return out.at[:, pl.ds(start, width)]

    def send(tag, origin, chip, half, source=None):
        copy = pltpu.make_async_remote_copy(
            src_ref=window(origin) if source is None else source, dst_ref=window(origin),
            send_sem=send_sem.at[tag], recv_sem=recv_sem.at[tag],
            device_id=(row, chip, half), device_id_type=MESH,
        )
        copy.start()
        return copy

    sent = [
        send(0, me, partner, core, src),
        send(1, me, up, core, src),
        send(2, me, down, core, src),
        send(7, me, me, sister, src),
    ]
    local = pltpu.make_async_copy(src, window(me), local_sem)
    local.start()

    def arrive(tag, origin):
        pltpu.make_async_remote_copy(
            src_ref=window(origin), dst_ref=window(origin), send_sem=send_sem.at[tag],
            recv_sem=recv_sem.at[tag], device_id=(row, me, sister), device_id_type=MESH,
        ).wait_recv()

    other = lax.rem(partner, 8)
    arrive(0, other)
    sent += [send(3, other, up, core), send(4, other, down, core), send(8, other, me, sister)]
    arrive(1, down)
    sent += [send(5, down, up, core), send(9, down, me, sister)]
    arrive(2, up)
    sent.append(send(10, up, me, sister))
    arrive(3, lax.rem(down + 4, 8))
    sent.append(send(11, lax.rem(down + 4, 8), me, sister))
    arrive(4, lax.rem(up + 4, 8))
    sent += [send(6, lax.rem(up + 4, 8), down, core), send(12, lax.rem(up + 4, 8), me, sister)]
    arrive(5, across)
    sent.append(send(13, across, me, sister))
    arrive(6, lax.rem(across + 4, 8))
    sent.append(send(14, lax.rem(across + 4, 8), me, sister))
    local.wait()

    def sister_window(origin):
        start = pl.multiple_of((origin * 2 + sister) * width, width)
        return out.at[:, pl.ds(start, width)]

    for tag, origin in ((7, me), (8, partner), (9, down), (10, up), (11, lax.rem(down + 4, 8)),
                        (12, lax.rem(up + 4, 8)), (13, across), (14, lax.rem(across + 4, 8))):
        pltpu.make_async_remote_copy(
            src_ref=sister_window(origin), dst_ref=sister_window(origin),
            send_sem=send_sem.at[tag], recv_sem=recv_sem.at[tag],
            device_id=(row, me, sister), device_id_type=MESH,
        ).wait_recv()
    for copy in sent:
        copy.wait_send()


def gather_cols(block, chips):
    slots, width = block.shape
    return pl.pallas_call(
        functools.partial(gather_kernel, width),
        out_shape=jax.ShapeDtypeStruct((slots, chips * 2 * width), block.dtype),
        in_specs=[pl.BlockSpec(memory_space=pl.ANY)],
        out_specs=pl.BlockSpec(memory_space=pl.ANY),
        scratch_shapes=[
            pltpu.SemaphoreType.DMA((15,)),
            pltpu.SemaphoreType.DMA((15,)),
            pltpu.SemaphoreType.DMA(()),
        ],
        compiler_params=pltpu.CompilerParams(collective_id=0, has_side_effects=True),
    )(block)


def add_blocks(dst, *sources):
    rows = dst.shape[0]
    step = 128

    def one(i, carry):
        part = pl.ds(pl.multiple_of(i * step, step), step)
        total = sources[0][part, :].astype(jnp.float32)
        for source in sources[1:]:
            total = total + source[part, :].astype(jnp.float32)
        dst[part, :] = total.astype(dst.dtype)
        return carry

    lax.fori_loop(0, rows // step, one, 0)


def scatter_kernel(parts, out, sending, landed, send_sem, recv_sem):
    row, me, core = lax.axis_index("row"), lax.axis_index("chip"), lax.axis_index("core")
    side, y = me // 4, me % 4
    partner = lax.rem(me + 4, 8)
    up = side * 4 + lax.rem(y + 1, 4)
    down = side * 4 + lax.rem(y + 3, 4)
    across = side * 4 + lax.rem(y + 2, 4)

    def far(chip):
        return lax.rem(chip + 4, 8)

    barrier = pltpu.get_barrier_semaphore()
    for chip in (partner, up, down):
        pl.semaphore_signal(barrier, inc=1, device_id=(row, chip, core), device_id_type=MESH)
    pl.semaphore_wait(barrier, 3)

    def send(tag, chip):
        copy = pltpu.make_async_remote_copy(
            src_ref=sending.at[tag], dst_ref=landed.at[tag], send_sem=send_sem.at[tag],
            recv_sem=recv_sem.at[tag], device_id=(row, chip, core), device_id_type=MESH,
        )
        copy.start()
        return copy

    def arrive(tag):
        pltpu.make_async_remote_copy(
            src_ref=sending.at[tag], dst_ref=landed.at[tag], send_sem=send_sem.at[tag],
            recv_sem=recv_sem.at[tag], device_id=(row, me, core), device_id_type=MESH,
        ).wait_recv()

    sent = []
    for tag, chip, target in ((0, down, far(down)), (1, down, across), (2, up, up),
                              (3, up, far(across))):
        add_blocks(sending.at[tag], parts.at[target])
        sent.append(send(tag, chip))
    arrive(1)
    add_blocks(sending.at[4], parts.at[down], landed.at[1])
    sent.append(send(4, down))
    arrive(3)
    add_blocks(sending.at[5], parts.at[far(up)], landed.at[3])
    sent.append(send(5, up))
    arrive(0)
    arrive(5)
    add_blocks(sending.at[6], parts.at[partner], landed.at[0], landed.at[5])
    sent.append(send(6, partner))
    arrive(2)
    arrive(4)
    add_blocks(out, parts.at[me], landed.at[2], landed.at[4])
    arrive(6)
    add_blocks(out, out, landed.at[6])
    for copy in sent:
        copy.wait_send()


def scatter_chips(parts):
    chips, slots, width = parts.shape
    return pl.pallas_call(
        scatter_kernel,
        out_shape=jax.ShapeDtypeStruct((slots, width), jnp.float32),
        in_specs=[pl.BlockSpec(memory_space=pltpu.VMEM)],
        out_specs=pl.BlockSpec(memory_space=pltpu.VMEM),
        scratch_shapes=[
            pltpu.VMEM((7, slots, width), jnp.bfloat16),
            pltpu.VMEM((7, slots, width), jnp.bfloat16),
            pltpu.SemaphoreType.DMA((7,)),
            pltpu.SemaphoreType.DMA((7,)),
        ],
        compiler_params=pltpu.CompilerParams(
            collective_id=1, has_side_effects=True, vmem_limit_bytes=48 * 1024 * 1024
        ),
    )(parts)


def exchange_kernel(rows, src, out, send_sem, recv_sem):
    me, chip, core = lax.axis_index("row"), lax.axis_index("chip"), lax.axis_index("core")
    barrier = pltpu.get_barrier_semaphore()
    for d in range(1, rows):
        peer = lax.rem(me + d, rows)
        pl.semaphore_signal(barrier, inc=1, device_id=(peer, chip, core), device_id_type=MESH)
    pl.semaphore_wait(barrier, rows - 1)
    out[me] = src[me]
    copies = []
    for d in range(1, rows):
        peer = lax.rem(me + d, rows)
        copy = pltpu.make_async_remote_copy(
            src_ref=src.at[peer], dst_ref=out.at[me], send_sem=send_sem.at[d],
            recv_sem=recv_sem.at[d], device_id=(peer, chip, core), device_id_type=MESH,
        )
        copy.start()
        copies.append(copy)
    for copy in copies:
        copy.wait()


def exchange_rows(blocks, collective_id):
    rows = blocks.shape[0]
    return pl.pallas_call(
        functools.partial(exchange_kernel, rows),
        out_shape=jax.ShapeDtypeStruct(blocks.shape, blocks.dtype),
        in_specs=[pl.BlockSpec(memory_space=pltpu.VMEM)],
        out_specs=pl.BlockSpec(memory_space=pltpu.VMEM),
        scratch_shapes=[pltpu.SemaphoreType.DMA((rows,)), pltpu.SemaphoreType.DMA((rows,))],
        compiler_params=pltpu.CompilerParams(collective_id=collective_id, has_side_effects=True),
    )(blocks)


def body(tokens, norm_gain, expert_ids, gate_weights, w_gate, w_up, w_down):
    chips = lax.psum(1, "chip")
    width = tokens.shape[1]
    core = lax.axis_index("core")

    picker, slot_index = route_tables(expert_ids, EXPERTS, CAP)
    packed = jnp.einsum("ts,td->sd", picker, tokens, preferred_element_type=jnp.float32).astype(
        jnp.bfloat16
    )
    packed = packed.reshape(EXPERTS, CAP, width)
    arrived = exchange_rows(packed, 2)
    arrived = arrived.reshape(EXPERTS * CAP, width)
    slots = arrived.shape[0]

    widened = gather_cols(arrived, chips)
    normed = normalize(widened, norm_gain)
    gate_part = jnp.dot(normed, w_gate[0], preferred_element_type=jnp.float32)
    up_part = jnp.dot(normed, w_up[0], preferred_element_type=jnp.float32)
    hidden = (jax.nn.silu(gate_part) * up_part).astype(jnp.bfloat16)
    down = w_down[0].reshape(w_down.shape[1], chips, 2, width)
    split = jnp.einsum("sf,fkjw->jksw", hidden, down, preferred_element_type=jnp.float32)

    keep = lax.dynamic_index_in_dim(split, core, 0, keepdims=False)
    give = lax.dynamic_index_in_dim(split, 1 - core, 0, keepdims=False)
    summed = keep + lax.ppermute(give, "core", perm=[(0, 1), (1, 0)])
    shares = scatter_chips(summed)
    shares = shares.reshape(EXPERTS, CAP, width)
    returned = exchange_rows(shares, 3)
    mixed = combine_rows(returned.reshape(-1, width), slot_index, gate_weights)
    return (tokens.astype(jnp.float32) + mixed).astype(jnp.bfloat16)


def solution(mesh):
    rows, cols = mesh.devices.shape
    split_mesh = Mesh(mesh.devices.reshape(rows, cols // 2, 2), ("row", "chip", "core"))
    placed = (
        P("row", COL),
        P(),
        P("row", None),
        P("row", None),
        P("row", None, COL),
        P("row", None, COL),
        P("row", COL, None),
    )
    return jax.shard_map(
        body, mesh=split_mesh, in_specs=placed, out_specs=P("row", COL), check_vma=False
    )
```

```python
import functools

import jax
import jax.numpy as jnp
from jax import lax
from jax.experimental import pallas as pl
from jax.experimental.pallas import tpu as pltpu
from jax.sharding import Mesh
from jax.sharding import PartitionSpec as P

EXPERTS = 8
CAP = 128
COL = ("chip", "core")
MESH = pl.DeviceIdType.MESH


def normalize(rows, norm_gain):
    values = rows.astype(jnp.float32)
    inverse_norm = lax.rsqrt(jnp.mean(values * values, axis=-1, keepdims=True) + 1e-05)
    return (values * inverse_norm * norm_gain).astype(jnp.bfloat16)


def route_tables(expert_ids, expert_count, capacity):
    token_count = expert_ids.shape[0]
    flat_ids = expert_ids.reshape(-1)
    expert_range = jnp.arange(expert_count, dtype=jnp.int32)
    expert_hits = (flat_ids[:, None] == expert_range[None, :]).astype(jnp.int32)
    earlier = jnp.cumsum(expert_hits, axis=0) - expert_hits
    ranks = jnp.sum(earlier * expert_hits, axis=1)
    slot_index = (flat_ids * capacity + ranks).reshape(token_count, -1)
    slot_ids = jnp.arange(expert_count * capacity, dtype=jnp.int32)
    matches = (slot_index[:, :, None] == slot_ids[None, None, :]).astype(jnp.float32)
    picker = jnp.sum(matches, axis=1)
    return (picker.astype(jnp.bfloat16), slot_index)


def combine_rows(slot_rows, slot_index, gate_weights):
    picked = slot_rows[slot_index]
    return jnp.sum(picked * gate_weights[:, :, None], axis=1)


def gather_kernel(width, src, out, send_sem, recv_sem, local_sem):
    row, me, core = lax.axis_index("row"), lax.axis_index("chip"), lax.axis_index("core")
    side, y = me // 4, me % 4
    partner = lax.rem(me + 4, 8)
    up = side * 4 + lax.rem(y + 1, 4)
    down = side * 4 + lax.rem(y + 3, 4)
    across = side * 4 + lax.rem(y + 2, 4)
    sister = 1 - core

    barrier = pltpu.get_barrier_semaphore()
    for chip, half in ((partner, core), (up, core), (down, core), (me, sister)):
        pl.semaphore_signal(barrier, inc=1, device_id=(row, chip, half), device_id_type=MESH)
    pl.semaphore_wait(barrier, 4)

    def window(chip):
        start = pl.multiple_of((chip * 2 + core) * width, width)
        return out.at[:, pl.ds(start, width)]

    def send(tag, origin, chip, half, source=None):
        copy = pltpu.make_async_remote_copy(
            src_ref=window(origin) if source is None else source, dst_ref=window(origin),
            send_sem=send_sem.at[tag], recv_sem=recv_sem.at[tag],
            device_id=(row, chip, half), device_id_type=MESH,
        )
        copy.start()
        return copy

    sent = [
        send(0, me, partner, core, src),
        send(1, me, up, core, src),
        send(2, me, down, core, src),
        send(7, me, me, sister, src),
    ]
    local = pltpu.make_async_copy(src, window(me), local_sem)
    local.start()

    def arrive(tag, origin):
        pltpu.make_async_remote_copy(
            src_ref=window(origin), dst_ref=window(origin), send_sem=send_sem.at[tag],
            recv_sem=recv_sem.at[tag], device_id=(row, me, sister), device_id_type=MESH,
        ).wait_recv()

    other = lax.rem(partner, 8)
    arrive(0, other)
    sent += [send(3, other, up, core), send(4, other, down, core), send(8, other, me, sister)]
    arrive(1, down)
    sent += [send(5, down, up, core), send(9, down, me, sister)]
    arrive(2, up)
    sent.append(send(10, up, me, sister))
    arrive(3, lax.rem(down + 4, 8))
    sent.append(send(11, lax.rem(down + 4, 8), me, sister))
    arrive(4, lax.rem(up + 4, 8))
    sent += [send(6, lax.rem(up + 4, 8), down, core), send(12, lax.rem(up + 4, 8), me, sister)]
    arrive(5, across)
    sent.append(send(13, across, me, sister))
    arrive(6, lax.rem(across + 4, 8))
    sent.append(send(14, lax.rem(across + 4, 8), me, sister))
    local.wait()

    def sister_window(origin):
        start = pl.multiple_of((origin * 2 + sister) * width, width)
        return out.at[:, pl.ds(start, width)]

    for tag, origin in ((7, me), (8, partner), (9, down), (10, up), (11, lax.rem(down + 4, 8)),
                        (12, lax.rem(up + 4, 8)), (13, across), (14, lax.rem(across + 4, 8))):
        pltpu.make_async_remote_copy(
            src_ref=sister_window(origin), dst_ref=sister_window(origin),
            send_sem=send_sem.at[tag], recv_sem=recv_sem.at[tag],
            device_id=(row, me, sister), device_id_type=MESH,
        ).wait_recv()
    for copy in sent:
        copy.wait_send()


def gather_cols(block, chips):
    slots, width = block.shape
    return pl.pallas_call(
        functools.partial(gather_kernel, width),
        out_shape=jax.ShapeDtypeStruct((slots, chips * 2 * width), block.dtype),
        in_specs=[pl.BlockSpec(memory_space=pl.ANY)],
        out_specs=pl.BlockSpec(memory_space=pl.ANY),
        scratch_shapes=[
            pltpu.SemaphoreType.DMA((15,)),
            pltpu.SemaphoreType.DMA((15,)),
            pltpu.SemaphoreType.DMA(()),
        ],
        compiler_params=pltpu.CompilerParams(collective_id=0, has_side_effects=True),
    )(block)


def add_blocks(dst, *sources):
    rows = dst.shape[0]
    step = 128

    def one(i, carry):
        part = pl.ds(pl.multiple_of(i * step, step), step)
        total = sources[0][part, :].astype(jnp.float32)
        for source in sources[1:]:
            total = total + source[part, :].astype(jnp.float32)
        dst[part, :] = total.astype(dst.dtype)
        return carry

    lax.fori_loop(0, rows // step, one, 0)


def scatter_kernel(width, parts, out, mine, theirs, sending, landed, local_sem, sister_send,
                   sister_recv, send_sem, recv_sem):
    row, me, core = lax.axis_index("row"), lax.axis_index("chip"), lax.axis_index("core")
    sister = 1 - core
    side, y = me // 4, me % 4
    partner = lax.rem(me + 4, 8)
    up = side * 4 + lax.rem(y + 1, 4)
    down = side * 4 + lax.rem(y + 3, 4)
    across = side * 4 + lax.rem(y + 2, 4)

    def far(chip):
        return lax.rem(chip + 4, 8)

    def columns(chip, half):
        start = pl.multiple_of((chip * 2 + half) * width, width)
        return parts.at[:, pl.ds(start, width)]

    barrier = pltpu.get_barrier_semaphore()
    for chip, half in ((partner, core), (up, core), (down, core), (me, sister)):
        pl.semaphore_signal(barrier, inc=1, device_id=(row, chip, half), device_id_type=MESH)
    pl.semaphore_wait(barrier, 4)

    order = (far(down), across, up, far(across), down, far(up), partner, me)
    swaps, loads = [], []
    for slot, chip in enumerate(order):
        swap = pltpu.make_async_remote_copy(
            src_ref=columns(chip, sister), dst_ref=theirs.at[slot], send_sem=sister_send.at[slot],
            recv_sem=sister_recv.at[slot], device_id=(row, me, sister), device_id_type=MESH,
        )
        swap.start()
        swaps.append(swap)
        load = pltpu.make_async_copy(columns(chip, core), mine.at[slot], local_sem.at[slot])
        load.start()
        loads.append(load)

    def ready(slot):
        loads[slot].wait()
        swaps[slot].wait_recv()
        return (mine.at[slot], theirs.at[slot])

    def send(tag, chip):
        copy = pltpu.make_async_remote_copy(
            src_ref=sending.at[tag], dst_ref=landed.at[tag], send_sem=send_sem.at[tag],
            recv_sem=recv_sem.at[tag], device_id=(row, chip, core), device_id_type=MESH,
        )
        copy.start()
        return copy

    def arrive(tag):
        pltpu.make_async_remote_copy(
            src_ref=sending.at[tag], dst_ref=landed.at[tag], send_sem=send_sem.at[tag],
            recv_sem=recv_sem.at[tag], device_id=(row, me, core), device_id_type=MESH,
        ).wait_recv()

    sent = []
    for tag, chip in ((0, down), (1, down), (2, up), (3, up)):
        add_blocks(sending.at[tag], *ready(tag))
        sent.append(send(tag, chip))
    arrive(1)
    add_blocks(sending.at[4], *ready(4), landed.at[1])
    sent.append(send(4, down))
    arrive(3)
    add_blocks(sending.at[5], *ready(5), landed.at[3])
    sent.append(send(5, up))
    arrive(0)
    arrive(5)
    add_blocks(sending.at[6], *ready(6), landed.at[0], landed.at[5])
    sent.append(send(6, partner))
    arrive(2)
    arrive(4)
    add_blocks(out, *ready(7), landed.at[2], landed.at[4])
    arrive(6)
    add_blocks(out, out, landed.at[6])
    for copy in sent + swaps:
        copy.wait_send()


def scatter_cols(parts, width):
    slots = parts.shape[0]
    return pl.pallas_call(
        functools.partial(scatter_kernel, width),
        out_shape=jax.ShapeDtypeStruct((slots, width), jnp.float32),
        in_specs=[pl.BlockSpec(memory_space=pl.ANY)],
        out_specs=pl.BlockSpec(memory_space=pltpu.VMEM),
        scratch_shapes=[
            pltpu.VMEM((8, slots, width), jnp.float32),
            pltpu.VMEM((8, slots, width), jnp.float32),
            pltpu.VMEM((7, slots, width), jnp.bfloat16),
            pltpu.VMEM((7, slots, width), jnp.bfloat16),
            pltpu.SemaphoreType.DMA((8,)),
            pltpu.SemaphoreType.DMA((8,)),
            pltpu.SemaphoreType.DMA((8,)),
            pltpu.SemaphoreType.DMA((7,)),
            pltpu.SemaphoreType.DMA((7,)),
        ],
        compiler_params=pltpu.CompilerParams(
            collective_id=1, has_side_effects=True, vmem_limit_bytes=56 * 1024 * 1024
        ),
    )(parts)


def body(tokens, norm_gain, expert_ids, gate_weights, w_gate, w_up, w_down):
    chips = lax.psum(1, "chip")
    width = tokens.shape[1]
    core = lax.axis_index("core")

    picker, slot_index = route_tables(expert_ids, EXPERTS, CAP)
    packed = jnp.einsum("ts,td->sd", picker, tokens, preferred_element_type=jnp.float32).astype(
        jnp.bfloat16
    )
    packed = packed.reshape(EXPERTS, CAP, width)
    arrived = lax.all_to_all(packed, "row", split_axis=0, concat_axis=0, tiled=True)
    arrived = arrived.reshape(EXPERTS * CAP, width)
    slots = arrived.shape[0]

    widened = gather_cols(arrived, chips)
    normed = normalize(widened, norm_gain)
    gate_part = jnp.dot(normed, w_gate[0], preferred_element_type=jnp.float32)
    up_part = jnp.dot(normed, w_up[0], preferred_element_type=jnp.float32)
    hidden = (jax.nn.silu(gate_part) * up_part).astype(jnp.bfloat16)
    outputs = jnp.dot(hidden, w_down[0], preferred_element_type=jnp.float32)
    shares = scatter_cols(outputs, width)
    shares = shares.reshape(EXPERTS, CAP, width)
    returned = lax.all_to_all(shares, "row", split_axis=0, concat_axis=0, tiled=True)
    mixed = combine_rows(returned.reshape(-1, width), slot_index, gate_weights)
    return (tokens.astype(jnp.float32) + mixed).astype(jnp.bfloat16)


def solution(mesh):
    rows, cols = mesh.devices.shape
    split_mesh = Mesh(mesh.devices.reshape(rows, cols // 2, 2), ("row", "chip", "core"))
    placed = (
        P("row", COL),
        P(),
        P("row", None),
        P("row", None),
        P("row", None, COL),
        P("row", None, COL),
        P("row", COL, None),
    )
    return jax.shard_map(
        body, mesh=split_mesh, in_specs=placed, out_specs=P("row", COL), check_vma=False
    )
```

```python
import functools

import jax
import jax.numpy as jnp
from jax import lax
from jax.experimental import pallas as pl
from jax.experimental.pallas import tpu as pltpu
from jax.sharding import Mesh
from jax.sharding import PartitionSpec as P

EXPERTS = 8
CAP = 128
COL = ("chip", "core")
MESH = pl.DeviceIdType.MESH


def normalize(rows, norm_gain):
    values = rows.astype(jnp.float32)
    inverse_norm = lax.rsqrt(jnp.mean(values * values, axis=-1, keepdims=True) + 1e-05)
    return (values * inverse_norm * norm_gain).astype(jnp.bfloat16)


def route_tables(expert_ids, expert_count, capacity):
    token_count = expert_ids.shape[0]
    flat_ids = expert_ids.reshape(-1)
    expert_range = jnp.arange(expert_count, dtype=jnp.int32)
    expert_hits = (flat_ids[:, None] == expert_range[None, :]).astype(jnp.int32)
    earlier = jnp.cumsum(expert_hits, axis=0) - expert_hits
    ranks = jnp.sum(earlier * expert_hits, axis=1)
    slot_index = (flat_ids * capacity + ranks).reshape(token_count, -1)
    slot_ids = jnp.arange(expert_count * capacity, dtype=jnp.int32)
    matches = (slot_index[:, :, None] == slot_ids[None, None, :]).astype(jnp.float32)
    picker = jnp.sum(matches, axis=1)
    return (picker.astype(jnp.bfloat16), slot_index)


def combine_rows(slot_rows, slot_index, gate_weights):
    picked = slot_rows[slot_index]
    return jnp.sum(picked * gate_weights[:, :, None], axis=1)


def gather_kernel(width, src, out, send_sem, recv_sem, local_sem):
    row, me, core = lax.axis_index("row"), lax.axis_index("chip"), lax.axis_index("core")
    side, y = me // 4, me % 4
    partner = lax.rem(me + 4, 8)
    up = side * 4 + lax.rem(y + 1, 4)
    down = side * 4 + lax.rem(y + 3, 4)
    across = side * 4 + lax.rem(y + 2, 4)
    sister = 1 - core

    barrier = pltpu.get_barrier_semaphore()
    for chip, half in ((partner, core), (up, core), (down, core), (me, sister)):
        pl.semaphore_signal(barrier, inc=1, device_id=(row, chip, half), device_id_type=MESH)
    pl.semaphore_wait(barrier, 4)

    def window(chip):
        start = pl.multiple_of((chip * 2 + core) * width, width)
        return out.at[:, pl.ds(start, width)]

    def send(tag, origin, chip, half, source=None):
        copy = pltpu.make_async_remote_copy(
            src_ref=window(origin) if source is None else source, dst_ref=window(origin),
            send_sem=send_sem.at[tag], recv_sem=recv_sem.at[tag],
            device_id=(row, chip, half), device_id_type=MESH,
        )
        copy.start()
        return copy

    sent = [
        send(0, me, partner, core, src),
        send(1, me, up, core, src),
        send(2, me, down, core, src),
        send(7, me, me, sister, src),
    ]
    local = pltpu.make_async_copy(src, window(me), local_sem)
    local.start()

    def arrive(tag, origin):
        pltpu.make_async_remote_copy(
            src_ref=window(origin), dst_ref=window(origin), send_sem=send_sem.at[tag],
            recv_sem=recv_sem.at[tag], device_id=(row, me, sister), device_id_type=MESH,
        ).wait_recv()

    other = lax.rem(partner, 8)
    arrive(0, other)
    sent += [send(3, other, up, core), send(4, other, down, core), send(8, other, me, sister)]
    arrive(1, down)
    sent += [send(5, down, up, core), send(9, down, me, sister)]
    arrive(2, up)
    sent.append(send(10, up, me, sister))
    arrive(3, lax.rem(down + 4, 8))
    sent.append(send(11, lax.rem(down + 4, 8), me, sister))
    arrive(4, lax.rem(up + 4, 8))
    sent += [send(6, lax.rem(up + 4, 8), down, core), send(12, lax.rem(up + 4, 8), me, sister)]
    arrive(5, across)
    sent.append(send(13, across, me, sister))
    arrive(6, lax.rem(across + 4, 8))
    sent.append(send(14, lax.rem(across + 4, 8), me, sister))
    local.wait()

    def sister_window(origin):
        start = pl.multiple_of((origin * 2 + sister) * width, width)
        return out.at[:, pl.ds(start, width)]

    for tag, origin in ((7, me), (8, partner), (9, down), (10, up), (11, lax.rem(down + 4, 8)),
                        (12, lax.rem(up + 4, 8)), (13, across), (14, lax.rem(across + 4, 8))):
        pltpu.make_async_remote_copy(
            src_ref=sister_window(origin), dst_ref=sister_window(origin),
            send_sem=send_sem.at[tag], recv_sem=recv_sem.at[tag],
            device_id=(row, me, sister), device_id_type=MESH,
        ).wait_recv()
    for copy in sent:
        copy.wait_send()


def gather_cols(block, chips):
    slots, width = block.shape
    return pl.pallas_call(
        functools.partial(gather_kernel, width),
        out_shape=jax.ShapeDtypeStruct((slots, chips * 2 * width), block.dtype),
        in_specs=[pl.BlockSpec(memory_space=pl.ANY)],
        out_specs=pl.BlockSpec(memory_space=pl.ANY),
        scratch_shapes=[
            pltpu.SemaphoreType.DMA((15,)),
            pltpu.SemaphoreType.DMA((15,)),
            pltpu.SemaphoreType.DMA(()),
        ],
        compiler_params=pltpu.CompilerParams(collective_id=0, has_side_effects=True),
    )(block)


def add_blocks(dst, *sources):
    rows = dst.shape[0]
    step = 128

    def one(i, carry):
        part = pl.ds(pl.multiple_of(i * step, step), step)
        total = sources[0][part, :].astype(jnp.float32)
        for source in sources[1:]:
            total = total + source[part, :].astype(jnp.float32)
        dst[part, :] = total.astype(dst.dtype)
        return carry

    lax.fori_loop(0, rows // step, one, 0)


def project(dst, hidden, weights, start):
    rows = dst.shape[0]
    step = 256
    cols = pl.ds(pl.multiple_of(start, 256), dst.shape[1])

    def one(i, carry):
        part = pl.ds(pl.multiple_of(i * step, step), step)
        dst[part, :] = jnp.dot(hidden[part, :], weights[:, cols], preferred_element_type=jnp.float32)
        return carry

    lax.fori_loop(0, rows // step, one, 0)


def scatter_kernel(width, hidden, weights, out, mine, theirs, outgoing, sending, landed,
                   sister_send, sister_recv, send_sem, recv_sem):
    row, me, core = lax.axis_index("row"), lax.axis_index("chip"), lax.axis_index("core")
    sister = 1 - core
    side, y = me // 4, me % 4
    partner = lax.rem(me + 4, 8)
    up = side * 4 + lax.rem(y + 1, 4)
    down = side * 4 + lax.rem(y + 3, 4)
    across = side * 4 + lax.rem(y + 2, 4)

    def far(chip):
        return lax.rem(chip + 4, 8)

    barrier = pltpu.get_barrier_semaphore()
    for chip, half in ((partner, core), (up, core), (down, core), (me, sister)):
        pl.semaphore_signal(barrier, inc=1, device_id=(row, chip, half), device_id_type=MESH)
    pl.semaphore_wait(barrier, 4)

    order = (far(down), across, up, far(across), down, far(up), partner, me)
    swaps = []
    for slot, chip in enumerate(order):
        project(outgoing.at[slot], hidden, weights, (chip * 2 + sister) * width)
        swap = pltpu.make_async_remote_copy(
            src_ref=outgoing.at[slot], dst_ref=theirs.at[slot], send_sem=sister_send.at[slot],
            recv_sem=sister_recv.at[slot], device_id=(row, me, sister), device_id_type=MESH,
        )
        swap.start()
        swaps.append(swap)
        project(mine.at[slot], hidden, weights, (chip * 2 + core) * width)

    def ready(slot):
        swaps[slot].wait_recv()
        return (mine.at[slot], theirs.at[slot])

    def send(tag, chip):
        copy = pltpu.make_async_remote_copy(
            src_ref=sending.at[tag], dst_ref=landed.at[tag], send_sem=send_sem.at[tag],
            recv_sem=recv_sem.at[tag], device_id=(row, chip, core), device_id_type=MESH,
        )
        copy.start()
        return copy

    def arrive(tag):
        pltpu.make_async_remote_copy(
            src_ref=sending.at[tag], dst_ref=landed.at[tag], send_sem=send_sem.at[tag],
            recv_sem=recv_sem.at[tag], device_id=(row, me, core), device_id_type=MESH,
        ).wait_recv()

    sent = []
    for tag, chip in ((0, down), (1, down), (2, up), (3, up)):
        add_blocks(sending.at[tag], *ready(tag))
        sent.append(send(tag, chip))
    arrive(1)
    add_blocks(sending.at[4], *ready(4), landed.at[1])
    sent.append(send(4, down))
    arrive(3)
    add_blocks(sending.at[5], *ready(5), landed.at[3])
    sent.append(send(5, up))
    arrive(0)
    arrive(5)
    add_blocks(sending.at[6], *ready(6), landed.at[0], landed.at[5])
    sent.append(send(6, partner))
    arrive(2)
    arrive(4)
    add_blocks(out, *ready(7), landed.at[2], landed.at[4])
    arrive(6)
    add_blocks(out, out, landed.at[6])
    for copy in sent + swaps:
        copy.wait_send()


def scatter_cols(hidden, weights, width):
    slots = hidden.shape[0]
    return pl.pallas_call(
        functools.partial(scatter_kernel, width),
        out_shape=jax.ShapeDtypeStruct((slots, width), jnp.float32),
        in_specs=[pl.BlockSpec(memory_space=pltpu.VMEM)] * 2,
        out_specs=pl.BlockSpec(memory_space=pltpu.VMEM),
        scratch_shapes=[
            pltpu.VMEM((8, slots, width), jnp.float32),
            pltpu.VMEM((8, slots, width), jnp.float32),
            pltpu.VMEM((8, slots, width), jnp.float32),
            pltpu.VMEM((7, slots, width), jnp.bfloat16),
            pltpu.VMEM((7, slots, width), jnp.bfloat16),
            pltpu.SemaphoreType.DMA((8,)),
            pltpu.SemaphoreType.DMA((8,)),
            pltpu.SemaphoreType.DMA((7,)),
            pltpu.SemaphoreType.DMA((7,)),
        ],
        compiler_params=pltpu.CompilerParams(
            collective_id=1, has_side_effects=True, vmem_limit_bytes=60 * 1024 * 1024
        ),
    )(hidden, weights)


def body(tokens, norm_gain, expert_ids, gate_weights, w_gate, w_up, w_down):
    chips = lax.psum(1, "chip")
    width = tokens.shape[1]
    core = lax.axis_index("core")

    picker, slot_index = route_tables(expert_ids, EXPERTS, CAP)
    packed = jnp.einsum("ts,td->sd", picker, tokens, preferred_element_type=jnp.float32).astype(
        jnp.bfloat16
    )
    packed = packed.reshape(EXPERTS, CAP, width)
    arrived = lax.all_to_all(packed, "row", split_axis=0, concat_axis=0, tiled=True)
    arrived = arrived.reshape(EXPERTS * CAP, width)
    slots = arrived.shape[0]

    widened = gather_cols(arrived, chips)
    normed = normalize(widened, norm_gain)
    gate_part = jnp.dot(normed, w_gate[0], preferred_element_type=jnp.float32)
    up_part = jnp.dot(normed, w_up[0], preferred_element_type=jnp.float32)
    hidden = (jax.nn.silu(gate_part) * up_part).astype(jnp.bfloat16)
    shares = scatter_cols(hidden, w_down[0], width)
    shares = shares.reshape(EXPERTS, CAP, width)
    returned = lax.all_to_all(shares, "row", split_axis=0, concat_axis=0, tiled=True)
    mixed = combine_rows(returned.reshape(-1, width), slot_index, gate_weights)
    return (tokens.astype(jnp.float32) + mixed).astype(jnp.bfloat16)


def solution(mesh):
    rows, cols = mesh.devices.shape
    split_mesh = Mesh(mesh.devices.reshape(rows, cols // 2, 2), ("row", "chip", "core"))
    placed = (
        P("row", COL),
        P(),
        P("row", None),
        P("row", None),
        P("row", None, COL),
        P("row", None, COL),
        P("row", COL, None),
    )
    return jax.shard_map(
        body, mesh=split_mesh, in_specs=placed, out_specs=P("row", COL), check_vma=False
    )
```

```python
import functools

import jax
import jax.numpy as jnp
from jax import lax
from jax.experimental import pallas as pl
from jax.experimental.pallas import tpu as pltpu
from jax.sharding import Mesh
from jax.sharding import PartitionSpec as P

EXPERTS = 8
CAP = 128
COL = ("chip", "core")
MESH = pl.DeviceIdType.MESH


def normalize(rows, norm_gain):
    values = rows.astype(jnp.float32)
    inverse_norm = lax.rsqrt(jnp.mean(values * values, axis=-1, keepdims=True) + 1e-05)
    return (values * inverse_norm * norm_gain).astype(jnp.bfloat16)


def route_tables(expert_ids, expert_count, capacity):
    token_count = expert_ids.shape[0]
    flat_ids = expert_ids.reshape(-1)
    expert_range = jnp.arange(expert_count, dtype=jnp.int32)
    expert_hits = (flat_ids[:, None] == expert_range[None, :]).astype(jnp.int32)
    earlier = jnp.cumsum(expert_hits, axis=0) - expert_hits
    ranks = jnp.sum(earlier * expert_hits, axis=1)
    slot_index = (flat_ids * capacity + ranks).reshape(token_count, -1)
    slot_ids = jnp.arange(expert_count * capacity, dtype=jnp.int32)
    matches = (slot_index[:, :, None] == slot_ids[None, None, :]).astype(jnp.float32)
    picker = jnp.sum(matches, axis=1)
    return (picker.astype(jnp.bfloat16), slot_index)


def combine_rows(slot_rows, slot_index, gate_weights):
    picked = slot_rows[slot_index]
    return jnp.sum(picked * gate_weights[:, :, None], axis=1)


def expert_in_kernel(width, src, gain, w_gate, w_up, hidden, xs, acc_gate, acc_up, squares,
                     send_sem, recv_sem, local_sem):
    row, me, core = lax.axis_index("row"), lax.axis_index("chip"), lax.axis_index("core")
    side, y = me // 4, me % 4
    partner = lax.rem(me + 4, 8)
    up = side * 4 + lax.rem(y + 1, 4)
    down = side * 4 + lax.rem(y + 3, 4)
    across = side * 4 + lax.rem(y + 2, 4)
    sister = 1 - core
    slots = xs.shape[0]
    step = 256

    barrier = pltpu.get_barrier_semaphore()
    for chip, half in ((partner, core), (up, core), (down, core), (me, sister)):
        pl.semaphore_signal(barrier, inc=1, device_id=(row, chip, half), device_id_type=MESH)
    pl.semaphore_wait(barrier, 4)

    def window(chip, half=core):
        start = pl.multiple_of((chip * 2 + half) * width, width)
        return xs.at[:, pl.ds(start, width)]

    def send(tag, origin, chip, half, source=None):
        copy = pltpu.make_async_remote_copy(
            src_ref=window(origin) if source is None else source, dst_ref=window(origin),
            send_sem=send_sem.at[tag], recv_sem=recv_sem.at[tag],
            device_id=(row, chip, half), device_id_type=MESH,
        )
        copy.start()
        return copy

    def arrive(tag, origin, half=core):
        pltpu.make_async_remote_copy(
            src_ref=window(origin, half), dst_ref=window(origin, half), send_sem=send_sem.at[tag],
            recv_sem=recv_sem.at[tag], device_id=(row, me, sister), device_id_type=MESH,
        ).wait_recv()

    def absorb(origin, half=core, first=False):
        block = origin * 2 + half
        start = pl.multiple_of(block * width, width)
        cols = pl.ds(start, width)
        scale = gain[:, cols]

        def one(i, carry):
            part = pl.ds(pl.multiple_of(i * step, step), step)
            values = xs[part, cols].astype(jnp.float32)
            total = jnp.sum(values * values, axis=1, keepdims=True)
            scaled = (values * scale).astype(jnp.bfloat16)
            gate_part = jnp.dot(scaled, w_gate[cols, :], preferred_element_type=jnp.float32)
            up_part = jnp.dot(scaled, w_up[cols, :], preferred_element_type=jnp.float32)
            if first:
                squares[part, :] = total
                acc_gate[part, :] = gate_part
                acc_up[part, :] = up_part
            else:
                squares[part, :] += total
                acc_gate[part, :] += gate_part
                acc_up[part, :] += up_part
            return carry

        lax.fori_loop(0, slots // step, one, 0)

    sent = [
        send(0, me, partner, core, src),
        send(1, me, up, core, src),
        send(2, me, down, core, src),
        send(7, me, me, sister, src),
    ]
    local = pltpu.make_async_copy(src, window(me), local_sem)
    local.start()
    local.wait()
    absorb(me, first=True)

    arrive(0, partner)
    sent += [send(3, partner, up, core), send(4, partner, down, core),
             send(8, partner, me, sister)]
    absorb(partner)
    arrive(1, down)
    sent += [send(5, down, up, core), send(9, down, me, sister)]
    absorb(down)
    arrive(2, up)
    sent.append(send(10, up, me, sister))
    absorb(up)
    arrive(3, far(down))
    sent.append(send(11, far(down), me, sister))
    absorb(far(down))
    arrive(4, far(up))
    sent += [send(6, far(up), down, core), send(12, far(up), me, sister)]
    absorb(far(up))
    arrive(5, across)
    sent.append(send(13, across, me, sister))
    absorb(across)
    arrive(6, far(across))
    sent.append(send(14, far(across), me, sister))
    absorb(far(across))

    for tag, origin in ((7, me), (8, partner), (9, down), (10, up), (11, far(down)),
                        (12, far(up)), (13, across), (14, far(across))):
        arrive(tag, origin, sister)
        absorb(origin, sister)

    features = gain.shape[1]

    def finish(i, carry):
        part = pl.ds(pl.multiple_of(i * step, step), step)
        inverse_norm = lax.rsqrt(squares[part, :] / features + 1e-05)
        gate_values = acc_gate[part, :] * inverse_norm
        up_values = acc_up[part, :] * inverse_norm
        silu = gate_values / (1.0 + jnp.exp(-gate_values))
        hidden[part, :] = (silu * up_values).astype(hidden.dtype)
        return carry

    lax.fori_loop(0, slots // step, finish, 0)
    for copy in sent:
        copy.wait_send()


def far(chip):
    return lax.rem(chip + 4, 8)


def expert_in(block, norm_gain, w_gate, w_up, chips):
    slots, width = block.shape
    features = chips * 2 * width
    hidden_units = w_gate.shape[1]
    return pl.pallas_call(
        functools.partial(expert_in_kernel, width),
        out_shape=jax.ShapeDtypeStruct((slots, hidden_units), jnp.bfloat16),
        in_specs=[pl.BlockSpec(memory_space=pltpu.VMEM)] * 4,
        out_specs=pl.BlockSpec(memory_space=pltpu.VMEM),
        scratch_shapes=[
            pltpu.VMEM((slots, features), jnp.bfloat16),
            pltpu.VMEM((slots, hidden_units), jnp.float32),
            pltpu.VMEM((slots, hidden_units), jnp.float32),
            pltpu.VMEM((slots, 1), jnp.float32),
            pltpu.SemaphoreType.DMA((15,)),
            pltpu.SemaphoreType.DMA((15,)),
            pltpu.SemaphoreType.DMA(()),
        ],
        compiler_params=pltpu.CompilerParams(
            collective_id=0, has_side_effects=True, vmem_limit_bytes=60 * 1024 * 1024
        ),
    )(block, norm_gain.reshape(1, features), w_gate, w_up)


def add_blocks(dst, *sources):
    rows = dst.shape[0]
    step = 128

    def one(i, carry):
        part = pl.ds(pl.multiple_of(i * step, step), step)
        total = sources[0][part, :].astype(jnp.float32)
        for source in sources[1:]:
            total = total + source[part, :].astype(jnp.float32)
        dst[part, :] = total.astype(dst.dtype)
        return carry

    lax.fori_loop(0, rows // step, one, 0)


def scatter_kernel(width, parts, out, mine, theirs, sending, landed, local_sem, sister_send,
                   sister_recv, send_sem, recv_sem):
    row, me, core = lax.axis_index("row"), lax.axis_index("chip"), lax.axis_index("core")
    sister = 1 - core
    side, y = me // 4, me % 4
    partner = lax.rem(me + 4, 8)
    up = side * 4 + lax.rem(y + 1, 4)
    down = side * 4 + lax.rem(y + 3, 4)
    across = side * 4 + lax.rem(y + 2, 4)

    def far(chip):
        return lax.rem(chip + 4, 8)

    def columns(chip, half):
        start = pl.multiple_of((chip * 2 + half) * width, width)
        return parts.at[:, pl.ds(start, width)]

    barrier = pltpu.get_barrier_semaphore()
    for chip, half in ((partner, core), (up, core), (down, core), (me, sister)):
        pl.semaphore_signal(barrier, inc=1, device_id=(row, chip, half), device_id_type=MESH)
    pl.semaphore_wait(barrier, 4)

    order = (far(down), across, up, far(across), down, far(up), partner, me)
    swaps, loads = [], []
    for slot, chip in enumerate(order):
        swap = pltpu.make_async_remote_copy(
            src_ref=columns(chip, sister), dst_ref=theirs.at[slot], send_sem=sister_send.at[slot],
            recv_sem=sister_recv.at[slot], device_id=(row, me, sister), device_id_type=MESH,
        )
        swap.start()
        swaps.append(swap)
        load = pltpu.make_async_copy(columns(chip, core), mine.at[slot], local_sem.at[slot])
        load.start()
        loads.append(load)

    def ready(slot):
        loads[slot].wait()
        swaps[slot].wait_recv()
        return (mine.at[slot], theirs.at[slot])

    def send(tag, chip):
        copy = pltpu.make_async_remote_copy(
            src_ref=sending.at[tag], dst_ref=landed.at[tag], send_sem=send_sem.at[tag],
            recv_sem=recv_sem.at[tag], device_id=(row, chip, core), device_id_type=MESH,
        )
        copy.start()
        return copy

    def arrive(tag):
        pltpu.make_async_remote_copy(
            src_ref=sending.at[tag], dst_ref=landed.at[tag], send_sem=send_sem.at[tag],
            recv_sem=recv_sem.at[tag], device_id=(row, me, core), device_id_type=MESH,
        ).wait_recv()

    sent = []
    for tag, chip in ((0, down), (1, down), (2, up), (3, up)):
        add_blocks(sending.at[tag], *ready(tag))
        sent.append(send(tag, chip))
    arrive(1)
    add_blocks(sending.at[4], *ready(4), landed.at[1])
    sent.append(send(4, down))
    arrive(3)
    add_blocks(sending.at[5], *ready(5), landed.at[3])
    sent.append(send(5, up))
    arrive(0)
    arrive(5)
    add_blocks(sending.at[6], *ready(6), landed.at[0], landed.at[5])
    sent.append(send(6, partner))
    arrive(2)
    arrive(4)
    add_blocks(out, *ready(7), landed.at[2], landed.at[4])
    arrive(6)
    add_blocks(out, out, landed.at[6])
    for copy in sent + swaps:
        copy.wait_send()


def scatter_cols(parts, width):
    slots = parts.shape[0]
    return pl.pallas_call(
        functools.partial(scatter_kernel, width),
        out_shape=jax.ShapeDtypeStruct((slots, width), jnp.float32),
        in_specs=[pl.BlockSpec(memory_space=pl.ANY)],
        out_specs=pl.BlockSpec(memory_space=pltpu.VMEM),
        scratch_shapes=[
            pltpu.VMEM((8, slots, width), jnp.float32),
            pltpu.VMEM((8, slots, width), jnp.float32),
            pltpu.VMEM((7, slots, width), jnp.bfloat16),
            pltpu.VMEM((7, slots, width), jnp.bfloat16),
            pltpu.SemaphoreType.DMA((8,)),
            pltpu.SemaphoreType.DMA((8,)),
            pltpu.SemaphoreType.DMA((8,)),
            pltpu.SemaphoreType.DMA((7,)),
            pltpu.SemaphoreType.DMA((7,)),
        ],
        compiler_params=pltpu.CompilerParams(
            collective_id=1, has_side_effects=True, vmem_limit_bytes=56 * 1024 * 1024
        ),
    )(parts)


def body(tokens, norm_gain, expert_ids, gate_weights, w_gate, w_up, w_down):
    chips = lax.psum(1, "chip")
    width = tokens.shape[1]
    core = lax.axis_index("core")

    picker, slot_index = route_tables(expert_ids, EXPERTS, CAP)
    packed = jnp.einsum("ts,td->sd", picker, tokens, preferred_element_type=jnp.float32).astype(
        jnp.bfloat16
    )
    packed = packed.reshape(EXPERTS, CAP, width)
    arrived = lax.all_to_all(packed, "row", split_axis=0, concat_axis=0, tiled=True)
    arrived = arrived.reshape(EXPERTS * CAP, width)
    slots = arrived.shape[0]

    hidden = expert_in(arrived, norm_gain, w_gate[0], w_up[0], chips)
    outputs = jnp.dot(hidden, w_down[0], preferred_element_type=jnp.float32)
    shares = scatter_cols(outputs, width)
    shares = shares.reshape(EXPERTS, CAP, width)
    returned = lax.all_to_all(shares, "row", split_axis=0, concat_axis=0, tiled=True)
    mixed = combine_rows(returned.reshape(-1, width), slot_index, gate_weights)
    return (tokens.astype(jnp.float32) + mixed).astype(jnp.bfloat16)


def solution(mesh):
    rows, cols = mesh.devices.shape
    split_mesh = Mesh(mesh.devices.reshape(rows, cols // 2, 2), ("row", "chip", "core"))
    placed = (
        P("row", COL),
        P(),
        P("row", None),
        P("row", None),
        P("row", None, COL),
        P("row", None, COL),
        P("row", COL, None),
    )
    return jax.shard_map(
        body, mesh=split_mesh, in_specs=placed, out_specs=P("row", COL), check_vma=False
    )
```

```python
import functools

import jax
import jax.numpy as jnp
from jax import lax
from jax.experimental import pallas as pl
from jax.experimental.pallas import tpu as pltpu
from jax.sharding import Mesh
from jax.sharding import PartitionSpec as P

EXPERTS = 8
CAP = 128
COL = ("chip", "core")
MESH = pl.DeviceIdType.MESH


def normalize(rows, norm_gain):
    values = rows.astype(jnp.float32)
    inverse_norm = lax.rsqrt(jnp.mean(values * values, axis=-1, keepdims=True) + 1e-05)
    return (values * inverse_norm * norm_gain).astype(jnp.bfloat16)


def route_tables(expert_ids, expert_count, capacity):
    token_count = expert_ids.shape[0]
    flat_ids = expert_ids.reshape(-1)
    expert_range = jnp.arange(expert_count, dtype=jnp.int32)
    expert_hits = (flat_ids[:, None] == expert_range[None, :]).astype(jnp.int32)
    earlier = jnp.cumsum(expert_hits, axis=0) - expert_hits
    ranks = jnp.sum(earlier * expert_hits, axis=1)
    slot_index = (flat_ids * capacity + ranks).reshape(token_count, -1)
    slot_ids = jnp.arange(expert_count * capacity, dtype=jnp.int32)
    matches = (slot_index[:, :, None] == slot_ids[None, None, :]).astype(jnp.float32)
    picker = jnp.sum(matches, axis=1)
    return (picker.astype(jnp.bfloat16), slot_index)


def combine_rows(slot_rows, slot_index, gate_weights):
    picked = slot_rows[slot_index]
    return jnp.sum(picked * gate_weights[:, :, None], axis=1)


def expert_in_kernel(width, src, squares_part, gain, w_gate_hbm, w_up_hbm, hidden, xs, w_gate,
                     w_up, acc_gate, acc_up, squares, send_sem, recv_sem, local_sem, weight_sem,
                     square_send, square_recv):
    row, me, core = lax.axis_index("row"), lax.axis_index("chip"), lax.axis_index("core")
    side, y = me // 4, me % 4
    partner = lax.rem(me + 4, 8)
    up = side * 4 + lax.rem(y + 1, 4)
    down = side * 4 + lax.rem(y + 3, 4)
    across = side * 4 + lax.rem(y + 2, 4)
    sister = 1 - core
    slots = xs.shape[0]
    step = 256
    blocks = squares.shape[0]
    mine = me * 2 + core

    loads = [pltpu.make_async_copy(w_gate_hbm, w_gate, weight_sem.at[0]),
             pltpu.make_async_copy(w_up_hbm, w_up, weight_sem.at[1])]
    for load in loads:
        load.start()

    barrier = pltpu.get_barrier_semaphore()
    for d in range(1, blocks):
        other = lax.rem(mine + d, blocks)
        pl.semaphore_signal(barrier, inc=1, device_id=(row, other // 2, other % 2),
                            device_id_type=MESH)
    pl.semaphore_wait(barrier, blocks - 1)

    square_copies = []
    for d in range(1, blocks):
        other = lax.rem(mine + d, blocks)
        copy = pltpu.make_async_remote_copy(
            src_ref=squares_part, dst_ref=squares.at[mine], send_sem=square_send.at[d],
            recv_sem=square_recv.at[d], device_id=(row, other // 2, other % 2),
            device_id_type=MESH,
        )
        copy.start()
        square_copies.append(copy)

    def window(chip, half=core):
        start = pl.multiple_of((chip * 2 + half) * width, width)
        return xs.at[:, pl.ds(start, width)]

    def send(tag, origin, chip, half, source=None):
        copy = pltpu.make_async_remote_copy(
            src_ref=window(origin) if source is None else source, dst_ref=window(origin),
            send_sem=send_sem.at[tag], recv_sem=recv_sem.at[tag],
            device_id=(row, chip, half), device_id_type=MESH,
        )
        copy.start()
        return copy

    def arrive(tag, origin, half=core):
        pltpu.make_async_remote_copy(
            src_ref=window(origin, half), dst_ref=window(origin, half), send_sem=send_sem.at[tag],
            recv_sem=recv_sem.at[tag], device_id=(row, me, sister), device_id_type=MESH,
        ).wait_recv()

    sent = [
        send(0, me, partner, core, src),
        send(1, me, up, core, src),
        send(2, me, down, core, src),
        send(7, me, me, sister, src),
    ]
    local = pltpu.make_async_copy(src, window(me), local_sem)
    local.start()
    squares[mine] = squares_part[...]
    for copy in square_copies:
        copy.wait_recv()
    total = squares[0]
    for b in range(1, blocks):
        total = total + squares[b]
    inverse_norm = lax.rsqrt(total / (blocks * width) + 1e-05)
    squares[0] = inverse_norm
    for load in loads:
        load.wait()
    local.wait()

    def absorb(origin, half=core, first=False):
        block = origin * 2 + half
        start = pl.multiple_of(block * width, width)
        cols = pl.ds(start, width)
        scale = gain[:, cols]

        def one(i, carry):
            part = pl.ds(pl.multiple_of(i * step, step), step)
            spread = jnp.broadcast_to(squares[0, pl.ds(i, 1), :], (128, step))
            column = jnp.transpose(spread)[:, 0:1]
            values = xs[part, cols].astype(jnp.float32)
            normed = (values * column * scale).astype(jnp.bfloat16)
            gate_part = jnp.dot(normed, w_gate[cols, :], preferred_element_type=jnp.float32)
            up_part = jnp.dot(normed, w_up[cols, :], preferred_element_type=jnp.float32)
            if first:
                acc_gate[part, :] = gate_part
                acc_up[part, :] = up_part
            else:
                acc_gate[part, :] += gate_part
                acc_up[part, :] += up_part
            return carry

        lax.fori_loop(0, slots // step, one, 0)

    absorb(me, first=True)
    arrive(0, partner)
    sent += [send(3, partner, up, core), send(4, partner, down, core),
             send(8, partner, me, sister)]
    absorb(partner)
    arrive(1, down)
    sent += [send(5, down, up, core), send(9, down, me, sister)]
    absorb(down)
    arrive(2, up)
    sent.append(send(10, up, me, sister))
    absorb(up)
    arrive(3, far(down))
    sent.append(send(11, far(down), me, sister))
    absorb(far(down))
    arrive(4, far(up))
    sent += [send(6, far(up), down, core), send(12, far(up), me, sister)]
    absorb(far(up))
    arrive(5, across)
    sent.append(send(13, across, me, sister))
    absorb(across)
    arrive(6, far(across))
    sent.append(send(14, far(across), me, sister))
    absorb(far(across))

    for tag, origin in ((7, me), (8, partner), (9, down), (10, up), (11, far(down)),
                        (12, far(up)), (13, across), (14, far(across))):
        arrive(tag, origin, sister)
        absorb(origin, sister)

    def finish(i, carry):
        part = pl.ds(pl.multiple_of(i * step, step), step)
        gate_values = acc_gate[part, :]
        silu = gate_values / (1.0 + jnp.exp(-gate_values))
        hidden[part, :] = (silu * acc_up[part, :]).astype(hidden.dtype)
        return carry

    lax.fori_loop(0, slots // step, finish, 0)
    for copy in sent + square_copies:
        copy.wait_send()


def far(chip):
    return lax.rem(chip + 4, 8)


def expert_in(block, norm_gain, w_gate, w_up, chips):
    slots, width = block.shape
    blocks = chips * 2
    features = blocks * width
    hidden_units = w_gate.shape[1]
    values = block.astype(jnp.float32)
    squares_part = jnp.sum(values * values, axis=1).reshape(slots // 256, 256)
    return pl.pallas_call(
        functools.partial(expert_in_kernel, width),
        out_shape=jax.ShapeDtypeStruct((slots, hidden_units), jnp.bfloat16),
        in_specs=[pl.BlockSpec(memory_space=pltpu.VMEM)] * 3
        + [pl.BlockSpec(memory_space=pl.ANY)] * 2,
        out_specs=pl.BlockSpec(memory_space=pltpu.VMEM),
        scratch_shapes=[
            pltpu.VMEM((slots, features), jnp.bfloat16),
            pltpu.VMEM(w_gate.shape, w_gate.dtype),
            pltpu.VMEM(w_up.shape, w_up.dtype),
            pltpu.VMEM((slots, hidden_units), jnp.float32),
            pltpu.VMEM((slots, hidden_units), jnp.float32),
            pltpu.VMEM((blocks, slots // 256, 256), jnp.float32),
            pltpu.SemaphoreType.DMA((15,)),
            pltpu.SemaphoreType.DMA((15,)),
            pltpu.SemaphoreType.DMA(()),
            pltpu.SemaphoreType.DMA((2,)),
            pltpu.SemaphoreType.DMA((blocks,)),
            pltpu.SemaphoreType.DMA((blocks,)),
        ],
        compiler_params=pltpu.CompilerParams(
            collective_id=0, has_side_effects=True, vmem_limit_bytes=60 * 1024 * 1024
        ),
    )(block, squares_part, norm_gain.reshape(1, features), w_gate, w_up)


def add_blocks(dst, *sources):
    rows = dst.shape[0]
    step = 128

    def one(i, carry):
        part = pl.ds(pl.multiple_of(i * step, step), step)
        total = sources[0][part, :].astype(jnp.float32)
        for source in sources[1:]:
            total = total + source[part, :].astype(jnp.float32)
        dst[part, :] = total.astype(dst.dtype)
        return carry

    lax.fori_loop(0, rows // step, one, 0)


def scatter_kernel(width, parts, out, mine, theirs, sending, landed, local_sem, sister_send,
                   sister_recv, send_sem, recv_sem):
    row, me, core = lax.axis_index("row"), lax.axis_index("chip"), lax.axis_index("core")
    sister = 1 - core
    side, y = me // 4, me % 4
    partner = lax.rem(me + 4, 8)
    up = side * 4 + lax.rem(y + 1, 4)
    down = side * 4 + lax.rem(y + 3, 4)
    across = side * 4 + lax.rem(y + 2, 4)

    def far(chip):
        return lax.rem(chip + 4, 8)

    def columns(chip, half):
        start = pl.multiple_of((chip * 2 + half) * width, width)
        return parts.at[:, pl.ds(start, width)]

    barrier = pltpu.get_barrier_semaphore()
    for chip, half in ((partner, core), (up, core), (down, core), (me, sister)):
        pl.semaphore_signal(barrier, inc=1, device_id=(row, chip, half), device_id_type=MESH)
    pl.semaphore_wait(barrier, 4)

    order = (far(down), across, up, far(across), down, far(up), partner, me)
    swaps, loads = [], []
    for slot, chip in enumerate(order):
        swap = pltpu.make_async_remote_copy(
            src_ref=columns(chip, sister), dst_ref=theirs.at[slot], send_sem=sister_send.at[slot],
            recv_sem=sister_recv.at[slot], device_id=(row, me, sister), device_id_type=MESH,
        )
        swap.start()
        swaps.append(swap)
        load = pltpu.make_async_copy(columns(chip, core), mine.at[slot], local_sem.at[slot])
        load.start()
        loads.append(load)

    def ready(slot):
        loads[slot].wait()
        swaps[slot].wait_recv()
        return (mine.at[slot], theirs.at[slot])

    def send(tag, chip):
        copy = pltpu.make_async_remote_copy(
            src_ref=sending.at[tag], dst_ref=landed.at[tag], send_sem=send_sem.at[tag],
            recv_sem=recv_sem.at[tag], device_id=(row, chip, core), device_id_type=MESH,
        )
        copy.start()
        return copy

    def arrive(tag):
        pltpu.make_async_remote_copy(
            src_ref=sending.at[tag], dst_ref=landed.at[tag], send_sem=send_sem.at[tag],
            recv_sem=recv_sem.at[tag], device_id=(row, me, core), device_id_type=MESH,
        ).wait_recv()

    sent = []
    for tag, chip in ((0, down), (1, down), (2, up), (3, up)):
        add_blocks(sending.at[tag], *ready(tag))
        sent.append(send(tag, chip))
    arrive(1)
    add_blocks(sending.at[4], *ready(4), landed.at[1])
    sent.append(send(4, down))
    arrive(3)
    add_blocks(sending.at[5], *ready(5), landed.at[3])
    sent.append(send(5, up))
    arrive(0)
    arrive(5)
    add_blocks(sending.at[6], *ready(6), landed.at[0], landed.at[5])
    sent.append(send(6, partner))
    arrive(2)
    arrive(4)
    add_blocks(out, *ready(7), landed.at[2], landed.at[4])
    arrive(6)
    add_blocks(out, out, landed.at[6])
    for copy in sent + swaps:
        copy.wait_send()


def scatter_cols(parts, width):
    slots = parts.shape[0]
    return pl.pallas_call(
        functools.partial(scatter_kernel, width),
        out_shape=jax.ShapeDtypeStruct((slots, width), jnp.float32),
        in_specs=[pl.BlockSpec(memory_space=pl.ANY)],
        out_specs=pl.BlockSpec(memory_space=pltpu.VMEM),
        scratch_shapes=[
            pltpu.VMEM((8, slots, width), jnp.float32),
            pltpu.VMEM((8, slots, width), jnp.float32),
            pltpu.VMEM((7, slots, width), jnp.bfloat16),
            pltpu.VMEM((7, slots, width), jnp.bfloat16),
            pltpu.SemaphoreType.DMA((8,)),
            pltpu.SemaphoreType.DMA((8,)),
            pltpu.SemaphoreType.DMA((8,)),
            pltpu.SemaphoreType.DMA((7,)),
            pltpu.SemaphoreType.DMA((7,)),
        ],
        compiler_params=pltpu.CompilerParams(
            collective_id=1, has_side_effects=True, vmem_limit_bytes=56 * 1024 * 1024
        ),
    )(parts)


def body(tokens, norm_gain, expert_ids, gate_weights, w_gate, w_up, w_down):
    chips = lax.psum(1, "chip")
    width = tokens.shape[1]
    core = lax.axis_index("core")

    picker, slot_index = route_tables(expert_ids, EXPERTS, CAP)
    packed = jnp.einsum("ts,td->sd", picker, tokens, preferred_element_type=jnp.float32).astype(
        jnp.bfloat16
    )
    packed = packed.reshape(EXPERTS, CAP, width)
    arrived = lax.all_to_all(packed, "row", split_axis=0, concat_axis=0, tiled=True)
    arrived = arrived.reshape(EXPERTS * CAP, width)
    slots = arrived.shape[0]

    hidden = expert_in(arrived, norm_gain, w_gate[0], w_up[0], chips)
    outputs = jnp.dot(hidden, w_down[0], preferred_element_type=jnp.float32)
    shares = scatter_cols(outputs, width)
    shares = shares.reshape(EXPERTS, CAP, width)
    returned = lax.all_to_all(shares, "row", split_axis=0, concat_axis=0, tiled=True)
    mixed = combine_rows(returned.reshape(-1, width), slot_index, gate_weights)
    return (tokens.astype(jnp.float32) + mixed).astype(jnp.bfloat16)


def solution(mesh):
    rows, cols = mesh.devices.shape
    split_mesh = Mesh(mesh.devices.reshape(rows, cols // 2, 2), ("row", "chip", "core"))
    placed = (
        P("row", COL),
        P(),
        P("row", None),
        P("row", None),
        P("row", None, COL),
        P("row", None, COL),
        P("row", COL, None),
    )
    return jax.shard_map(
        body, mesh=split_mesh, in_specs=placed, out_specs=P("row", COL), check_vma=False
    )
```

```python
import functools

import jax
import jax.numpy as jnp
from jax import lax
from jax.experimental import pallas as pl
from jax.experimental.pallas import tpu as pltpu
from jax.sharding import Mesh
from jax.sharding import PartitionSpec as P

EXPERTS = 8
CAP = 128
COL = ("chip", "core")
MESH = pl.DeviceIdType.MESH


def normalize(rows, norm_gain):
    values = rows.astype(jnp.float32)
    inverse_norm = lax.rsqrt(jnp.mean(values * values, axis=-1, keepdims=True) + 1e-05)
    return (values * inverse_norm * norm_gain).astype(jnp.bfloat16)


def route_tables(expert_ids, expert_count, capacity):
    token_count = expert_ids.shape[0]
    flat_ids = expert_ids.reshape(-1)
    expert_range = jnp.arange(expert_count, dtype=jnp.int32)
    expert_hits = (flat_ids[:, None] == expert_range[None, :]).astype(jnp.int32)
    earlier = jnp.cumsum(expert_hits, axis=0) - expert_hits
    ranks = jnp.sum(earlier * expert_hits, axis=1)
    slot_index = (flat_ids * capacity + ranks).reshape(token_count, -1)
    slot_ids = jnp.arange(expert_count * capacity, dtype=jnp.int32)
    matches = (slot_index[:, :, None] == slot_ids[None, None, :]).astype(jnp.float32)
    picker = jnp.sum(matches, axis=1)
    return (picker.astype(jnp.bfloat16), slot_index)


def combine_rows(slot_rows, slot_index, gate_weights):
    picked = slot_rows[slot_index]
    return jnp.sum(picked * gate_weights[:, :, None], axis=1)


def expert_in_kernel(width, src, squares_part, gain, w_gate_hbm, w_up_hbm, hidden, xs, w_gate,
                     w_up, acc_gate, acc_up, squares, send_sem, recv_sem, local_sem, weight_sem,
                     square_send, square_recv):
    row, me, core = lax.axis_index("row"), lax.axis_index("chip"), lax.axis_index("core")
    side, y = me // 4, me % 4
    partner = lax.rem(me + 4, 8)
    up = side * 4 + lax.rem(y + 1, 4)
    down = side * 4 + lax.rem(y + 3, 4)
    across = side * 4 + lax.rem(y + 2, 4)
    sister = 1 - core
    slots = xs.shape[0]
    step = 256
    blocks = squares.shape[0]
    mine = me * 2 + core

    loads = [pltpu.make_async_copy(w_gate_hbm, w_gate, weight_sem.at[0]),
             pltpu.make_async_copy(w_up_hbm, w_up, weight_sem.at[1])]
    for load in loads:
        load.start()

    barrier = pltpu.get_barrier_semaphore()
    for d in range(1, blocks):
        other = lax.rem(mine + d, blocks)
        pl.semaphore_signal(barrier, inc=1, device_id=(row, other // 2, other % 2),
                            device_id_type=MESH)
    pl.semaphore_wait(barrier, blocks - 1)

    square_copies = []
    for d in range(1, blocks):
        other = lax.rem(mine + d, blocks)
        copy = pltpu.make_async_remote_copy(
            src_ref=squares_part, dst_ref=squares.at[mine], send_sem=square_send.at[d],
            recv_sem=square_recv.at[d], device_id=(row, other // 2, other % 2),
            device_id_type=MESH,
        )
        copy.start()
        square_copies.append(copy)

    def window(chip, half=core):
        start = pl.multiple_of((chip * 2 + half) * width, width)
        return xs.at[:, pl.ds(start, width)]

    def send(tag, origin, chip, half, source=None):
        copy = pltpu.make_async_remote_copy(
            src_ref=window(origin) if source is None else source, dst_ref=window(origin),
            send_sem=send_sem.at[tag], recv_sem=recv_sem.at[tag],
            device_id=(row, chip, half), device_id_type=MESH,
        )
        copy.start()
        return copy

    def arrive(tag, origin, half=core):
        pltpu.make_async_remote_copy(
            src_ref=window(origin, half), dst_ref=window(origin, half), send_sem=send_sem.at[tag],
            recv_sem=recv_sem.at[tag], device_id=(row, me, sister), device_id_type=MESH,
        ).wait_recv()

    sent = [
        send(0, me, partner, core, src),
        send(1, me, up, core, src),
        send(2, me, down, core, src),
        send(7, me, me, sister, src),
    ]
    local = pltpu.make_async_copy(src, window(me), local_sem)
    local.start()
    squares[mine] = squares_part[...]
    for copy in square_copies:
        copy.wait_recv()
    total = squares[0]
    for b in range(1, blocks):
        total = total + squares[b]
    inverse_norm = lax.rsqrt(total / (blocks * width) + 1e-05)
    squares[0] = inverse_norm
    for load in loads:
        load.wait()
    local.wait()

    def absorb(origin, half=core, first=False):
        block = origin * 2 + half
        start = pl.multiple_of(block * width, width)
        cols = pl.ds(start, width)
        scale = gain[:, cols]

        def one(i, carry):
            part = pl.ds(pl.multiple_of(i * step, step), step)
            spread = jnp.broadcast_to(squares[0, pl.ds(i, 1), :], (128, step))
            column = jnp.transpose(spread)[:, 0:1]
            values = xs[part, cols].astype(jnp.float32)
            normed = (values * column * scale).astype(jnp.bfloat16)
            gate_part = jnp.dot(normed, w_gate[cols, :], preferred_element_type=jnp.float32)
            up_part = jnp.dot(normed, w_up[cols, :], preferred_element_type=jnp.float32)
            if first:
                acc_gate[part, :] = gate_part
                acc_up[part, :] = up_part
            else:
                acc_gate[part, :] += gate_part
                acc_up[part, :] += up_part
            return carry

        lax.fori_loop(0, slots // step, one, 0)

    absorb(me, first=True)
    arrive(0, partner)
    sent += [send(3, partner, up, core), send(4, partner, down, core),
             send(8, partner, me, sister)]
    arrive(1, down)
    sent += [send(5, down, up, core), send(9, down, me, sister)]
    arrive(2, up)
    sent.append(send(10, up, me, sister))
    absorb(partner)
    arrive(3, far(down))
    sent.append(send(11, far(down), me, sister))
    arrive(4, far(up))
    sent += [send(6, far(up), down, core), send(12, far(up), me, sister)]
    absorb(down)
    arrive(5, across)
    sent.append(send(13, across, me, sister))
    arrive(6, far(across))
    sent.append(send(14, far(across), me, sister))
    for origin in (up, far(down), far(up), across, far(across)):
        absorb(origin)

    for tag, origin in ((7, me), (8, partner), (9, down), (10, up), (11, far(down)),
                        (12, far(up)), (13, across), (14, far(across))):
        arrive(tag, origin, sister)
        absorb(origin, sister)

    def finish(i, carry):
        part = pl.ds(pl.multiple_of(i * step, step), step)
        gate_values = acc_gate[part, :]
        silu = gate_values / (1.0 + jnp.exp(-gate_values))
        hidden[part, :] = (silu * acc_up[part, :]).astype(hidden.dtype)
        return carry

    lax.fori_loop(0, slots // step, finish, 0)
    for copy in sent + square_copies:
        copy.wait_send()


def far(chip):
    return lax.rem(chip + 4, 8)


def expert_in(block, norm_gain, w_gate, w_up, chips):
    slots, width = block.shape
    blocks = chips * 2
    features = blocks * width
    hidden_units = w_gate.shape[1]
    values = block.astype(jnp.float32)
    squares_part = jnp.sum(values * values, axis=1).reshape(slots // 256, 256)
    return pl.pallas_call(
        functools.partial(expert_in_kernel, width),
        out_shape=jax.ShapeDtypeStruct((slots, hidden_units), jnp.bfloat16),
        in_specs=[pl.BlockSpec(memory_space=pltpu.VMEM)] * 3
        + [pl.BlockSpec(memory_space=pl.ANY)] * 2,
        out_specs=pl.BlockSpec(memory_space=pltpu.VMEM),
        scratch_shapes=[
            pltpu.VMEM((slots, features), jnp.bfloat16),
            pltpu.VMEM(w_gate.shape, w_gate.dtype),
            pltpu.VMEM(w_up.shape, w_up.dtype),
            pltpu.VMEM((slots, hidden_units), jnp.float32),
            pltpu.VMEM((slots, hidden_units), jnp.float32),
            pltpu.VMEM((blocks, slots // 256, 256), jnp.float32),
            pltpu.SemaphoreType.DMA((15,)),
            pltpu.SemaphoreType.DMA((15,)),
            pltpu.SemaphoreType.DMA(()),
            pltpu.SemaphoreType.DMA((2,)),
            pltpu.SemaphoreType.DMA((blocks,)),
            pltpu.SemaphoreType.DMA((blocks,)),
        ],
        compiler_params=pltpu.CompilerParams(
            collective_id=0, has_side_effects=True, vmem_limit_bytes=60 * 1024 * 1024
        ),
    )(block, squares_part, norm_gain.reshape(1, features), w_gate, w_up)


def add_blocks(dst, *sources):
    rows = dst.shape[0]
    step = 128

    def one(i, carry):
        part = pl.ds(pl.multiple_of(i * step, step), step)
        total = sources[0][part, :].astype(jnp.float32)
        for source in sources[1:]:
            total = total + source[part, :].astype(jnp.float32)
        dst[part, :] = total.astype(dst.dtype)
        return carry

    lax.fori_loop(0, rows // step, one, 0)


def scatter_kernel(width, parts, out, mine, theirs, sending, landed, local_sem, sister_send,
                   sister_recv, send_sem, recv_sem):
    row, me, core = lax.axis_index("row"), lax.axis_index("chip"), lax.axis_index("core")
    sister = 1 - core
    side, y = me // 4, me % 4
    partner = lax.rem(me + 4, 8)
    up = side * 4 + lax.rem(y + 1, 4)
    down = side * 4 + lax.rem(y + 3, 4)
    across = side * 4 + lax.rem(y + 2, 4)

    def far(chip):
        return lax.rem(chip + 4, 8)

    def columns(chip, half):
        start = pl.multiple_of((chip * 2 + half) * width, width)
        return parts.at[:, pl.ds(start, width)]

    barrier = pltpu.get_barrier_semaphore()
    for chip, half in ((partner, core), (up, core), (down, core), (me, sister)):
        pl.semaphore_signal(barrier, inc=1, device_id=(row, chip, half), device_id_type=MESH)
    pl.semaphore_wait(barrier, 4)

    order = (far(down), across, up, far(across), down, far(up), partner, me)
    swaps, loads = [], []
    for slot, chip in enumerate(order):
        swap = pltpu.make_async_remote_copy(
            src_ref=columns(chip, sister), dst_ref=theirs.at[slot], send_sem=sister_send.at[slot],
            recv_sem=sister_recv.at[slot], device_id=(row, me, sister), device_id_type=MESH,
        )
        swap.start()
        swaps.append(swap)
        load = pltpu.make_async_copy(columns(chip, core), mine.at[slot], local_sem.at[slot])
        load.start()
        loads.append(load)

    def ready(slot):
        loads[slot].wait()
        swaps[slot].wait_recv()
        return (mine.at[slot], theirs.at[slot])

    def send(tag, chip):
        copy = pltpu.make_async_remote_copy(
            src_ref=sending.at[tag], dst_ref=landed.at[tag], send_sem=send_sem.at[tag],
            recv_sem=recv_sem.at[tag], device_id=(row, chip, core), device_id_type=MESH,
        )
        copy.start()
        return copy

    def arrive(tag):
        pltpu.make_async_remote_copy(
            src_ref=sending.at[tag], dst_ref=landed.at[tag], send_sem=send_sem.at[tag],
            recv_sem=recv_sem.at[tag], device_id=(row, me, core), device_id_type=MESH,
        ).wait_recv()

    sent = []
    for tag, chip in ((0, down), (1, down), (2, up), (3, up)):
        add_blocks(sending.at[tag], *ready(tag))
        sent.append(send(tag, chip))
    arrive(1)
    add_blocks(sending.at[4], *ready(4), landed.at[1])
    sent.append(send(4, down))
    arrive(3)
    add_blocks(sending.at[5], *ready(5), landed.at[3])
    sent.append(send(5, up))
    arrive(0)
    arrive(5)
    add_blocks(sending.at[6], *ready(6), landed.at[0], landed.at[5])
    sent.append(send(6, partner))
    arrive(2)
    arrive(4)
    add_blocks(out, *ready(7), landed.at[2], landed.at[4])
    arrive(6)
    add_blocks(out, out, landed.at[6])
    for copy in sent + swaps:
        copy.wait_send()


def scatter_cols(parts, width):
    slots = parts.shape[0]
    return pl.pallas_call(
        functools.partial(scatter_kernel, width),
        out_shape=jax.ShapeDtypeStruct((slots, width), jnp.float32),
        in_specs=[pl.BlockSpec(memory_space=pl.ANY)],
        out_specs=pl.BlockSpec(memory_space=pltpu.VMEM),
        scratch_shapes=[
            pltpu.VMEM((8, slots, width), jnp.float32),
            pltpu.VMEM((8, slots, width), jnp.float32),
            pltpu.VMEM((7, slots, width), jnp.bfloat16),
            pltpu.VMEM((7, slots, width), jnp.bfloat16),
            pltpu.SemaphoreType.DMA((8,)),
            pltpu.SemaphoreType.DMA((8,)),
            pltpu.SemaphoreType.DMA((8,)),
            pltpu.SemaphoreType.DMA((7,)),
            pltpu.SemaphoreType.DMA((7,)),
        ],
        compiler_params=pltpu.CompilerParams(
            collective_id=1, has_side_effects=True, vmem_limit_bytes=56 * 1024 * 1024
        ),
    )(parts)


def body(tokens, norm_gain, expert_ids, gate_weights, w_gate, w_up, w_down):
    chips = lax.psum(1, "chip")
    width = tokens.shape[1]
    core = lax.axis_index("core")

    picker, slot_index = route_tables(expert_ids, EXPERTS, CAP)
    packed = jnp.einsum("ts,td->sd", picker, tokens, preferred_element_type=jnp.float32).astype(
        jnp.bfloat16
    )
    packed = packed.reshape(EXPERTS, CAP, width)
    arrived = lax.all_to_all(packed, "row", split_axis=0, concat_axis=0, tiled=True)
    arrived = arrived.reshape(EXPERTS * CAP, width)
    slots = arrived.shape[0]

    hidden = expert_in(arrived, norm_gain, w_gate[0], w_up[0], chips)
    outputs = jnp.dot(hidden, w_down[0], preferred_element_type=jnp.float32)
    shares = scatter_cols(outputs, width)
    shares = shares.reshape(EXPERTS, CAP, width)
    returned = lax.all_to_all(shares, "row", split_axis=0, concat_axis=0, tiled=True)
    mixed = combine_rows(returned.reshape(-1, width), slot_index, gate_weights)
    return (tokens.astype(jnp.float32) + mixed).astype(jnp.bfloat16)


def solution(mesh):
    rows, cols = mesh.devices.shape
    split_mesh = Mesh(mesh.devices.reshape(rows, cols // 2, 2), ("row", "chip", "core"))
    placed = (
        P("row", COL),
        P(),
        P("row", None),
        P("row", None),
        P("row", None, COL),
        P("row", None, COL),
        P("row", COL, None),
    )
    return jax.shard_map(
        body, mesh=split_mesh, in_specs=placed, out_specs=P("row", COL), check_vma=False
    )
```

```python
import functools

import jax
import jax.numpy as jnp
from jax import lax
from jax.experimental import pallas as pl
from jax.experimental.pallas import tpu as pltpu
from jax.sharding import Mesh
from jax.sharding import PartitionSpec as P

EXPERTS = 8
CAP = 128
COL = ("chip", "core")
MESH = pl.DeviceIdType.MESH


def normalize(rows, norm_gain):
    values = rows.astype(jnp.float32)
    inverse_norm = lax.rsqrt(jnp.mean(values * values, axis=-1, keepdims=True) + 1e-05)
    return (values * inverse_norm * norm_gain).astype(jnp.bfloat16)


def route_tables(expert_ids, expert_count, capacity):
    token_count = expert_ids.shape[0]
    flat_ids = expert_ids.reshape(-1)
    expert_range = jnp.arange(expert_count, dtype=jnp.int32)
    expert_hits = (flat_ids[:, None] == expert_range[None, :]).astype(jnp.int32)
    earlier = jnp.cumsum(expert_hits, axis=0) - expert_hits
    ranks = jnp.sum(earlier * expert_hits, axis=1)
    slot_index = (flat_ids * capacity + ranks).reshape(token_count, -1)
    slot_ids = jnp.arange(expert_count * capacity, dtype=jnp.int32)
    matches = (slot_index[:, :, None] == slot_ids[None, None, :]).astype(jnp.float32)
    picker = jnp.sum(matches, axis=1)
    return (picker.astype(jnp.bfloat16), slot_index)


def combine_rows(slot_rows, slot_index, gate_weights):
    picked = slot_rows[slot_index]
    return jnp.sum(picked * gate_weights[:, :, None], axis=1)


def expert_in_kernel(width, src, squares_part, gain_in, w_gate_hbm, w_up_hbm, hidden, xs, w_gate,
                     w_up, gain, acc_gate, acc_up, squares, send_sem, recv_sem, local_sem,
                     weight_sem, square_send, square_recv):
    row, me, core = lax.axis_index("row"), lax.axis_index("chip"), lax.axis_index("core")
    side, y = me // 4, me % 4
    partner = lax.rem(me + 4, 8)
    up = side * 4 + lax.rem(y + 1, 4)
    down = side * 4 + lax.rem(y + 3, 4)
    across = side * 4 + lax.rem(y + 2, 4)
    sister = 1 - core
    slots = xs.shape[0]
    step = 256
    blocks = squares.shape[0]
    mine = me * 2 + core
    chips = (me, partner, down, up, far(down), far(up), across, far(across))
    features = [(chip * 2 + core) * width for chip in chips]
    features += [(chip * 2 + sister) * width for chip in chips]

    loads = []
    for place, start in enumerate(features):
        rows = pl.ds(pl.multiple_of(start, width), width)
        for index, (source, target) in enumerate(((w_gate_hbm, w_gate), (w_up_hbm, w_up))):
            load = pltpu.make_async_copy(source.at[rows, :], target.at[pl.ds(place * width, width), :],
                                         weight_sem.at[index, place])
            load.start()
            loads.append(load)
        gain[:, pl.ds(place * width, width)] = gain_in[:, rows]

    barrier = pltpu.get_barrier_semaphore()
    for d in range(1, blocks):
        other = lax.rem(mine + d, blocks)
        pl.semaphore_signal(barrier, inc=1, device_id=(row, other // 2, other % 2),
                            device_id_type=MESH)
    pl.semaphore_wait(barrier, blocks - 1)

    square_copies = []
    for d in range(1, blocks):
        other = lax.rem(mine + d, blocks)
        copy = pltpu.make_async_remote_copy(
            src_ref=squares_part, dst_ref=squares.at[mine], send_sem=square_send.at[d],
            recv_sem=square_recv.at[d], device_id=(row, other // 2, other % 2),
            device_id_type=MESH,
        )
        copy.start()
        square_copies.append(copy)

    def place(p):
        return xs.at[:, pl.ds(p * width, width)]

    def send(tag, source, target, chip, half):
        copy = pltpu.make_async_remote_copy(
            src_ref=source, dst_ref=place(target), send_sem=send_sem.at[tag],
            recv_sem=recv_sem.at[tag], device_id=(row, chip, half), device_id_type=MESH,
        )
        copy.start()
        return copy

    def arrive(tag, target):
        pltpu.make_async_remote_copy(
            src_ref=place(target), dst_ref=place(target), send_sem=send_sem.at[tag],
            recv_sem=recv_sem.at[tag], device_id=(row, me, sister), device_id_type=MESH,
        ).wait_recv()

    sent = [
        send(0, src, 1, partner, core),
        send(1, src, 2, up, core),
        send(2, src, 3, down, core),
        send(7, src, 8, me, sister),
    ]
    local = pltpu.make_async_copy(src, place(0), local_sem)
    local.start()
    squares[mine] = squares_part[...]
    for copy in square_copies:
        copy.wait_recv()
    total = squares[0]
    for b in range(1, blocks):
        total = total + squares[b]
    squares[0] = lax.rsqrt(total / (blocks * width) + 1e-05)

    arrive(0, 1)
    sent += [send(3, place(1), 4, up, core), send(4, place(1), 5, down, core),
             send(8, place(1), 9, me, sister)]
    arrive(1, 2)
    sent += [send(5, place(2), 6, up, core), send(9, place(2), 10, me, sister)]
    arrive(2, 3)
    sent.append(send(10, place(3), 11, me, sister))
    for load in loads:
        load.wait()
    local.wait()

    def absorb(first_place, first=False):
        cols = pl.ds(first_place * width, 4 * width)
        scale = gain[:, cols]

        def one(i, carry):
            part = pl.ds(pl.multiple_of(i * step, step), step)
            spread = jnp.broadcast_to(squares[0, pl.ds(i, 1), :], (128, step))
            column = jnp.transpose(spread)[:, 0:1]
            values = xs[part, cols].astype(jnp.float32)
            normed = (values * column * scale).astype(jnp.bfloat16)
            gate_part = jnp.dot(normed, w_gate[cols, :], preferred_element_type=jnp.float32)
            up_part = jnp.dot(normed, w_up[cols, :], preferred_element_type=jnp.float32)
            if first:
                acc_gate[part, :] = gate_part
                acc_up[part, :] = up_part
            else:
                acc_gate[part, :] += gate_part
                acc_up[part, :] += up_part
            return carry

        lax.fori_loop(0, slots // step, one, 0)

    absorb(0, first=True)
    arrive(3, 4)
    sent.append(send(11, place(4), 12, me, sister))
    arrive(4, 5)
    sent += [send(6, place(5), 7, down, core), send(12, place(5), 13, me, sister)]
    arrive(5, 6)
    sent.append(send(13, place(6), 14, me, sister))
    arrive(6, 7)
    sent.append(send(14, place(7), 15, me, sister))
    absorb(4)
    for tag in range(7, 11):
        arrive(tag, tag + 1)
    absorb(8)
    for tag in range(11, 15):
        arrive(tag, tag + 1)
    absorb(12)

    def finish(i, carry):
        part = pl.ds(pl.multiple_of(i * step, step), step)
        gate_values = acc_gate[part, :]
        silu = gate_values / (1.0 + jnp.exp(-gate_values))
        hidden[part, :] = (silu * acc_up[part, :]).astype(hidden.dtype)
        return carry

    lax.fori_loop(0, slots // step, finish, 0)
    for copy in sent + square_copies:
        copy.wait_send()


def far(chip):
    return lax.rem(chip + 4, 8)


def expert_in(block, norm_gain, w_gate, w_up, chips):
    slots, width = block.shape
    blocks = chips * 2
    features = blocks * width
    hidden_units = w_gate.shape[1]
    values = block.astype(jnp.float32)
    squares_part = jnp.sum(values * values, axis=1).reshape(slots // 256, 256)
    return pl.pallas_call(
        functools.partial(expert_in_kernel, width),
        out_shape=jax.ShapeDtypeStruct((slots, hidden_units), jnp.bfloat16),
        in_specs=[pl.BlockSpec(memory_space=pltpu.VMEM)] * 3
        + [pl.BlockSpec(memory_space=pl.ANY)] * 2,
        out_specs=pl.BlockSpec(memory_space=pltpu.VMEM),
        scratch_shapes=[
            pltpu.VMEM((slots, features), jnp.bfloat16),
            pltpu.VMEM(w_gate.shape, w_gate.dtype),
            pltpu.VMEM(w_up.shape, w_up.dtype),
            pltpu.VMEM((1, features), jnp.float32),
            pltpu.VMEM((slots, hidden_units), jnp.float32),
            pltpu.VMEM((slots, hidden_units), jnp.float32),
            pltpu.VMEM((blocks, slots // 256, 256), jnp.float32),
            pltpu.SemaphoreType.DMA((15,)),
            pltpu.SemaphoreType.DMA((15,)),
            pltpu.SemaphoreType.DMA(()),
            pltpu.SemaphoreType.DMA((2, blocks)),
            pltpu.SemaphoreType.DMA((blocks,)),
            pltpu.SemaphoreType.DMA((blocks,)),
        ],
        compiler_params=pltpu.CompilerParams(
            collective_id=0, has_side_effects=True, vmem_limit_bytes=60 * 1024 * 1024
        ),
    )(block, squares_part, norm_gain.reshape(1, features), w_gate, w_up)


def add_blocks(dst, *sources):
    rows = dst.shape[0]
    step = 128

    def one(i, carry):
        part = pl.ds(pl.multiple_of(i * step, step), step)
        total = sources[0][part, :].astype(jnp.float32)
        for source in sources[1:]:
            total = total + source[part, :].astype(jnp.float32)
        dst[part, :] = total.astype(dst.dtype)
        return carry

    lax.fori_loop(0, rows // step, one, 0)


def scatter_kernel(width, parts, out, mine, theirs, sending, landed, local_sem, sister_send,
                   sister_recv, send_sem, recv_sem):
    row, me, core = lax.axis_index("row"), lax.axis_index("chip"), lax.axis_index("core")
    sister = 1 - core
    side, y = me // 4, me % 4
    partner = lax.rem(me + 4, 8)
    up = side * 4 + lax.rem(y + 1, 4)
    down = side * 4 + lax.rem(y + 3, 4)
    across = side * 4 + lax.rem(y + 2, 4)

    def far(chip):
        return lax.rem(chip + 4, 8)

    def columns(chip, half):
        start = pl.multiple_of((chip * 2 + half) * width, width)
        return parts.at[:, pl.ds(start, width)]

    barrier = pltpu.get_barrier_semaphore()
    for chip, half in ((partner, core), (up, core), (down, core), (me, sister)):
        pl.semaphore_signal(barrier, inc=1, device_id=(row, chip, half), device_id_type=MESH)
    pl.semaphore_wait(barrier, 4)

    order = (far(down), across, up, far(across), down, far(up), partner, me)
    swaps, loads = [], []
    for slot, chip in enumerate(order):
        swap = pltpu.make_async_remote_copy(
            src_ref=columns(chip, sister), dst_ref=theirs.at[slot], send_sem=sister_send.at[slot],
            recv_sem=sister_recv.at[slot], device_id=(row, me, sister), device_id_type=MESH,
        )
        swap.start()
        swaps.append(swap)
        load = pltpu.make_async_copy(columns(chip, core), mine.at[slot], local_sem.at[slot])
        load.start()
        loads.append(load)

    def ready(slot):
        loads[slot].wait()
        swaps[slot].wait_recv()
        return (mine.at[slot], theirs.at[slot])

    def send(tag, chip):
        copy = pltpu.make_async_remote_copy(
            src_ref=sending.at[tag], dst_ref=landed.at[tag], send_sem=send_sem.at[tag],
            recv_sem=recv_sem.at[tag], device_id=(row, chip, core), device_id_type=MESH,
        )
        copy.start()
        return copy

    def arrive(tag):
        pltpu.make_async_remote_copy(
            src_ref=sending.at[tag], dst_ref=landed.at[tag], send_sem=send_sem.at[tag],
            recv_sem=recv_sem.at[tag], device_id=(row, me, core), device_id_type=MESH,
        ).wait_recv()

    sent = []
    for tag, chip in ((0, down), (1, down), (2, up), (3, up)):
        add_blocks(sending.at[tag], *ready(tag))
        sent.append(send(tag, chip))
    arrive(1)
    add_blocks(sending.at[4], *ready(4), landed.at[1])
    sent.append(send(4, down))
    arrive(3)
    add_blocks(sending.at[5], *ready(5), landed.at[3])
    sent.append(send(5, up))
    arrive(0)
    arrive(5)
    add_blocks(sending.at[6], *ready(6), landed.at[0], landed.at[5])
    sent.append(send(6, partner))
    arrive(2)
    arrive(4)
    add_blocks(out, *ready(7), landed.at[2], landed.at[4])
    arrive(6)
    add_blocks(out, out, landed.at[6])
    for copy in sent + swaps:
        copy.wait_send()


def scatter_cols(parts, width):
    slots = parts.shape[0]
    return pl.pallas_call(
        functools.partial(scatter_kernel, width),
        out_shape=jax.ShapeDtypeStruct((slots, width), jnp.float32),
        in_specs=[pl.BlockSpec(memory_space=pl.ANY)],
        out_specs=pl.BlockSpec(memory_space=pltpu.VMEM),
        scratch_shapes=[
            pltpu.VMEM((8, slots, width), jnp.float32),
            pltpu.VMEM((8, slots, width), jnp.float32),
            pltpu.VMEM((7, slots, width), jnp.bfloat16),
            pltpu.VMEM((7, slots, width), jnp.bfloat16),
            pltpu.SemaphoreType.DMA((8,)),
            pltpu.SemaphoreType.DMA((8,)),
            pltpu.SemaphoreType.DMA((8,)),
            pltpu.SemaphoreType.DMA((7,)),
            pltpu.SemaphoreType.DMA((7,)),
        ],
        compiler_params=pltpu.CompilerParams(
            collective_id=1, has_side_effects=True, vmem_limit_bytes=56 * 1024 * 1024
        ),
    )(parts)


def body(tokens, norm_gain, expert_ids, gate_weights, w_gate, w_up, w_down):
    chips = lax.psum(1, "chip")
    width = tokens.shape[1]
    core = lax.axis_index("core")

    picker, slot_index = route_tables(expert_ids, EXPERTS, CAP)
    packed = jnp.einsum("ts,td->sd", picker, tokens, preferred_element_type=jnp.float32).astype(
        jnp.bfloat16
    )
    packed = packed.reshape(EXPERTS, CAP, width)
    arrived = lax.all_to_all(packed, "row", split_axis=0, concat_axis=0, tiled=True)
    arrived = arrived.reshape(EXPERTS * CAP, width)
    slots = arrived.shape[0]

    hidden = expert_in(arrived, norm_gain, w_gate[0], w_up[0], chips)
    outputs = jnp.dot(hidden, w_down[0], preferred_element_type=jnp.float32)
    shares = scatter_cols(outputs, width)
    shares = shares.reshape(EXPERTS, CAP, width)
    returned = lax.all_to_all(shares, "row", split_axis=0, concat_axis=0, tiled=True)
    mixed = combine_rows(returned.reshape(-1, width), slot_index, gate_weights)
    return (tokens.astype(jnp.float32) + mixed).astype(jnp.bfloat16)


def solution(mesh):
    rows, cols = mesh.devices.shape
    split_mesh = Mesh(mesh.devices.reshape(rows, cols // 2, 2), ("row", "chip", "core"))
    placed = (
        P("row", COL),
        P(),
        P("row", None),
        P("row", None),
        P("row", None, COL),
        P("row", None, COL),
        P("row", COL, None),
    )
    return jax.shard_map(
        body, mesh=split_mesh, in_specs=placed, out_specs=P("row", COL), check_vma=False
    )
```

```python
import functools

import jax
import jax.numpy as jnp
from jax import lax
from jax.experimental import pallas as pl
from jax.experimental.pallas import tpu as pltpu
from jax.sharding import Mesh
from jax.sharding import PartitionSpec as P

EXPERTS = 8
CAP = 128
COL = ("chip", "core")
MESH = pl.DeviceIdType.MESH


def normalize(rows, norm_gain):
    values = rows.astype(jnp.float32)
    inverse_norm = lax.rsqrt(jnp.mean(values * values, axis=-1, keepdims=True) + 1e-05)
    return (values * inverse_norm * norm_gain).astype(jnp.bfloat16)


def route_tables(expert_ids, expert_count, capacity):
    token_count = expert_ids.shape[0]
    flat_ids = expert_ids.reshape(-1)
    expert_range = jnp.arange(expert_count, dtype=jnp.int32)
    expert_hits = (flat_ids[:, None] == expert_range[None, :]).astype(jnp.int32)
    earlier = jnp.cumsum(expert_hits, axis=0) - expert_hits
    ranks = jnp.sum(earlier * expert_hits, axis=1)
    slot_index = (flat_ids * capacity + ranks).reshape(token_count, -1)
    slot_ids = jnp.arange(expert_count * capacity, dtype=jnp.int32)
    matches = (slot_index[:, :, None] == slot_ids[None, None, :]).astype(jnp.float32)
    picker = jnp.sum(matches, axis=1)
    return (picker.astype(jnp.bfloat16), slot_index)


def combine_rows(slot_rows, slot_index, gate_weights):
    picked = slot_rows[slot_index]
    return jnp.sum(picked * gate_weights[:, :, None], axis=1)


def expert_in_kernel(width, src, squares_part, gain_in, w_gate_hbm, w_up_hbm, hidden, xs, w_gate,
                     w_up, gain, acc_gate, acc_up, squares, send_sem, recv_sem, local_sem,
                     weight_sem, square_send, square_recv):
    row, me, core = lax.axis_index("row"), lax.axis_index("chip"), lax.axis_index("core")
    side, y = me // 4, me % 4
    partner = lax.rem(me + 4, 8)
    up = side * 4 + lax.rem(y + 1, 4)
    down = side * 4 + lax.rem(y + 3, 4)
    across = side * 4 + lax.rem(y + 2, 4)
    sister = 1 - core
    slots = xs.shape[0]
    step = 256
    blocks = squares.shape[0]
    mine = me * 2 + core
    chips = (me, partner, down, up, far(down), far(up), across, far(across))
    features = [(chip * 2 + core) * width for chip in chips]
    features += [(chip * 2 + sister) * width for chip in chips]

    loads = []
    for place, start in enumerate(features):
        rows = pl.ds(pl.multiple_of(start, width), width)
        for index, (source, target) in enumerate(((w_gate_hbm, w_gate), (w_up_hbm, w_up))):
            load = pltpu.make_async_copy(source.at[rows, :], target.at[pl.ds(place * width, width), :],
                                         weight_sem.at[index, place])
            load.start()
            loads.append(load)
        gain[:, pl.ds(place * width, width)] = gain_in[:, rows]

    barrier = pltpu.get_barrier_semaphore()
    for d in range(1, blocks):
        other = lax.rem(mine + d, blocks)
        pl.semaphore_signal(barrier, inc=1, device_id=(row, other // 2, other % 2),
                            device_id_type=MESH)
    pl.semaphore_wait(barrier, blocks - 1)

    square_copies = []
    for d in range(1, blocks):
        other = lax.rem(mine + d, blocks)
        copy = pltpu.make_async_remote_copy(
            src_ref=squares_part, dst_ref=squares.at[mine], send_sem=square_send.at[d],
            recv_sem=square_recv.at[d], device_id=(row, other // 2, other % 2),
            device_id_type=MESH,
        )
        copy.start()
        square_copies.append(copy)

    def place(p):
        return xs.at[:, pl.ds(p * width, width)]

    def send(tag, source, target, chip, half):
        copy = pltpu.make_async_remote_copy(
            src_ref=source, dst_ref=place(target), send_sem=send_sem.at[tag],
            recv_sem=recv_sem.at[tag], device_id=(row, chip, half), device_id_type=MESH,
        )
        copy.start()
        return copy

    def arrive(tag, target):
        pltpu.make_async_remote_copy(
            src_ref=place(target), dst_ref=place(target), send_sem=send_sem.at[tag],
            recv_sem=recv_sem.at[tag], device_id=(row, me, sister), device_id_type=MESH,
        ).wait_recv()

    sent = [
        send(0, src, 1, partner, core),
        send(1, src, 2, up, core),
        send(2, src, 3, down, core),
        send(7, src, 8, me, sister),
    ]
    local = pltpu.make_async_copy(src, place(0), local_sem)
    local.start()
    squares[mine] = squares_part[...]
    for copy in square_copies:
        copy.wait_recv()
    total = squares[0]
    for b in range(1, blocks):
        total = total + squares[b]
    squares[0] = lax.rsqrt(total / (blocks * width) + 1e-05)

    arrive(0, 1)
    sent += [send(3, place(1), 4, up, core), send(4, place(1), 5, down, core),
             send(8, place(1), 9, me, sister)]
    arrive(1, 2)
    sent += [send(5, place(2), 6, up, core), send(9, place(2), 10, me, sister)]
    arrive(2, 3)
    sent.append(send(10, place(3), 11, me, sister))
    for load in loads:
        load.wait()
    local.wait()

    def absorb(first_place, first=False):
        cols = pl.ds(first_place * width, 4 * width)
        scale = gain[:, cols]

        def one(i, carry):
            part = pl.ds(pl.multiple_of(i * step, step), step)
            spread = jnp.broadcast_to(squares[0, pl.ds(i, 1), :], (128, step))
            column = jnp.transpose(spread)[:, 0:1]
            values = xs[part, cols].astype(jnp.float32)
            normed = (values * column * scale).astype(jnp.bfloat16)
            gate_part = jnp.dot(normed, w_gate[cols, :], preferred_element_type=jnp.float32)
            up_part = jnp.dot(normed, w_up[cols, :], preferred_element_type=jnp.float32)
            if first:
                acc_gate[part, :] = gate_part
                acc_up[part, :] = up_part
            else:
                acc_gate[part, :] += gate_part
                acc_up[part, :] += up_part
            return carry

        lax.fori_loop(0, slots // step, one, 0)

    absorb(0, first=True)
    arrive(3, 4)
    sent.append(send(11, place(4), 12, me, sister))
    arrive(4, 5)
    sent += [send(6, place(5), 7, down, core), send(12, place(5), 13, me, sister)]
    arrive(5, 6)
    sent.append(send(13, place(6), 14, me, sister))
    arrive(6, 7)
    sent.append(send(14, place(7), 15, me, sister))
    absorb(4)
    for tag in range(7, 11):
        arrive(tag, tag + 1)
    absorb(8)
    for tag in range(11, 15):
        arrive(tag, tag + 1)
    absorb(12)

    def finish(i, carry):
        part = pl.ds(pl.multiple_of(i * step, step), step)
        gate_values = acc_gate[part, :]
        silu = gate_values / (1.0 + jnp.exp(-gate_values))
        hidden[part, :] = (silu * acc_up[part, :]).astype(hidden.dtype)
        return carry

    lax.fori_loop(0, slots // step, finish, 0)
    for copy in sent + square_copies:
        copy.wait_send()


def far(chip):
    return lax.rem(chip + 4, 8)


def expert_in(block, norm_gain, w_gate, w_up, chips):
    slots, width = block.shape
    blocks = chips * 2
    features = blocks * width
    hidden_units = w_gate.shape[1]
    values = block.astype(jnp.float32)
    squares_part = jnp.sum(values * values, axis=1).reshape(slots // 256, 256)
    return pl.pallas_call(
        functools.partial(expert_in_kernel, width),
        out_shape=jax.ShapeDtypeStruct((slots, hidden_units), jnp.bfloat16),
        in_specs=[pl.BlockSpec(memory_space=pltpu.VMEM)] * 3
        + [pl.BlockSpec(memory_space=pl.ANY)] * 2,
        out_specs=pl.BlockSpec(memory_space=pltpu.VMEM),
        scratch_shapes=[
            pltpu.VMEM((slots, features), jnp.bfloat16),
            pltpu.VMEM(w_gate.shape, w_gate.dtype),
            pltpu.VMEM(w_up.shape, w_up.dtype),
            pltpu.VMEM((1, features), jnp.float32),
            pltpu.VMEM((slots, hidden_units), jnp.float32),
            pltpu.VMEM((slots, hidden_units), jnp.float32),
            pltpu.VMEM((blocks, slots // 256, 256), jnp.float32),
            pltpu.SemaphoreType.DMA((15,)),
            pltpu.SemaphoreType.DMA((15,)),
            pltpu.SemaphoreType.DMA(()),
            pltpu.SemaphoreType.DMA((2, blocks)),
            pltpu.SemaphoreType.DMA((blocks,)),
            pltpu.SemaphoreType.DMA((blocks,)),
        ],
        compiler_params=pltpu.CompilerParams(
            collective_id=0, has_side_effects=True, vmem_limit_bytes=60 * 1024 * 1024
        ),
    )(block, squares_part, norm_gain.reshape(1, features), w_gate, w_up)


def project(dst, hidden, weights, start):
    rows = dst.shape[0]
    step = 256
    cols = pl.ds(pl.multiple_of(start, 256), dst.shape[1])

    def one(i, carry):
        part = pl.ds(pl.multiple_of(i * step, step), step)
        dst[part, :] = jnp.dot(hidden[part, :], weights[:, cols], preferred_element_type=jnp.float32)
        return carry

    lax.fori_loop(0, rows // step, one, 0)


def add_blocks(dst, *sources):
    rows = dst.shape[0]
    step = 128

    def one(i, carry):
        part = pl.ds(pl.multiple_of(i * step, step), step)
        total = sources[0][part, :].astype(jnp.float32)
        for source in sources[1:]:
            total = total + source[part, :].astype(jnp.float32)
        dst[part, :] = total.astype(dst.dtype)
        return carry

    lax.fori_loop(0, rows // step, one, 0)


def scatter_kernel(width, hidden, weights, out, mine, theirs, outgoing, sending, landed,
                   sister_send, sister_recv, send_sem, recv_sem):
    row, me, core = lax.axis_index("row"), lax.axis_index("chip"), lax.axis_index("core")
    sister = 1 - core
    side, y = me // 4, me % 4
    partner = lax.rem(me + 4, 8)
    up = side * 4 + lax.rem(y + 1, 4)
    down = side * 4 + lax.rem(y + 3, 4)
    across = side * 4 + lax.rem(y + 2, 4)

    def far(chip):
        return lax.rem(chip + 4, 8)

    barrier = pltpu.get_barrier_semaphore()
    for chip, half in ((partner, core), (up, core), (down, core), (me, sister)):
        pl.semaphore_signal(barrier, inc=1, device_id=(row, chip, half), device_id_type=MESH)
    pl.semaphore_wait(barrier, 4)

    order = (far(down), across, up, far(across), down, far(up), partner, me)
    swaps = []

    def produce(slots):
        for slot in slots:
            project(outgoing.at[slot], hidden, weights, (order[slot] * 2 + sister) * width)
            swap = pltpu.make_async_remote_copy(
                src_ref=outgoing.at[slot], dst_ref=theirs.at[slot], send_sem=sister_send.at[slot],
                recv_sem=sister_recv.at[slot], device_id=(row, me, sister), device_id_type=MESH,
            )
            swap.start()
            swaps.append(swap)
        for slot in slots:
            project(mine.at[slot], hidden, weights, (order[slot] * 2 + core) * width)

    produce(range(4))

    def ready(slot):
        swaps[slot].wait_recv()
        return (mine.at[slot], theirs.at[slot])

    def send(tag, chip):
        copy = pltpu.make_async_remote_copy(
            src_ref=sending.at[tag], dst_ref=landed.at[tag], send_sem=send_sem.at[tag],
            recv_sem=recv_sem.at[tag], device_id=(row, chip, core), device_id_type=MESH,
        )
        copy.start()
        return copy

    def arrive(tag):
        pltpu.make_async_remote_copy(
            src_ref=sending.at[tag], dst_ref=landed.at[tag], send_sem=send_sem.at[tag],
            recv_sem=recv_sem.at[tag], device_id=(row, me, core), device_id_type=MESH,
        ).wait_recv()

    sent = []
    for tag, chip in ((0, down), (1, down), (2, up), (3, up)):
        add_blocks(sending.at[tag], *ready(tag))
        sent.append(send(tag, chip))
    produce(range(4, 8))
    arrive(1)
    add_blocks(sending.at[4], *ready(4), landed.at[1])
    sent.append(send(4, down))
    arrive(3)
    add_blocks(sending.at[5], *ready(5), landed.at[3])
    sent.append(send(5, up))
    arrive(0)
    arrive(5)
    add_blocks(sending.at[6], *ready(6), landed.at[0], landed.at[5])
    sent.append(send(6, partner))
    arrive(2)
    arrive(4)
    add_blocks(out, *ready(7), landed.at[2], landed.at[4])
    arrive(6)
    add_blocks(out, out, landed.at[6])
    for copy in sent + swaps:
        copy.wait_send()


def scatter_cols(hidden, weights, width):
    slots = hidden.shape[0]
    return pl.pallas_call(
        functools.partial(scatter_kernel, width),
        out_shape=jax.ShapeDtypeStruct((slots, width), jnp.float32),
        in_specs=[pl.BlockSpec(memory_space=pltpu.VMEM)] * 2,
        out_specs=pl.BlockSpec(memory_space=pltpu.VMEM),
        scratch_shapes=[
            pltpu.VMEM((8, slots, width), jnp.float32),
            pltpu.VMEM((8, slots, width), jnp.float32),
            pltpu.VMEM((8, slots, width), jnp.float32),
            pltpu.VMEM((7, slots, width), jnp.bfloat16),
            pltpu.VMEM((7, slots, width), jnp.bfloat16),
            pltpu.SemaphoreType.DMA((8,)),
            pltpu.SemaphoreType.DMA((8,)),
            pltpu.SemaphoreType.DMA((7,)),
            pltpu.SemaphoreType.DMA((7,)),
        ],
        compiler_params=pltpu.CompilerParams(
            collective_id=1, has_side_effects=True, vmem_limit_bytes=60 * 1024 * 1024
        ),
    )(hidden, weights)


def body(tokens, norm_gain, expert_ids, gate_weights, w_gate, w_up, w_down):
    chips = lax.psum(1, "chip")
    width = tokens.shape[1]
    core = lax.axis_index("core")

    picker, slot_index = route_tables(expert_ids, EXPERTS, CAP)
    packed = jnp.einsum("ts,td->sd", picker, tokens, preferred_element_type=jnp.float32).astype(
        jnp.bfloat16
    )
    packed = packed.reshape(EXPERTS, CAP, width)
    arrived = lax.all_to_all(packed, "row", split_axis=0, concat_axis=0, tiled=True)
    arrived = arrived.reshape(EXPERTS * CAP, width)
    slots = arrived.shape[0]

    hidden = expert_in(arrived, norm_gain, w_gate[0], w_up[0], chips)
    shares = scatter_cols(hidden, w_down[0], width)
    shares = shares.reshape(EXPERTS, CAP, width)
    returned = lax.all_to_all(shares, "row", split_axis=0, concat_axis=0, tiled=True)
    mixed = combine_rows(returned.reshape(-1, width), slot_index, gate_weights)
    return (tokens.astype(jnp.float32) + mixed).astype(jnp.bfloat16)


def solution(mesh):
    rows, cols = mesh.devices.shape
    split_mesh = Mesh(mesh.devices.reshape(rows, cols // 2, 2), ("row", "chip", "core"))
    placed = (
        P("row", COL),
        P(),
        P("row", None),
        P("row", None),
        P("row", None, COL),
        P("row", None, COL),
        P("row", COL, None),
    )
    return jax.shard_map(
        body, mesh=split_mesh, in_specs=placed, out_specs=P("row", COL), check_vma=False
    )
```

```python
import functools

import jax
import jax.numpy as jnp
from jax import lax
from jax.experimental import pallas as pl
from jax.experimental.pallas import tpu as pltpu
from jax.sharding import Mesh
from jax.sharding import PartitionSpec as P

EXPERTS = 8
CAP = 128
COL = ("chip", "core")
MESH = pl.DeviceIdType.MESH


def normalize(rows, norm_gain):
    values = rows.astype(jnp.float32)
    inverse_norm = lax.rsqrt(jnp.mean(values * values, axis=-1, keepdims=True) + 1e-05)
    return (values * inverse_norm * norm_gain).astype(jnp.bfloat16)


def route_tables(expert_ids, expert_count, capacity):
    token_count = expert_ids.shape[0]
    flat_ids = expert_ids.reshape(-1)
    expert_range = jnp.arange(expert_count, dtype=jnp.int32)
    expert_hits = (flat_ids[:, None] == expert_range[None, :]).astype(jnp.int32)
    earlier = jnp.cumsum(expert_hits, axis=0) - expert_hits
    ranks = jnp.sum(earlier * expert_hits, axis=1)
    slot_index = (flat_ids * capacity + ranks).reshape(token_count, -1)
    slot_ids = jnp.arange(expert_count * capacity, dtype=jnp.int32)
    matches = (slot_index[:, :, None] == slot_ids[None, None, :]).astype(jnp.float32)
    picker = jnp.sum(matches, axis=1)
    return (picker.astype(jnp.bfloat16), slot_index)


def combine_rows(slot_rows, slot_index, gate_weights):
    picked = slot_rows[slot_index]
    return jnp.sum(picked * gate_weights[:, :, None], axis=1)


def expert_in_kernel(width, src, squares_part, gain_in, w_gate_hbm, w_up_hbm, hidden, xs, w_gate,
                     w_up, gain, acc_gate, acc_up, squares, send_sem, recv_sem, local_sem,
                     weight_sem, square_send, square_recv):
    row, me, core = lax.axis_index("row"), lax.axis_index("chip"), lax.axis_index("core")
    side, y = me // 4, me % 4
    partner = lax.rem(me + 4, 8)
    up = side * 4 + lax.rem(y + 1, 4)
    down = side * 4 + lax.rem(y + 3, 4)
    across = side * 4 + lax.rem(y + 2, 4)
    sister = 1 - core
    slots = xs.shape[0]
    step = 256
    blocks = squares.shape[0]
    mine = me * 2 + core
    chips = (me, partner, down, up, far(down), far(up), across, far(across))
    features = [(chip * 2 + core) * width for chip in chips]
    features += [(chip * 2 + sister) * width for chip in chips]

    loads = []
    for place, start in enumerate(features):
        rows = pl.ds(pl.multiple_of(start, width), width)
        for index, (source, target) in enumerate(((w_gate_hbm, w_gate), (w_up_hbm, w_up))):
            load = pltpu.make_async_copy(source.at[rows, :], target.at[pl.ds(place * width, width), :],
                                         weight_sem.at[index, place])
            load.start()
            loads.append(load)
        gain[:, pl.ds(place * width, width)] = gain_in[:, rows]

    barrier = pltpu.get_barrier_semaphore()
    for d in range(1, blocks):
        other = lax.rem(mine + d, blocks)
        pl.semaphore_signal(barrier, inc=1, device_id=(row, other // 2, other % 2),
                            device_id_type=MESH)
    pl.semaphore_wait(barrier, blocks - 1)

    square_copies = []
    for d in range(1, blocks):
        other = lax.rem(mine + d, blocks)
        copy = pltpu.make_async_remote_copy(
            src_ref=squares_part, dst_ref=squares.at[mine], send_sem=square_send.at[d],
            recv_sem=square_recv.at[d], device_id=(row, other // 2, other % 2),
            device_id_type=MESH,
        )
        copy.start()
        square_copies.append(copy)

    def place(p):
        return xs.at[:, pl.ds(p * width, width)]

    def send(tag, source, target, chip, half):
        copy = pltpu.make_async_remote_copy(
            src_ref=source, dst_ref=place(target), send_sem=send_sem.at[tag],
            recv_sem=recv_sem.at[tag], device_id=(row, chip, half), device_id_type=MESH,
        )
        copy.start()
        return copy

    def arrive(tag, target):
        pltpu.make_async_remote_copy(
            src_ref=place(target), dst_ref=place(target), send_sem=send_sem.at[tag],
            recv_sem=recv_sem.at[tag], device_id=(row, me, sister), device_id_type=MESH,
        ).wait_recv()

    sent = [
        send(0, src, 1, partner, core),
        send(1, src, 2, up, core),
        send(2, src, 3, down, core),
        send(7, src, 8, me, sister),
    ]
    local = pltpu.make_async_copy(src, place(0), local_sem)
    local.start()
    squares[mine] = squares_part[...]
    for copy in square_copies:
        copy.wait_recv()
    total = squares[0]
    for b in range(1, blocks):
        total = total + squares[b]
    squares[0] = lax.rsqrt(total / (blocks * width) + 1e-05)

    arrive(0, 1)
    sent += [send(3, place(1), 4, up, core), send(4, place(1), 5, down, core),
             send(8, place(1), 9, me, sister)]
    arrive(1, 2)
    sent += [send(5, place(2), 6, up, core), send(9, place(2), 10, me, sister)]
    arrive(2, 3)
    sent.append(send(10, place(3), 11, me, sister))
    for load in loads:
        load.wait()
    local.wait()

    def absorb(first_place, first=False):
        cols = pl.ds(first_place * width, 4 * width)
        scale = gain[:, cols]

        def one(i, carry):
            part = pl.ds(pl.multiple_of(i * step, step), step)
            spread = jnp.broadcast_to(squares[0, pl.ds(i, 1), :], (128, step))
            column = jnp.transpose(spread)[:, 0:1]
            values = xs[part, cols].astype(jnp.float32)
            normed = (values * column * scale).astype(jnp.bfloat16)
            gate_part = jnp.dot(normed, w_gate[cols, :], preferred_element_type=jnp.float32)
            up_part = jnp.dot(normed, w_up[cols, :], preferred_element_type=jnp.float32)
            if first:
                acc_gate[part, :] = gate_part
                acc_up[part, :] = up_part
            else:
                acc_gate[part, :] += gate_part
                acc_up[part, :] += up_part
            return carry

        lax.fori_loop(0, slots // step, one, 0)

    absorb(0, first=True)
    arrive(3, 4)
    sent.append(send(11, place(4), 12, me, sister))
    arrive(4, 5)
    sent += [send(6, place(5), 7, down, core), send(12, place(5), 13, me, sister)]
    arrive(5, 6)
    sent.append(send(13, place(6), 14, me, sister))
    arrive(6, 7)
    sent.append(send(14, place(7), 15, me, sister))
    absorb(4)
    for tag in range(7, 11):
        arrive(tag, tag + 1)
    absorb(8)
    for tag in range(11, 15):
        arrive(tag, tag + 1)
    absorb(12)

    def finish(i, carry):
        part = pl.ds(pl.multiple_of(i * step, step), step)
        gate_values = acc_gate[part, :]
        silu = gate_values / (1.0 + jnp.exp(-gate_values))
        hidden[part, :] = (silu * acc_up[part, :]).astype(hidden.dtype)
        return carry

    lax.fori_loop(0, slots // step, finish, 0)
    for copy in sent + square_copies:
        copy.wait_send()


def far(chip):
    return lax.rem(chip + 4, 8)


def expert_in(block, norm_gain, w_gate, w_up, chips):
    slots, width = block.shape
    blocks = chips * 2
    features = blocks * width
    hidden_units = w_gate.shape[1]
    values = block.astype(jnp.float32)
    squares_part = jnp.sum(values * values, axis=1).reshape(slots // 256, 256)
    return pl.pallas_call(
        functools.partial(expert_in_kernel, width),
        out_shape=jax.ShapeDtypeStruct((slots, hidden_units), jnp.bfloat16),
        in_specs=[pl.BlockSpec(memory_space=pltpu.VMEM)] * 3
        + [pl.BlockSpec(memory_space=pl.ANY)] * 2,
        out_specs=pl.BlockSpec(memory_space=pltpu.VMEM),
        scratch_shapes=[
            pltpu.VMEM((slots, features), jnp.bfloat16),
            pltpu.VMEM(w_gate.shape, w_gate.dtype),
            pltpu.VMEM(w_up.shape, w_up.dtype),
            pltpu.VMEM((1, features), jnp.float32),
            pltpu.VMEM((slots, hidden_units), jnp.float32),
            pltpu.VMEM((slots, hidden_units), jnp.float32),
            pltpu.VMEM((blocks, slots // 256, 256), jnp.float32),
            pltpu.SemaphoreType.DMA((15,)),
            pltpu.SemaphoreType.DMA((15,)),
            pltpu.SemaphoreType.DMA(()),
            pltpu.SemaphoreType.DMA((2, blocks)),
            pltpu.SemaphoreType.DMA((blocks,)),
            pltpu.SemaphoreType.DMA((blocks,)),
        ],
        compiler_params=pltpu.CompilerParams(
            collective_id=0, has_side_effects=True, vmem_limit_bytes=60 * 1024 * 1024
        ),
    )(block, squares_part, norm_gain.reshape(1, features), w_gate, w_up)


def project(dst, hidden, weights, start):
    rows = dst.shape[0]
    step = 256
    cols = pl.ds(pl.multiple_of(start, 256), dst.shape[1])

    def one(i, carry):
        part = pl.ds(pl.multiple_of(i * step, step), step)
        dst[part, :] = jnp.dot(hidden[part, :], weights[:, cols], preferred_element_type=jnp.float32)
        return carry

    lax.fori_loop(0, rows // step, one, 0)


def add_blocks(dst, *sources):
    rows = dst.shape[0]
    step = 128

    def one(i, carry):
        part = pl.ds(pl.multiple_of(i * step, step), step)
        total = sources[0][part, :].astype(jnp.float32)
        for source in sources[1:]:
            total = total + source[part, :].astype(jnp.float32)
        dst[part, :] = total.astype(dst.dtype)
        return carry

    lax.fori_loop(0, rows // step, one, 0)


def scatter_kernel(width, hidden, weights, returned, out, mine, theirs, outgoing, sending,
                   landed, sister_send, sister_recv, send_sem, recv_sem, back_send, back_recv):
    row, me, core = lax.axis_index("row"), lax.axis_index("chip"), lax.axis_index("core")
    sister = 1 - core
    side, y = me // 4, me % 4
    partner = lax.rem(me + 4, 8)
    up = side * 4 + lax.rem(y + 1, 4)
    down = side * 4 + lax.rem(y + 3, 4)
    across = side * 4 + lax.rem(y + 2, 4)

    def far(chip):
        return lax.rem(chip + 4, 8)

    rows = returned.shape[0]
    barrier = pltpu.get_barrier_semaphore()
    for chip, half in ((partner, core), (up, core), (down, core), (me, sister)):
        pl.semaphore_signal(barrier, inc=1, device_id=(row, chip, half), device_id_type=MESH)
    for d in range(1, rows):
        pl.semaphore_signal(barrier, inc=1, device_id=(lax.rem(row + d, rows), me, core),
                            device_id_type=MESH)
    pl.semaphore_wait(barrier, 4 + rows - 1)

    order = (far(down), across, up, far(across), down, far(up), partner, me)
    swaps = []

    def produce(slots):
        for slot in slots:
            project(outgoing.at[slot], hidden, weights, (order[slot] * 2 + sister) * width)
            swap = pltpu.make_async_remote_copy(
                src_ref=outgoing.at[slot], dst_ref=theirs.at[slot], send_sem=sister_send.at[slot],
                recv_sem=sister_recv.at[slot], device_id=(row, me, sister), device_id_type=MESH,
            )
            swap.start()
            swaps.append(swap)
        for slot in slots:
            project(mine.at[slot], hidden, weights, (order[slot] * 2 + core) * width)

    produce(range(4))

    def ready(slot):
        swaps[slot].wait_recv()
        return (mine.at[slot], theirs.at[slot])

    def send(tag, chip):
        copy = pltpu.make_async_remote_copy(
            src_ref=sending.at[tag], dst_ref=landed.at[tag], send_sem=send_sem.at[tag],
            recv_sem=recv_sem.at[tag], device_id=(row, chip, core), device_id_type=MESH,
        )
        copy.start()
        return copy

    def arrive(tag):
        pltpu.make_async_remote_copy(
            src_ref=sending.at[tag], dst_ref=landed.at[tag], send_sem=send_sem.at[tag],
            recv_sem=recv_sem.at[tag], device_id=(row, me, core), device_id_type=MESH,
        ).wait_recv()

    sent = []
    for tag, chip in ((0, down), (1, down), (2, up), (3, up)):
        add_blocks(sending.at[tag], *ready(tag))
        sent.append(send(tag, chip))
    produce(range(4, 8))
    arrive(1)
    add_blocks(sending.at[4], *ready(4), landed.at[1])
    sent.append(send(4, down))
    arrive(3)
    add_blocks(sending.at[5], *ready(5), landed.at[3])
    sent.append(send(5, up))
    arrive(0)
    arrive(5)
    add_blocks(sending.at[6], *ready(6), landed.at[0], landed.at[5])
    sent.append(send(6, partner))
    arrive(2)
    arrive(4)
    add_blocks(out, *ready(7), landed.at[2], landed.at[4])
    arrive(6)
    add_blocks(out, out, landed.at[6])
    depth = returned.shape[1]
    returned[row] = out[pl.ds(pl.multiple_of(row * depth, depth), depth), :]
    backs = []
    for d in range(1, rows):
        source = lax.rem(row + d, rows)
        back = pltpu.make_async_remote_copy(
            src_ref=out.at[pl.ds(pl.multiple_of(source * depth, depth), depth), :],
            dst_ref=returned.at[row], send_sem=back_send.at[d], recv_sem=back_recv.at[d],
            device_id=(source, me, core), device_id_type=MESH,
        )
        back.start()
        backs.append(back)
    for copy in sent + swaps:
        copy.wait_send()
    for back in backs:
        back.wait()


def scatter_cols(hidden, weights, width, rows):
    slots = hidden.shape[0]
    return pl.pallas_call(
        functools.partial(scatter_kernel, width),
        out_shape=jax.ShapeDtypeStruct((rows, slots // rows, width), jnp.float32),
        in_specs=[pl.BlockSpec(memory_space=pltpu.VMEM)] * 2,
        out_specs=pl.BlockSpec(memory_space=pltpu.VMEM),
        scratch_shapes=[
            pltpu.VMEM((slots, width), jnp.float32),
            pltpu.VMEM((8, slots, width), jnp.float32),
            pltpu.VMEM((8, slots, width), jnp.float32),
            pltpu.VMEM((8, slots, width), jnp.float32),
            pltpu.VMEM((7, slots, width), jnp.bfloat16),
            pltpu.VMEM((7, slots, width), jnp.bfloat16),
            pltpu.SemaphoreType.DMA((8,)),
            pltpu.SemaphoreType.DMA((8,)),
            pltpu.SemaphoreType.DMA((7,)),
            pltpu.SemaphoreType.DMA((7,)),
            pltpu.SemaphoreType.DMA((rows,)),
            pltpu.SemaphoreType.DMA((rows,)),
        ],
        compiler_params=pltpu.CompilerParams(
            collective_id=1, has_side_effects=True, vmem_limit_bytes=60 * 1024 * 1024
        ),
    )(hidden, weights)


def body(tokens, norm_gain, expert_ids, gate_weights, w_gate, w_up, w_down):
    chips = lax.psum(1, "chip")
    width = tokens.shape[1]
    core = lax.axis_index("core")

    picker, slot_index = route_tables(expert_ids, EXPERTS, CAP)
    packed = jnp.einsum("ts,td->sd", picker, tokens, preferred_element_type=jnp.float32).astype(
        jnp.bfloat16
    )
    packed = packed.reshape(EXPERTS, CAP, width)
    arrived = lax.all_to_all(packed, "row", split_axis=0, concat_axis=0, tiled=True)
    arrived = arrived.reshape(EXPERTS * CAP, width)
    slots = arrived.shape[0]

    hidden = expert_in(arrived, norm_gain, w_gate[0], w_up[0], chips)
    returned = scatter_cols(hidden, w_down[0], width, EXPERTS)
    mixed = combine_rows(returned.reshape(-1, width), slot_index, gate_weights)
    return (tokens.astype(jnp.float32) + mixed).astype(jnp.bfloat16)


def solution(mesh):
    rows, cols = mesh.devices.shape
    split_mesh = Mesh(mesh.devices.reshape(rows, cols // 2, 2), ("row", "chip", "core"))
    placed = (
        P("row", COL),
        P(),
        P("row", None),
        P("row", None),
        P("row", None, COL),
        P("row", None, COL),
        P("row", COL, None),
    )
    return jax.shard_map(
        body, mesh=split_mesh, in_specs=placed, out_specs=P("row", COL), check_vma=False
    )
```

```python
import functools

import jax
import jax.numpy as jnp
from jax import lax
from jax.experimental import pallas as pl
from jax.experimental.pallas import tpu as pltpu
from jax.sharding import Mesh
from jax.sharding import PartitionSpec as P

EXPERTS = 8
CAP = 128
COL = ("chip", "core")
MESH = pl.DeviceIdType.MESH


def normalize(rows, norm_gain):
    values = rows.astype(jnp.float32)
    inverse_norm = lax.rsqrt(jnp.mean(values * values, axis=-1, keepdims=True) + 1e-05)
    return (values * inverse_norm * norm_gain).astype(jnp.bfloat16)


def route_tables(expert_ids, expert_count, capacity):
    token_count = expert_ids.shape[0]
    flat_ids = expert_ids.reshape(-1)
    expert_range = jnp.arange(expert_count, dtype=jnp.int32)
    expert_hits = (flat_ids[:, None] == expert_range[None, :]).astype(jnp.int32)
    earlier = jnp.cumsum(expert_hits, axis=0) - expert_hits
    ranks = jnp.sum(earlier * expert_hits, axis=1)
    slot_index = (flat_ids * capacity + ranks).reshape(token_count, -1)
    slot_ids = jnp.arange(expert_count * capacity, dtype=jnp.int32)
    matches = (slot_index[:, :, None] == slot_ids[None, None, :]).astype(jnp.float32)
    picker = jnp.sum(matches, axis=1)
    return (picker.astype(jnp.bfloat16), slot_index)


def combine_rows(slot_rows, slot_index, gate_weights):
    picked = slot_rows[slot_index]
    return jnp.sum(picked * gate_weights[:, :, None], axis=1)


def expert_in_kernel(width, packed, gain_in, w_gate_hbm, w_up_hbm, hidden, src, squares_part, xs,
                     w_gate, w_up, gain, acc_gate, acc_up, squares, send_sem, recv_sem, local_sem,
                     weight_sem, square_send, square_recv, come_send, come_recv):
    row, me, core = lax.axis_index("row"), lax.axis_index("chip"), lax.axis_index("core")
    side, y = me // 4, me % 4
    partner = lax.rem(me + 4, 8)
    up = side * 4 + lax.rem(y + 1, 4)
    down = side * 4 + lax.rem(y + 3, 4)
    across = side * 4 + lax.rem(y + 2, 4)
    sister = 1 - core
    slots = xs.shape[0]
    step = 256
    blocks = squares.shape[0]
    mine = me * 2 + core
    chips = (me, partner, down, up, far(down), far(up), across, far(across))
    features = [(chip * 2 + core) * width for chip in chips]
    features += [(chip * 2 + sister) * width for chip in chips]

    loads = []
    for place, start in enumerate(features):
        rows = pl.ds(pl.multiple_of(start, width), width)
        for index, (source, target) in enumerate(((w_gate_hbm, w_gate), (w_up_hbm, w_up))):
            load = pltpu.make_async_copy(source.at[rows, :], target.at[pl.ds(place * width, width), :],
                                         weight_sem.at[index, place])
            load.start()
            loads.append(load)
        gain[:, pl.ds(place * width, width)] = gain_in[:, rows]

    rows, depth = packed.shape[0], packed.shape[1]
    barrier = pltpu.get_barrier_semaphore()
    for d in range(1, blocks):
        other = lax.rem(mine + d, blocks)
        pl.semaphore_signal(barrier, inc=1, device_id=(row, other // 2, other % 2),
                            device_id_type=MESH)
    for d in range(1, rows):
        pl.semaphore_signal(barrier, inc=1, device_id=(lax.rem(row + d, rows), me, core),
                            device_id_type=MESH)
    pl.semaphore_wait(barrier, blocks - 1 + rows - 1)

    def rows_of(r):
        return pl.ds(pl.multiple_of(r * depth, depth), depth)

    comes = []
    for d in range(1, rows):
        target = lax.rem(row + d, rows)
        come = pltpu.make_async_remote_copy(
            src_ref=packed.at[target], dst_ref=src.at[rows_of(row), :],
            send_sem=come_send.at[d], recv_sem=come_recv.at[d],
            device_id=(target, me, core), device_id_type=MESH,
        )
        come.start()
        comes.append(come)
    src[rows_of(row), :] = packed[row]
    for come in comes:
        come.wait_recv()

    def sum_squares(i, carry):
        part = pl.ds(pl.multiple_of(i * step, step), step)
        values = src[part, :].astype(jnp.float32)
        total = jnp.sum(values * values, axis=1, keepdims=True)
        squares_part[pl.ds(i, 1), :] = jnp.transpose(jnp.broadcast_to(total, (step, 128)))[0:1, :]
        return carry

    lax.fori_loop(0, slots // step, sum_squares, 0)

    square_copies = []
    for d in range(1, blocks):
        other = lax.rem(mine + d, blocks)
        copy = pltpu.make_async_remote_copy(
            src_ref=squares_part, dst_ref=squares.at[mine], send_sem=square_send.at[d],
            recv_sem=square_recv.at[d], device_id=(row, other // 2, other % 2),
            device_id_type=MESH,
        )
        copy.start()
        square_copies.append(copy)

    def place(p):
        return xs.at[:, pl.ds(p * width, width)]

    def send(tag, source, target, chip, half):
        copy = pltpu.make_async_remote_copy(
            src_ref=source, dst_ref=place(target), send_sem=send_sem.at[tag],
            recv_sem=recv_sem.at[tag], device_id=(row, chip, half), device_id_type=MESH,
        )
        copy.start()
        return copy

    def arrive(tag, target):
        pltpu.make_async_remote_copy(
            src_ref=place(target), dst_ref=place(target), send_sem=send_sem.at[tag],
            recv_sem=recv_sem.at[tag], device_id=(row, me, sister), device_id_type=MESH,
        ).wait_recv()

    sent = [
        send(0, src, 1, partner, core),
        send(1, src, 2, up, core),
        send(2, src, 3, down, core),
        send(7, src, 8, me, sister),
    ]
    local = pltpu.make_async_copy(src, place(0), local_sem)
    local.start()
    squares[mine] = squares_part[...]
    for copy in square_copies:
        copy.wait_recv()
    total = squares[0]
    for b in range(1, blocks):
        total = total + squares[b]
    squares[0] = lax.rsqrt(total / (blocks * width) + 1e-05)

    arrive(0, 1)
    sent += [send(3, place(1), 4, up, core), send(4, place(1), 5, down, core),
             send(8, place(1), 9, me, sister)]
    arrive(1, 2)
    sent += [send(5, place(2), 6, up, core), send(9, place(2), 10, me, sister)]
    arrive(2, 3)
    sent.append(send(10, place(3), 11, me, sister))
    for load in loads:
        load.wait()
    local.wait()

    def absorb(first_place, first=False):
        cols = pl.ds(first_place * width, 4 * width)
        scale = gain[:, cols]

        def one(i, carry):
            part = pl.ds(pl.multiple_of(i * step, step), step)
            spread = jnp.broadcast_to(squares[0, pl.ds(i, 1), :], (128, step))
            column = jnp.transpose(spread)[:, 0:1]
            values = xs[part, cols].astype(jnp.float32)
            normed = (values * column * scale).astype(jnp.bfloat16)
            gate_part = jnp.dot(normed, w_gate[cols, :], preferred_element_type=jnp.float32)
            up_part = jnp.dot(normed, w_up[cols, :], preferred_element_type=jnp.float32)
            if first:
                acc_gate[part, :] = gate_part
                acc_up[part, :] = up_part
            else:
                acc_gate[part, :] += gate_part
                acc_up[part, :] += up_part
            return carry

        lax.fori_loop(0, slots // step, one, 0)

    absorb(0, first=True)
    arrive(3, 4)
    sent.append(send(11, place(4), 12, me, sister))
    arrive(4, 5)
    sent += [send(6, place(5), 7, down, core), send(12, place(5), 13, me, sister)]
    arrive(5, 6)
    sent.append(send(13, place(6), 14, me, sister))
    arrive(6, 7)
    sent.append(send(14, place(7), 15, me, sister))
    absorb(4)
    for tag in range(7, 11):
        arrive(tag, tag + 1)
    absorb(8)
    for tag in range(11, 15):
        arrive(tag, tag + 1)
    absorb(12)

    def finish(i, carry):
        part = pl.ds(pl.multiple_of(i * step, step), step)
        gate_values = acc_gate[part, :]
        silu = gate_values / (1.0 + jnp.exp(-gate_values))
        hidden[part, :] = (silu * acc_up[part, :]).astype(hidden.dtype)
        return carry

    lax.fori_loop(0, slots // step, finish, 0)
    for copy in sent + square_copies + comes:
        copy.wait_send()


def far(chip):
    return lax.rem(chip + 4, 8)


def expert_in(packed, norm_gain, w_gate, w_up, chips):
    rows, depth, width = packed.shape
    slots = rows * depth
    blocks = chips * 2
    features = blocks * width
    hidden_units = w_gate.shape[1]
    return pl.pallas_call(
        functools.partial(expert_in_kernel, width),
        out_shape=jax.ShapeDtypeStruct((slots, hidden_units), jnp.bfloat16),
        in_specs=[pl.BlockSpec(memory_space=pltpu.VMEM)] * 2
        + [pl.BlockSpec(memory_space=pl.ANY)] * 2,
        out_specs=pl.BlockSpec(memory_space=pltpu.VMEM),
        scratch_shapes=[
            pltpu.VMEM((slots, width), packed.dtype),
            pltpu.VMEM((slots // 256, 256), jnp.float32),
            pltpu.VMEM((slots, features), jnp.bfloat16),
            pltpu.VMEM(w_gate.shape, w_gate.dtype),
            pltpu.VMEM(w_up.shape, w_up.dtype),
            pltpu.VMEM((1, features), jnp.float32),
            pltpu.VMEM((slots, hidden_units), jnp.float32),
            pltpu.VMEM((slots, hidden_units), jnp.float32),
            pltpu.VMEM((blocks, slots // 256, 256), jnp.float32),
            pltpu.SemaphoreType.DMA((15,)),
            pltpu.SemaphoreType.DMA((15,)),
            pltpu.SemaphoreType.DMA(()),
            pltpu.SemaphoreType.DMA((2, blocks)),
            pltpu.SemaphoreType.DMA((blocks,)),
            pltpu.SemaphoreType.DMA((blocks,)),
            pltpu.SemaphoreType.DMA((rows,)),
            pltpu.SemaphoreType.DMA((rows,)),
        ],
        compiler_params=pltpu.CompilerParams(
            collective_id=0, has_side_effects=True, vmem_limit_bytes=60 * 1024 * 1024
        ),
    )(packed, norm_gain.reshape(1, features), w_gate, w_up)


def project(dst, hidden, weights, start):
    rows = dst.shape[0]
    step = 256
    cols = pl.ds(pl.multiple_of(start, 256), dst.shape[1])

    def one(i, carry):
        part = pl.ds(pl.multiple_of(i * step, step), step)
        dst[part, :] = jnp.dot(hidden[part, :], weights[:, cols], preferred_element_type=jnp.float32)
        return carry

    lax.fori_loop(0, rows // step, one, 0)


def add_blocks(dst, *sources):
    rows = dst.shape[0]
    step = 128

    def one(i, carry):
        part = pl.ds(pl.multiple_of(i * step, step), step)
        total = sources[0][part, :].astype(jnp.float32)
        for source in sources[1:]:
            total = total + source[part, :].astype(jnp.float32)
        dst[part, :] = total.astype(dst.dtype)
        return carry

    lax.fori_loop(0, rows // step, one, 0)


def scatter_kernel(width, hidden, weights, returned, out, mine, theirs, outgoing, sending,
                   landed, sister_send, sister_recv, send_sem, recv_sem, back_send, back_recv):
    row, me, core = lax.axis_index("row"), lax.axis_index("chip"), lax.axis_index("core")
    sister = 1 - core
    side, y = me // 4, me % 4
    partner = lax.rem(me + 4, 8)
    up = side * 4 + lax.rem(y + 1, 4)
    down = side * 4 + lax.rem(y + 3, 4)
    across = side * 4 + lax.rem(y + 2, 4)

    def far(chip):
        return lax.rem(chip + 4, 8)

    rows = returned.shape[0]
    barrier = pltpu.get_barrier_semaphore()
    for chip, half in ((partner, core), (up, core), (down, core), (me, sister)):
        pl.semaphore_signal(barrier, inc=1, device_id=(row, chip, half), device_id_type=MESH)
    for d in range(1, rows):
        pl.semaphore_signal(barrier, inc=1, device_id=(lax.rem(row + d, rows), me, core),
                            device_id_type=MESH)
    pl.semaphore_wait(barrier, 4 + rows - 1)

    order = (far(down), across, up, far(across), down, far(up), partner, me)
    swaps = []

    def produce(slots):
        for slot in slots:
            project(outgoing.at[slot], hidden, weights, (order[slot] * 2 + sister) * width)
            swap = pltpu.make_async_remote_copy(
                src_ref=outgoing.at[slot], dst_ref=theirs.at[slot], send_sem=sister_send.at[slot],
                recv_sem=sister_recv.at[slot], device_id=(row, me, sister), device_id_type=MESH,
            )
            swap.start()
            swaps.append(swap)
        for slot in slots:
            project(mine.at[slot], hidden, weights, (order[slot] * 2 + core) * width)

    produce(range(4))

    def ready(slot):
        swaps[slot].wait_recv()
        return (mine.at[slot], theirs.at[slot])

    def send(tag, chip):
        copy = pltpu.make_async_remote_copy(
            src_ref=sending.at[tag], dst_ref=landed.at[tag], send_sem=send_sem.at[tag],
            recv_sem=recv_sem.at[tag], device_id=(row, chip, core), device_id_type=MESH,
        )
        copy.start()
        return copy

    def arrive(tag):
        pltpu.make_async_remote_copy(
            src_ref=sending.at[tag], dst_ref=landed.at[tag], send_sem=send_sem.at[tag],
            recv_sem=recv_sem.at[tag], device_id=(row, me, core), device_id_type=MESH,
        ).wait_recv()

    sent = []
    for tag, chip in ((0, down), (1, down), (2, up), (3, up)):
        add_blocks(sending.at[tag], *ready(tag))
        sent.append(send(tag, chip))
    produce(range(4, 8))
    arrive(1)
    add_blocks(sending.at[4], *ready(4), landed.at[1])
    sent.append(send(4, down))
    arrive(3)
    add_blocks(sending.at[5], *ready(5), landed.at[3])
    sent.append(send(5, up))
    arrive(0)
    arrive(5)
    add_blocks(sending.at[6], *ready(6), landed.at[0], landed.at[5])
    sent.append(send(6, partner))
    arrive(2)
    arrive(4)
    add_blocks(out, *ready(7), landed.at[2], landed.at[4])
    arrive(6)
    add_blocks(out, out, landed.at[6])
    depth = returned.shape[1]
    returned[row] = out[pl.ds(pl.multiple_of(row * depth, depth), depth), :]
    backs = []
    for d in range(1, rows):
        source = lax.rem(row + d, rows)
        back = pltpu.make_async_remote_copy(
            src_ref=out.at[pl.ds(pl.multiple_of(source * depth, depth), depth), :],
            dst_ref=returned.at[row], send_sem=back_send.at[d], recv_sem=back_recv.at[d],
            device_id=(source, me, core), device_id_type=MESH,
        )
        back.start()
        backs.append(back)
    for copy in sent + swaps:
        copy.wait_send()
    for back in backs:
        back.wait()


def scatter_cols(hidden, weights, width, rows):
    slots = hidden.shape[0]
    return pl.pallas_call(
        functools.partial(scatter_kernel, width),
        out_shape=jax.ShapeDtypeStruct((rows, slots // rows, width), jnp.float32),
        in_specs=[pl.BlockSpec(memory_space=pltpu.VMEM)] * 2,
        out_specs=pl.BlockSpec(memory_space=pltpu.VMEM),
        scratch_shapes=[
            pltpu.VMEM((slots, width), jnp.float32),
            pltpu.VMEM((8, slots, width), jnp.float32),
            pltpu.VMEM((8, slots, width), jnp.float32),
            pltpu.VMEM((8, slots, width), jnp.float32),
            pltpu.VMEM((7, slots, width), jnp.bfloat16),
            pltpu.VMEM((7, slots, width), jnp.bfloat16),
            pltpu.SemaphoreType.DMA((8,)),
            pltpu.SemaphoreType.DMA((8,)),
            pltpu.SemaphoreType.DMA((7,)),
            pltpu.SemaphoreType.DMA((7,)),
            pltpu.SemaphoreType.DMA((rows,)),
            pltpu.SemaphoreType.DMA((rows,)),
        ],
        compiler_params=pltpu.CompilerParams(
            collective_id=1, has_side_effects=True, vmem_limit_bytes=60 * 1024 * 1024
        ),
    )(hidden, weights)


def body(tokens, norm_gain, expert_ids, gate_weights, w_gate, w_up, w_down):
    chips = lax.psum(1, "chip")
    width = tokens.shape[1]
    core = lax.axis_index("core")

    picker, slot_index = route_tables(expert_ids, EXPERTS, CAP)
    packed = jnp.einsum("ts,td->sd", picker, tokens, preferred_element_type=jnp.float32).astype(
        jnp.bfloat16
    )
    packed = packed.reshape(EXPERTS, CAP, width)
    hidden = expert_in(packed, norm_gain, w_gate[0], w_up[0], chips)
    returned = scatter_cols(hidden, w_down[0], width, EXPERTS)
    mixed = combine_rows(returned.reshape(-1, width), slot_index, gate_weights)
    return (tokens.astype(jnp.float32) + mixed).astype(jnp.bfloat16)


def solution(mesh):
    rows, cols = mesh.devices.shape
    split_mesh = Mesh(mesh.devices.reshape(rows, cols // 2, 2), ("row", "chip", "core"))
    placed = (
        P("row", COL),
        P(),
        P("row", None),
        P("row", None),
        P("row", None, COL),
        P("row", None, COL),
        P("row", COL, None),
    )
    return jax.shard_map(
        body, mesh=split_mesh, in_specs=placed, out_specs=P("row", COL), check_vma=False
    )
```

```python
import functools

import jax
import jax.numpy as jnp
from jax import lax
from jax.experimental import pallas as pl
from jax.experimental.pallas import tpu as pltpu
from jax.sharding import Mesh
from jax.sharding import PartitionSpec as P

EXPERTS = 8
CAP = 128
COL = ("chip", "core")
MESH = pl.DeviceIdType.MESH


def normalize(rows, norm_gain):
    values = rows.astype(jnp.float32)
    inverse_norm = lax.rsqrt(jnp.mean(values * values, axis=-1, keepdims=True) + 1e-05)
    return (values * inverse_norm * norm_gain).astype(jnp.bfloat16)


def route_tables(expert_ids, expert_count, capacity):
    token_count = expert_ids.shape[0]
    flat_ids = expert_ids.reshape(-1)
    expert_range = jnp.arange(expert_count, dtype=jnp.int32)
    expert_hits = (flat_ids[:, None] == expert_range[None, :]).astype(jnp.int32)
    earlier = jnp.cumsum(expert_hits, axis=0) - expert_hits
    ranks = jnp.sum(earlier * expert_hits, axis=1)
    slot_index = (flat_ids * capacity + ranks).reshape(token_count, -1)
    slot_ids = jnp.arange(expert_count * capacity, dtype=jnp.int32)
    matches = (slot_index[:, :, None] == slot_ids[None, None, :]).astype(jnp.float32)
    picker = jnp.sum(matches, axis=1)
    return (picker.astype(jnp.bfloat16), slot_index)


def combine_rows(slot_rows, slot_index, gate_weights):
    picked = slot_rows[slot_index]
    return jnp.sum(picked * gate_weights[:, :, None], axis=1)


def expert_in_kernel(width, packed, gain_in, w_gate_hbm, w_up_hbm, hidden, src, squares_part, xs,
                     w_gate, w_up, gain, acc_gate, acc_up, squares, send_sem, recv_sem, local_sem,
                     weight_sem, square_send, square_recv, come_send, come_recv):
    row, me, core = lax.axis_index("row"), lax.axis_index("chip"), lax.axis_index("core")
    side, y = me // 4, me % 4
    partner = lax.rem(me + 4, 8)
    up = side * 4 + lax.rem(y + 1, 4)
    down = side * 4 + lax.rem(y + 3, 4)
    across = side * 4 + lax.rem(y + 2, 4)
    sister = 1 - core
    slots = xs.shape[0]
    step = 256
    blocks = squares.shape[0]
    mine = me * 2 + core
    chips = (me, partner, down, up, far(down), far(up), across, far(across))
    features = [(chip * 2 + core) * width for chip in chips]
    features += [(chip * 2 + sister) * width for chip in chips]

    loads = []
    for place, start in enumerate(features):
        rows = pl.ds(pl.multiple_of(start, width), width)
        for index, (source, target) in enumerate(((w_gate_hbm, w_gate), (w_up_hbm, w_up))):
            load = pltpu.make_async_copy(source.at[rows, :], target.at[pl.ds(place * width, width), :],
                                         weight_sem.at[index, place])
            load.start()
            loads.append(load)
        gain[:, pl.ds(place * width, width)] = gain_in[:, rows]

    rows, depth = packed.shape[0], packed.shape[1]
    barrier = pltpu.get_barrier_semaphore()
    for d in range(1, blocks):
        other = lax.rem(mine + d, blocks)
        pl.semaphore_signal(barrier, inc=1, device_id=(row, other // 2, other % 2),
                            device_id_type=MESH)
    for d in range(1, rows):
        pl.semaphore_signal(barrier, inc=1, device_id=(lax.rem(row + d, rows), me, core),
                            device_id_type=MESH)
    pl.semaphore_wait(barrier, blocks - 1 + rows - 1)

    def rows_of(r):
        return pl.ds(pl.multiple_of(r * depth, depth), depth)

    comes = []
    for d in range(1, rows):
        target = lax.rem(row + d, rows)
        come = pltpu.make_async_remote_copy(
            src_ref=packed.at[target], dst_ref=src.at[rows_of(row), :],
            send_sem=come_send.at[d], recv_sem=come_recv.at[d],
            device_id=(target, me, core), device_id_type=MESH,
        )
        come.start()
        comes.append(come)
    src[rows_of(row), :] = packed[row]
    for come in comes:
        come.wait_recv()

    def sum_squares(i, carry):
        part = pl.ds(pl.multiple_of(i * step, step), step)
        values = src[part, :].astype(jnp.float32)
        total = jnp.sum(values * values, axis=1, keepdims=True)
        squares_part[pl.ds(i, 1), :] = jnp.transpose(jnp.broadcast_to(total, (step, 128)))[0:1, :]
        return carry

    lax.fori_loop(0, slots // step, sum_squares, 0)

    square_copies = []
    for d in range(1, blocks):
        other = lax.rem(mine + d, blocks)
        copy = pltpu.make_async_remote_copy(
            src_ref=squares_part, dst_ref=squares.at[mine], send_sem=square_send.at[d],
            recv_sem=square_recv.at[d], device_id=(row, other // 2, other % 2),
            device_id_type=MESH,
        )
        copy.start()
        square_copies.append(copy)

    def place(p):
        return xs.at[:, pl.ds(p * width, width)]

    def send(tag, source, target, chip, half):
        copy = pltpu.make_async_remote_copy(
            src_ref=source, dst_ref=place(target), send_sem=send_sem.at[tag],
            recv_sem=recv_sem.at[tag], device_id=(row, chip, half), device_id_type=MESH,
        )
        copy.start()
        return copy

    def arrive(tag, target):
        pltpu.make_async_remote_copy(
            src_ref=place(target), dst_ref=place(target), send_sem=send_sem.at[tag],
            recv_sem=recv_sem.at[tag], device_id=(row, me, sister), device_id_type=MESH,
        ).wait_recv()

    sent = [
        send(0, src, 1, partner, core),
        send(1, src, 2, up, core),
        send(2, src, 3, down, core),
        send(7, src, 8, me, sister),
    ]
    local = pltpu.make_async_copy(src, place(0), local_sem)
    local.start()
    squares[mine] = squares_part[...]
    for copy in square_copies:
        copy.wait_recv()
    total = squares[0]
    for b in range(1, blocks):
        total = total + squares[b]
    squares[0] = lax.rsqrt(total / (blocks * width) + 1e-05)

    arrive(0, 1)
    sent += [send(3, place(1), 4, up, core), send(4, place(1), 5, down, core),
             send(8, place(1), 9, me, sister)]
    arrive(1, 2)
    sent += [send(5, place(2), 6, up, core), send(9, place(2), 10, me, sister)]
    arrive(2, 3)
    sent.append(send(10, place(3), 11, me, sister))
    for load in loads:
        load.wait()
    local.wait()

    def absorb(first_place, first=False):
        cols = pl.ds(first_place * width, 4 * width)
        scale = gain[:, cols]

        def one(i, carry):
            part = pl.ds(pl.multiple_of(i * step, step), step)
            spread = jnp.broadcast_to(squares[0, pl.ds(i, 1), :], (128, step))
            column = jnp.transpose(spread)[:, 0:1]
            values = xs[part, cols].astype(jnp.float32)
            normed = (values * column * scale).astype(jnp.bfloat16)
            gate_part = jnp.dot(normed, w_gate[cols, :], preferred_element_type=jnp.float32)
            up_part = jnp.dot(normed, w_up[cols, :], preferred_element_type=jnp.float32)
            if first:
                acc_gate[part, :] = gate_part
                acc_up[part, :] = up_part
            else:
                acc_gate[part, :] += gate_part
                acc_up[part, :] += up_part
            return carry

        lax.fori_loop(0, slots // step, one, 0)

    absorb(0, first=True)
    arrive(3, 4)
    sent.append(send(11, place(4), 12, me, sister))
    arrive(4, 5)
    sent += [send(6, place(5), 7, down, core), send(12, place(5), 13, me, sister)]
    arrive(5, 6)
    sent.append(send(13, place(6), 14, me, sister))
    arrive(6, 7)
    sent.append(send(14, place(7), 15, me, sister))
    absorb(4)
    for tag in range(7, 11):
        arrive(tag, tag + 1)
    absorb(8)
    for tag in range(11, 15):
        arrive(tag, tag + 1)
    absorb(12)

    def finish(i, carry):
        part = pl.ds(pl.multiple_of(i * step, step), step)
        gate_values = acc_gate[part, :]
        silu = gate_values / (1.0 + jnp.exp(-gate_values))
        hidden[part, :] = (silu * acc_up[part, :]).astype(hidden.dtype)
        return carry

    lax.fori_loop(0, slots // step, finish, 0)
    for copy in sent + square_copies + comes:
        copy.wait_send()


def far(chip):
    return lax.rem(chip + 4, 8)


def expert_in(packed, norm_gain, w_gate, w_up, chips):
    rows, depth, width = packed.shape
    slots = rows * depth
    blocks = chips * 2
    features = blocks * width
    hidden_units = w_gate.shape[1]
    return pl.pallas_call(
        functools.partial(expert_in_kernel, width),
        out_shape=jax.ShapeDtypeStruct((slots, hidden_units), jnp.bfloat16),
        in_specs=[pl.BlockSpec(memory_space=pltpu.VMEM)] * 2
        + [pl.BlockSpec(memory_space=pl.ANY)] * 2,
        out_specs=pl.BlockSpec(memory_space=pltpu.VMEM),
        scratch_shapes=[
            pltpu.VMEM((slots, width), packed.dtype),
            pltpu.VMEM((slots // 256, 256), jnp.float32),
            pltpu.VMEM((slots, features), jnp.bfloat16),
            pltpu.VMEM(w_gate.shape, w_gate.dtype),
            pltpu.VMEM(w_up.shape, w_up.dtype),
            pltpu.VMEM((1, features), jnp.float32),
            pltpu.VMEM((slots, hidden_units), jnp.float32),
            pltpu.VMEM((slots, hidden_units), jnp.float32),
            pltpu.VMEM((blocks, slots // 256, 256), jnp.float32),
            pltpu.SemaphoreType.DMA((15,)),
            pltpu.SemaphoreType.DMA((15,)),
            pltpu.SemaphoreType.DMA(()),
            pltpu.SemaphoreType.DMA((2, blocks)),
            pltpu.SemaphoreType.DMA((blocks,)),
            pltpu.SemaphoreType.DMA((blocks,)),
            pltpu.SemaphoreType.DMA((rows,)),
            pltpu.SemaphoreType.DMA((rows,)),
        ],
        compiler_params=pltpu.CompilerParams(
            collective_id=0, has_side_effects=True, vmem_limit_bytes=60 * 1024 * 1024
        ),
    )(packed, norm_gain.reshape(1, features), w_gate, w_up)


def project(dst, hidden, weights, start):
    rows = dst.shape[0]
    step = 256
    cols = pl.ds(pl.multiple_of(start, 256), dst.shape[1])

    def one(i, carry):
        part = pl.ds(pl.multiple_of(i * step, step), step)
        dst[part, :] = jnp.dot(hidden[part, :], weights[:, cols], preferred_element_type=jnp.float32)
        return carry

    lax.fori_loop(0, rows // step, one, 0)


def add_blocks(dst, *sources):
    rows = dst.shape[0]
    step = 128

    def one(i, carry):
        part = pl.ds(pl.multiple_of(i * step, step), step)
        total = sources[0][part, :].astype(jnp.float32)
        for source in sources[1:]:
            total = total + source[part, :].astype(jnp.float32)
        dst[part, :] = total.astype(dst.dtype)
        return carry

    lax.fori_loop(0, rows // step, one, 0)


def scatter_kernel(width, hidden, weights_hbm, returned, weights, out, mine, theirs, outgoing,
                   sending, landed, weight_sem, sister_send, sister_recv, send_sem, recv_sem,
                   back_send, back_recv):
    row, me, core = lax.axis_index("row"), lax.axis_index("chip"), lax.axis_index("core")
    sister = 1 - core
    side, y = me // 4, me % 4
    partner = lax.rem(me + 4, 8)
    up = side * 4 + lax.rem(y + 1, 4)
    down = side * 4 + lax.rem(y + 3, 4)
    across = side * 4 + lax.rem(y + 2, 4)

    def far(chip):
        return lax.rem(chip + 4, 8)

    rows = returned.shape[0]
    order = (far(down), across, up, far(across), down, far(up), partner, me)
    loads = {}
    for slot, chip in enumerate(order):
        for index, half in enumerate((sister, core)):
            cols = pl.ds(pl.multiple_of((chip * 2 + half) * width, width), width)
            load = pltpu.make_async_copy(weights_hbm.at[:, cols], weights.at[:, cols],
                                         weight_sem.at[index, slot])
            load.start()
            loads[(slot, index)] = load
    barrier = pltpu.get_barrier_semaphore()
    for chip, half in ((partner, core), (up, core), (down, core), (me, sister)):
        pl.semaphore_signal(barrier, inc=1, device_id=(row, chip, half), device_id_type=MESH)
    for d in range(1, rows):
        pl.semaphore_signal(barrier, inc=1, device_id=(lax.rem(row + d, rows), me, core),
                            device_id_type=MESH)
    pl.semaphore_wait(barrier, 4 + rows - 1)

    swaps = []

    def produce(slots, own=True):
        for slot in slots:
            loads[(slot, 0)].wait()
            project(outgoing.at[slot], hidden, weights, (order[slot] * 2 + sister) * width)
            swap = pltpu.make_async_remote_copy(
                src_ref=outgoing.at[slot], dst_ref=theirs.at[slot], send_sem=sister_send.at[slot],
                recv_sem=sister_recv.at[slot], device_id=(row, me, sister), device_id_type=MESH,
            )
            swap.start()
            swaps.append(swap)
        if own:
            for slot in slots:
                own_block(slot)

    def own_block(slot):
        loads[(slot, 1)].wait()
        project(mine.at[slot], hidden, weights, (order[slot] * 2 + core) * width)

    produce(range(4), own=False)

    def ready(slot):
        swaps[slot].wait_recv()
        return (mine.at[slot], theirs.at[slot])

    def send(tag, chip):
        copy = pltpu.make_async_remote_copy(
            src_ref=sending.at[tag], dst_ref=landed.at[tag], send_sem=send_sem.at[tag],
            recv_sem=recv_sem.at[tag], device_id=(row, chip, core), device_id_type=MESH,
        )
        copy.start()
        return copy

    def arrive(tag):
        pltpu.make_async_remote_copy(
            src_ref=sending.at[tag], dst_ref=landed.at[tag], send_sem=send_sem.at[tag],
            recv_sem=recv_sem.at[tag], device_id=(row, me, core), device_id_type=MESH,
        ).wait_recv()

    sent = []
    for tag, chip in ((0, down), (1, down), (2, up), (3, up)):
        own_block(tag)
        add_blocks(sending.at[tag], *ready(tag))
        sent.append(send(tag, chip))
    produce(range(4, 8))
    arrive(1)
    add_blocks(sending.at[4], *ready(4), landed.at[1])
    sent.append(send(4, down))
    arrive(3)
    add_blocks(sending.at[5], *ready(5), landed.at[3])
    sent.append(send(5, up))
    arrive(0)
    arrive(5)
    add_blocks(sending.at[6], *ready(6), landed.at[0], landed.at[5])
    sent.append(send(6, partner))
    arrive(2)
    arrive(4)
    add_blocks(out, *ready(7), landed.at[2], landed.at[4])
    arrive(6)
    add_blocks(out, out, landed.at[6])
    depth = returned.shape[1]
    returned[row] = out[pl.ds(pl.multiple_of(row * depth, depth), depth), :]
    backs = []
    for d in range(1, rows):
        source = lax.rem(row + d, rows)
        back = pltpu.make_async_remote_copy(
            src_ref=out.at[pl.ds(pl.multiple_of(source * depth, depth), depth), :],
            dst_ref=returned.at[row], send_sem=back_send.at[d], recv_sem=back_recv.at[d],
            device_id=(source, me, core), device_id_type=MESH,
        )
        back.start()
        backs.append(back)
    for copy in sent + swaps:
        copy.wait_send()
    for back in backs:
        back.wait()


def scatter_cols(hidden, weights, width, rows):
    slots = hidden.shape[0]
    return pl.pallas_call(
        functools.partial(scatter_kernel, width),
        out_shape=jax.ShapeDtypeStruct((rows, slots // rows, width), jnp.float32),
        in_specs=[pl.BlockSpec(memory_space=pltpu.VMEM), pl.BlockSpec(memory_space=pl.ANY)],
        out_specs=pl.BlockSpec(memory_space=pltpu.VMEM),
        scratch_shapes=[
            pltpu.VMEM(weights.shape, weights.dtype),
            pltpu.VMEM((slots, width), jnp.float32),
            pltpu.VMEM((8, slots, width), jnp.float32),
            pltpu.VMEM((8, slots, width), jnp.float32),
            pltpu.VMEM((8, slots, width), jnp.float32),
            pltpu.VMEM((7, slots, width), jnp.bfloat16),
            pltpu.VMEM((7, slots, width), jnp.bfloat16),
            pltpu.SemaphoreType.DMA((2, 8)),
            pltpu.SemaphoreType.DMA((8,)),
            pltpu.SemaphoreType.DMA((8,)),
            pltpu.SemaphoreType.DMA((7,)),
            pltpu.SemaphoreType.DMA((7,)),
            pltpu.SemaphoreType.DMA((rows,)),
            pltpu.SemaphoreType.DMA((rows,)),
        ],
        compiler_params=pltpu.CompilerParams(
            collective_id=1, has_side_effects=True, vmem_limit_bytes=60 * 1024 * 1024
        ),
    )(hidden, weights)


def body(tokens, norm_gain, expert_ids, gate_weights, w_gate, w_up, w_down):
    chips = lax.psum(1, "chip")
    width = tokens.shape[1]
    core = lax.axis_index("core")

    picker, slot_index = route_tables(expert_ids, EXPERTS, CAP)
    packed = jnp.einsum("ts,td->sd", picker, tokens, preferred_element_type=jnp.float32).astype(
        jnp.bfloat16
    )
    packed = packed.reshape(EXPERTS, CAP, width)
    hidden = expert_in(packed, norm_gain, w_gate[0], w_up[0], chips)
    returned = scatter_cols(hidden, w_down[0], width, EXPERTS)
    mixed = combine_rows(returned.reshape(-1, width), slot_index, gate_weights)
    return (tokens.astype(jnp.float32) + mixed).astype(jnp.bfloat16)


def solution(mesh):
    rows, cols = mesh.devices.shape
    split_mesh = Mesh(mesh.devices.reshape(rows, cols // 2, 2), ("row", "chip", "core"))
    placed = (
        P("row", COL),
        P(),
        P("row", None),
        P("row", None),
        P("row", None, COL),
        P("row", None, COL),
        P("row", COL, None),
    )
    return jax.shard_map(
        body, mesh=split_mesh, in_specs=placed, out_specs=P("row", COL), check_vma=False
    )
```

```python
import functools

import jax
import jax.numpy as jnp
from jax import lax
from jax.experimental import pallas as pl
from jax.experimental.pallas import tpu as pltpu
from jax.sharding import Mesh
from jax.sharding import PartitionSpec as P

EXPERTS = 8
CAP = 128
COL = ("chip", "core")
MESH = pl.DeviceIdType.MESH


def normalize(rows, norm_gain):
    values = rows.astype(jnp.float32)
    inverse_norm = lax.rsqrt(jnp.mean(values * values, axis=-1, keepdims=True) + 1e-05)
    return (values * inverse_norm * norm_gain).astype(jnp.bfloat16)


def route_tables(expert_ids, expert_count, capacity):
    token_count = expert_ids.shape[0]
    flat_ids = expert_ids.reshape(-1)
    expert_range = jnp.arange(expert_count, dtype=jnp.int32)
    expert_hits = (flat_ids[:, None] == expert_range[None, :]).astype(jnp.int32)
    earlier = jnp.cumsum(expert_hits, axis=0) - expert_hits
    ranks = jnp.sum(earlier * expert_hits, axis=1)
    slot_index = (flat_ids * capacity + ranks).reshape(token_count, -1)
    slot_ids = jnp.arange(expert_count * capacity, dtype=jnp.int32)
    matches = (slot_index[:, :, None] == slot_ids[None, None, :]).astype(jnp.float32)
    picker = jnp.sum(matches, axis=1)
    return (picker.astype(jnp.bfloat16), slot_index)


def combine_rows(slot_rows, slot_index, gate_weights):
    picked = slot_rows[slot_index]
    return jnp.sum(picked * gate_weights[:, :, None], axis=1)


def expert_in_kernel(width, packed, gain_in, w_gate_hbm, w_up_hbm, hidden, src, squares_part, xs,
                     w_gate, w_up, gain, acc_gate, acc_up, squares, send_sem, recv_sem, local_sem,
                     weight_sem, square_send, square_recv, come_send, come_recv):
    row, me, core = lax.axis_index("row"), lax.axis_index("chip"), lax.axis_index("core")
    side, y = me // 4, me % 4
    partner = lax.rem(me + 4, 8)
    up = side * 4 + lax.rem(y + 1, 4)
    down = side * 4 + lax.rem(y + 3, 4)
    across = side * 4 + lax.rem(y + 2, 4)
    sister = 1 - core
    slots = xs.shape[0]
    step = 256
    blocks = squares.shape[0]
    mine = me * 2 + core
    chips = (me, partner, down, up, far(down), far(up), across, far(across))
    features = [(chip * 2 + core) * width for chip in chips]
    features += [(chip * 2 + sister) * width for chip in chips]

    loads = []
    for place, start in enumerate(features):
        rows = pl.ds(pl.multiple_of(start, width), width)
        for index, (source, target) in enumerate(((w_gate_hbm, w_gate), (w_up_hbm, w_up))):
            load = pltpu.make_async_copy(source.at[rows, :], target.at[pl.ds(place * width, width), :],
                                         weight_sem.at[index, place])
            load.start()
            loads.append(load)
        gain[:, pl.ds(place * width, width)] = gain_in[:, rows]

    rows, depth = packed.shape[0], packed.shape[1]
    barrier = pltpu.get_barrier_semaphore()
    for d in range(1, blocks):
        other = lax.rem(mine + d, blocks)
        pl.semaphore_signal(barrier, inc=1, device_id=(row, other // 2, other % 2),
                            device_id_type=MESH)
    for d in range(1, rows):
        pl.semaphore_signal(barrier, inc=1, device_id=(lax.rem(row + d, rows), me, core),
                            device_id_type=MESH)
    pl.semaphore_wait(barrier, blocks - 1 + rows - 1)

    def rows_of(r):
        return pl.ds(pl.multiple_of(r * depth, depth), depth)

    comes = []
    for d in range(1, rows):
        target = lax.rem(row + d, rows)
        come = pltpu.make_async_remote_copy(
            src_ref=packed.at[target], dst_ref=src.at[rows_of(row), :],
            send_sem=come_send.at[d], recv_sem=come_recv.at[d],
            device_id=(target, me, core), device_id_type=MESH,
        )
        come.start()
        comes.append(come)
    src[rows_of(row), :] = packed[row]
    for come in comes:
        come.wait_recv()

    def sum_squares(i, carry):
        part = pl.ds(pl.multiple_of(i * step, step), step)
        values = src[part, :].astype(jnp.float32)
        total = jnp.sum(values * values, axis=1, keepdims=True)
        squares_part[pl.ds(i, 1), :] = jnp.transpose(jnp.broadcast_to(total, (step, 128)))[0:1, :]
        return carry

    lax.fori_loop(0, slots // step, sum_squares, 0)

    square_copies = []
    for d in range(1, blocks):
        other = lax.rem(mine + d, blocks)
        copy = pltpu.make_async_remote_copy(
            src_ref=squares_part, dst_ref=squares.at[mine], send_sem=square_send.at[d],
            recv_sem=square_recv.at[d], device_id=(row, other // 2, other % 2),
            device_id_type=MESH,
        )
        copy.start()
        square_copies.append(copy)

    def place(p):
        return xs.at[:, pl.ds(p * width, width)]

    def send(tag, source, target, chip, half):
        copy = pltpu.make_async_remote_copy(
            src_ref=source, dst_ref=place(target), send_sem=send_sem.at[tag],
            recv_sem=recv_sem.at[tag], device_id=(row, chip, half), device_id_type=MESH,
        )
        copy.start()
        return copy

    def arrive(tag, target):
        pltpu.make_async_remote_copy(
            src_ref=place(target), dst_ref=place(target), send_sem=send_sem.at[tag],
            recv_sem=recv_sem.at[tag], device_id=(row, me, sister), device_id_type=MESH,
        ).wait_recv()

    sent = [
        send(0, src, 1, partner, core),
        send(1, src, 2, up, core),
        send(2, src, 3, down, core),
        send(7, src, 8, me, sister),
    ]
    local = pltpu.make_async_copy(src, place(0), local_sem)
    local.start()
    squares[mine] = squares_part[...]
    for copy in square_copies:
        copy.wait_recv()
    total = squares[0]
    for b in range(1, blocks):
        total = total + squares[b]
    squares[0] = lax.rsqrt(total / (blocks * width) + 1e-05)

    arrive(0, 1)
    sent += [send(3, place(1), 4, up, core), send(4, place(1), 5, down, core),
             send(8, place(1), 9, me, sister)]
    arrive(1, 2)
    sent += [send(5, place(2), 6, up, core), send(9, place(2), 10, me, sister)]
    arrive(2, 3)
    sent.append(send(10, place(3), 11, me, sister))
    for load in loads:
        load.wait()
    local.wait()

    def absorb(first_place, count=4, first=False, last=False):
        cols = pl.ds(first_place * width, count * width)
        scale = gain[:, cols]

        def one(i, carry):
            part = pl.ds(pl.multiple_of(i * step, step), step)
            spread = jnp.broadcast_to(squares[0, pl.ds(i, 1), :], (128, step))
            column = jnp.transpose(spread)[:, 0:1]
            values = xs[part, cols].astype(jnp.float32)
            normed = (values * column * scale).astype(jnp.bfloat16)
            gate_part = jnp.dot(normed, w_gate[cols, :], preferred_element_type=jnp.float32)
            up_part = jnp.dot(normed, w_up[cols, :], preferred_element_type=jnp.float32)
            if first:
                acc_gate[part, :] = gate_part
                acc_up[part, :] = up_part
            elif last:
                gate_values = acc_gate[part, :] + gate_part
                silu = gate_values / (1.0 + jnp.exp(-gate_values))
                hidden[part, :] = (silu * (acc_up[part, :] + up_part)).astype(hidden.dtype)
            else:
                acc_gate[part, :] += gate_part
                acc_up[part, :] += up_part
            return carry

        lax.fori_loop(0, slots // step, one, 0)

    absorb(0, first=True)
    arrive(3, 4)
    sent.append(send(11, place(4), 12, me, sister))
    arrive(4, 5)
    sent += [send(6, place(5), 7, down, core), send(12, place(5), 13, me, sister)]
    arrive(5, 6)
    sent.append(send(13, place(6), 14, me, sister))
    arrive(6, 7)
    sent.append(send(14, place(7), 15, me, sister))
    absorb(4)
    for tag in range(7, 11):
        arrive(tag, tag + 1)
    absorb(8)
    for tag in range(11, 13):
        arrive(tag, tag + 1)
    absorb(12, count=2)
    for tag in range(13, 15):
        arrive(tag, tag + 1)
    absorb(14, count=2, last=True)
    for copy in sent + square_copies + comes:
        copy.wait_send()


def far(chip):
    return lax.rem(chip + 4, 8)


def expert_in(packed, norm_gain, w_gate, w_up, chips):
    rows, depth, width = packed.shape
    slots = rows * depth
    blocks = chips * 2
    features = blocks * width
    hidden_units = w_gate.shape[1]
    return pl.pallas_call(
        functools.partial(expert_in_kernel, width),
        out_shape=jax.ShapeDtypeStruct((slots, hidden_units), jnp.bfloat16),
        in_specs=[pl.BlockSpec(memory_space=pltpu.VMEM)] * 2
        + [pl.BlockSpec(memory_space=pl.ANY)] * 2,
        out_specs=pl.BlockSpec(memory_space=pltpu.VMEM),
        scratch_shapes=[
            pltpu.VMEM((slots, width), packed.dtype),
            pltpu.VMEM((slots // 256, 256), jnp.float32),
            pltpu.VMEM((slots, features), jnp.bfloat16),
            pltpu.VMEM(w_gate.shape, w_gate.dtype),
            pltpu.VMEM(w_up.shape, w_up.dtype),
            pltpu.VMEM((1, features), jnp.float32),
            pltpu.VMEM((slots, hidden_units), jnp.float32),
            pltpu.VMEM((slots, hidden_units), jnp.float32),
            pltpu.VMEM((blocks, slots // 256, 256), jnp.float32),
            pltpu.SemaphoreType.DMA((15,)),
            pltpu.SemaphoreType.DMA((15,)),
            pltpu.SemaphoreType.DMA(()),
            pltpu.SemaphoreType.DMA((2, blocks)),
            pltpu.SemaphoreType.DMA((blocks,)),
            pltpu.SemaphoreType.DMA((blocks,)),
            pltpu.SemaphoreType.DMA((rows,)),
            pltpu.SemaphoreType.DMA((rows,)),
        ],
        compiler_params=pltpu.CompilerParams(
            collective_id=0, has_side_effects=True, vmem_limit_bytes=60 * 1024 * 1024
        ),
    )(packed, norm_gain.reshape(1, features), w_gate, w_up)


def project(dst, hidden, weights, start):
    rows = dst.shape[0]
    step = 256
    cols = pl.ds(pl.multiple_of(start, 256), dst.shape[1])

    def one(i, carry):
        part = pl.ds(pl.multiple_of(i * step, step), step)
        dst[part, :] = jnp.dot(hidden[part, :], weights[:, cols], preferred_element_type=jnp.float32)
        return carry

    lax.fori_loop(0, rows // step, one, 0)


def add_blocks(dst, *sources):
    rows = dst.shape[0]
    step = 128

    def one(i, carry):
        part = pl.ds(pl.multiple_of(i * step, step), step)
        total = sources[0][part, :].astype(jnp.float32)
        for source in sources[1:]:
            total = total + source[part, :].astype(jnp.float32)
        dst[part, :] = total.astype(dst.dtype)
        return carry

    lax.fori_loop(0, rows // step, one, 0)


def scatter_kernel(width, hidden, weights_hbm, returned, weights, out, mine, theirs, outgoing,
                   sending, landed, weight_sem, sister_send, sister_recv, send_sem, recv_sem,
                   back_send, back_recv):
    row, me, core = lax.axis_index("row"), lax.axis_index("chip"), lax.axis_index("core")
    sister = 1 - core
    side, y = me // 4, me % 4
    partner = lax.rem(me + 4, 8)
    up = side * 4 + lax.rem(y + 1, 4)
    down = side * 4 + lax.rem(y + 3, 4)
    across = side * 4 + lax.rem(y + 2, 4)

    def far(chip):
        return lax.rem(chip + 4, 8)

    rows = returned.shape[0]
    order = (far(down), across, up, far(across), down, far(up), partner, me)
    loads = {}
    for slot, chip in enumerate(order):
        for index, half in enumerate((sister, core)):
            cols = pl.ds(pl.multiple_of((chip * 2 + half) * width, width), width)
            load = pltpu.make_async_copy(weights_hbm.at[:, cols], weights.at[:, cols],
                                         weight_sem.at[index, slot])
            load.start()
            loads[(slot, index)] = load
    barrier = pltpu.get_barrier_semaphore()
    for chip, half in ((partner, core), (up, core), (down, core), (me, sister)):
        pl.semaphore_signal(barrier, inc=1, device_id=(row, chip, half), device_id_type=MESH)
    for d in range(1, rows):
        pl.semaphore_signal(barrier, inc=1, device_id=(lax.rem(row + d, rows), me, core),
                            device_id_type=MESH)
    pl.semaphore_wait(barrier, 4 + rows - 1)

    swaps = []

    def produce(slots, own=True):
        for slot in slots:
            loads[(slot, 0)].wait()
            project(outgoing.at[slot], hidden, weights, (order[slot] * 2 + sister) * width)
            swap = pltpu.make_async_remote_copy(
                src_ref=outgoing.at[slot], dst_ref=theirs.at[slot], send_sem=sister_send.at[slot],
                recv_sem=sister_recv.at[slot], device_id=(row, me, sister), device_id_type=MESH,
            )
            swap.start()
            swaps.append(swap)
        if own:
            for slot in slots:
                own_block(slot)

    def own_block(slot):
        loads[(slot, 1)].wait()
        project(mine.at[slot], hidden, weights, (order[slot] * 2 + core) * width)

    produce(range(4), own=False)

    def ready(slot):
        swaps[slot].wait_recv()
        return (mine.at[slot], theirs.at[slot])

    def send(tag, chip):
        copy = pltpu.make_async_remote_copy(
            src_ref=sending.at[tag], dst_ref=landed.at[tag], send_sem=send_sem.at[tag],
            recv_sem=recv_sem.at[tag], device_id=(row, chip, core), device_id_type=MESH,
        )
        copy.start()
        return copy

    def arrive(tag):
        pltpu.make_async_remote_copy(
            src_ref=sending.at[tag], dst_ref=landed.at[tag], send_sem=send_sem.at[tag],
            recv_sem=recv_sem.at[tag], device_id=(row, me, core), device_id_type=MESH,
        ).wait_recv()

    sent = []
    for tag, chip in ((0, down), (1, down), (2, up), (3, up)):
        own_block(tag)
        add_blocks(sending.at[tag], *ready(tag))
        sent.append(send(tag, chip))
    produce(range(4, 8))
    arrive(1)
    add_blocks(sending.at[4], *ready(4), landed.at[1])
    sent.append(send(4, down))
    arrive(3)
    add_blocks(sending.at[5], *ready(5), landed.at[3])
    sent.append(send(5, up))
    arrive(0)
    arrive(5)
    add_blocks(sending.at[6], *ready(6), landed.at[0], landed.at[5])
    sent.append(send(6, partner))
    arrive(2)
    arrive(4)
    add_blocks(out, *ready(7), landed.at[2], landed.at[4])
    arrive(6)
    add_blocks(out, out, landed.at[6])
    depth = returned.shape[1]
    returned[row] = out[pl.ds(pl.multiple_of(row * depth, depth), depth), :]
    backs = []
    for d in range(1, rows):
        source = lax.rem(row + d, rows)
        back = pltpu.make_async_remote_copy(
            src_ref=out.at[pl.ds(pl.multiple_of(source * depth, depth), depth), :],
            dst_ref=returned.at[row], send_sem=back_send.at[d], recv_sem=back_recv.at[d],
            device_id=(source, me, core), device_id_type=MESH,
        )
        back.start()
        backs.append(back)
    for copy in sent + swaps:
        copy.wait_send()
    for back in backs:
        back.wait()


def scatter_cols(hidden, weights, width, rows):
    slots = hidden.shape[0]
    return pl.pallas_call(
        functools.partial(scatter_kernel, width),
        out_shape=jax.ShapeDtypeStruct((rows, slots // rows, width), jnp.float32),
        in_specs=[pl.BlockSpec(memory_space=pltpu.VMEM), pl.BlockSpec(memory_space=pl.ANY)],
        out_specs=pl.BlockSpec(memory_space=pltpu.VMEM),
        scratch_shapes=[
            pltpu.VMEM(weights.shape, weights.dtype),
            pltpu.VMEM((slots, width), jnp.float32),
            pltpu.VMEM((8, slots, width), jnp.float32),
            pltpu.VMEM((8, slots, width), jnp.float32),
            pltpu.VMEM((8, slots, width), jnp.float32),
            pltpu.VMEM((7, slots, width), jnp.bfloat16),
            pltpu.VMEM((7, slots, width), jnp.bfloat16),
            pltpu.SemaphoreType.DMA((2, 8)),
            pltpu.SemaphoreType.DMA((8,)),
            pltpu.SemaphoreType.DMA((8,)),
            pltpu.SemaphoreType.DMA((7,)),
            pltpu.SemaphoreType.DMA((7,)),
            pltpu.SemaphoreType.DMA((rows,)),
            pltpu.SemaphoreType.DMA((rows,)),
        ],
        compiler_params=pltpu.CompilerParams(
            collective_id=1, has_side_effects=True, vmem_limit_bytes=60 * 1024 * 1024
        ),
    )(hidden, weights)


def body(tokens, norm_gain, expert_ids, gate_weights, w_gate, w_up, w_down):
    chips = lax.psum(1, "chip")
    width = tokens.shape[1]
    core = lax.axis_index("core")

    picker, slot_index = route_tables(expert_ids, EXPERTS, CAP)
    packed = jnp.einsum("ts,td->sd", picker, tokens, preferred_element_type=jnp.float32).astype(
        jnp.bfloat16
    )
    packed = packed.reshape(EXPERTS, CAP, width)
    hidden = expert_in(packed, norm_gain, w_gate[0], w_up[0], chips)
    returned = scatter_cols(hidden, w_down[0], width, EXPERTS)
    mixed = combine_rows(returned.reshape(-1, width), slot_index, gate_weights)
    return (tokens.astype(jnp.float32) + mixed).astype(jnp.bfloat16)


def solution(mesh):
    rows, cols = mesh.devices.shape
    split_mesh = Mesh(mesh.devices.reshape(rows, cols // 2, 2), ("row", "chip", "core"))
    placed = (
        P("row", COL),
        P(),
        P("row", None),
        P("row", None),
        P("row", None, COL),
        P("row", None, COL),
        P("row", COL, None),
    )
    return jax.shard_map(
        body, mesh=split_mesh, in_specs=placed, out_specs=P("row", COL), check_vma=False
    )
```

```python
import functools

import jax
import jax.numpy as jnp
from jax import lax
from jax.experimental import pallas as pl
from jax.experimental.pallas import tpu as pltpu
from jax.sharding import Mesh
from jax.sharding import PartitionSpec as P

EXPERTS = 8
CAP = 128
COL = ("chip", "core")
MESH = pl.DeviceIdType.MESH


def normalize(rows, norm_gain):
    values = rows.astype(jnp.float32)
    inverse_norm = lax.rsqrt(jnp.mean(values * values, axis=-1, keepdims=True) + 1e-05)
    return (values * inverse_norm * norm_gain).astype(jnp.bfloat16)


def route_tables(expert_ids, expert_count, capacity):
    token_count = expert_ids.shape[0]
    flat_ids = expert_ids.reshape(-1)
    expert_range = jnp.arange(expert_count, dtype=jnp.int32)
    expert_hits = (flat_ids[:, None] == expert_range[None, :]).astype(jnp.int32)
    earlier = jnp.cumsum(expert_hits, axis=0) - expert_hits
    ranks = jnp.sum(earlier * expert_hits, axis=1)
    slot_index = (flat_ids * capacity + ranks).reshape(token_count, -1)
    slot_ids = jnp.arange(expert_count * capacity, dtype=jnp.int32)
    matches = (slot_index[:, :, None] == slot_ids[None, None, :]).astype(jnp.float32)
    picker = jnp.sum(matches, axis=1)
    return (picker.astype(jnp.bfloat16), slot_index)


def combine_rows(slot_rows, slot_index, gate_weights):
    picked = slot_rows[slot_index]
    return jnp.sum(picked * gate_weights[:, :, None], axis=1)


def expert_in_kernel(width, packed, gain_in, w_gate_hbm, w_up_hbm, hidden, src, squares_part, xs,
                     w_gate, w_up, gain, acc_gate, acc_up, squares, send_sem, recv_sem, local_sem,
                     weight_sem, square_send, square_recv, come_send, come_recv):
    row, me, core = lax.axis_index("row"), lax.axis_index("chip"), lax.axis_index("core")
    side, y = me // 4, me % 4
    partner = lax.rem(me + 4, 8)
    up = side * 4 + lax.rem(y + 1, 4)
    down = side * 4 + lax.rem(y + 3, 4)
    across = side * 4 + lax.rem(y + 2, 4)
    sister = 1 - core
    slots = xs.shape[0]
    step = 256
    blocks = squares.shape[0]
    mine = me * 2 + core
    chips = (me, partner, down, up, far(down), far(up), across, far(across))
    features = [(chip * 2 + core) * width for chip in chips]
    features += [(chip * 2 + sister) * width for chip in chips]

    loads = []
    for place, start in enumerate(features):
        rows = pl.ds(pl.multiple_of(start, width), width)
        for index, (source, target) in enumerate(((w_gate_hbm, w_gate), (w_up_hbm, w_up))):
            load = pltpu.make_async_copy(source.at[rows, :], target.at[pl.ds(place * width, width), :],
                                         weight_sem.at[index, place])
            load.start()
            loads.append(load)
        gain[:, pl.ds(place * width, width)] = gain_in[:, rows]

    rows, depth = packed.shape[0], packed.shape[1]
    barrier = pltpu.get_barrier_semaphore()
    for d in range(1, blocks):
        other = lax.rem(mine + d, blocks)
        pl.semaphore_signal(barrier, inc=1, device_id=(row, other // 2, other % 2),
                            device_id_type=MESH)
    for d in range(1, rows):
        pl.semaphore_signal(barrier, inc=1, device_id=(lax.rem(row + d, rows), me, core),
                            device_id_type=MESH)
    pl.semaphore_wait(barrier, blocks - 1 + rows - 1)

    def rows_of(r):
        return pl.ds(pl.multiple_of(r * depth, depth), depth)

    comes = []
    for d in range(1, rows):
        target = lax.rem(row + d, rows)
        come = pltpu.make_async_remote_copy(
            src_ref=packed.at[target], dst_ref=src.at[rows_of(row), :],
            send_sem=come_send.at[d], recv_sem=come_recv.at[d],
            device_id=(target, me, core), device_id_type=MESH,
        )
        come.start()
        comes.append(come)
    src[rows_of(row), :] = packed[row]
    for come in comes:
        come.wait_recv()

    def sum_squares(i, carry):
        part = pl.ds(pl.multiple_of(i * step, step), step)
        values = src[part, :].astype(jnp.float32)
        total = jnp.sum(values * values, axis=1, keepdims=True)
        squares_part[pl.ds(i, 1), :] = jnp.transpose(jnp.broadcast_to(total, (step, 128)))[0:1, :]
        return carry

    lax.fori_loop(0, slots // step, sum_squares, 0)

    square_copies = []
    for d in range(1, blocks):
        other = lax.rem(mine + d, blocks)
        copy = pltpu.make_async_remote_copy(
            src_ref=squares_part, dst_ref=squares.at[mine], send_sem=square_send.at[d],
            recv_sem=square_recv.at[d], device_id=(row, other // 2, other % 2),
            device_id_type=MESH,
        )
        copy.start()
        square_copies.append(copy)

    half_rows = slots // 2

    def rows_half(h):
        return pl.ds(h * half_rows, half_rows)

    def place(p, h=None):
        if h is None:
            return xs.at[:, pl.ds(p * width, width)]
        return xs.at[rows_half(h), pl.ds(p * width, width)]

    def send(tag, source, target, chip, half, h):
        origin = src.at[rows_half(h), :] if source is None else place(source, h)
        copy = pltpu.make_async_remote_copy(
            src_ref=origin, dst_ref=place(target, h), send_sem=send_sem.at[tag, h],
            recv_sem=recv_sem.at[tag, h], device_id=(row, chip, half), device_id_type=MESH,
        )
        copy.start()
        return copy

    def arrive(tag, target, h):
        pltpu.make_async_remote_copy(
            src_ref=place(target, h), dst_ref=place(target, h), send_sem=send_sem.at[tag, h],
            recv_sem=recv_sem.at[tag, h], device_id=(row, me, sister), device_id_type=MESH,
        ).wait_recv()

    sent = []
    for h in (0, 1):
        sent += [send(0, None, 1, partner, core, h), send(1, None, 2, up, core, h),
                 send(2, None, 3, down, core, h), send(7, None, 8, me, sister, h)]
    local = pltpu.make_async_copy(src, place(0), local_sem)
    local.start()
    squares[mine] = squares_part[...]
    for copy in square_copies:
        copy.wait_recv()
    total = squares[0]
    for b in range(1, blocks):
        total = total + squares[b]
    squares[0] = lax.rsqrt(total / (blocks * width) + 1e-05)

    for h in (0, 1):
        arrive(0, 1, h)
        sent += [send(3, 1, 4, up, core, h), send(4, 1, 5, down, core, h),
                 send(8, 1, 9, me, sister, h)]
        arrive(1, 2, h)
        sent += [send(5, 2, 6, up, core, h), send(9, 2, 10, me, sister, h)]
        arrive(2, 3, h)
        sent.append(send(10, 3, 11, me, sister, h))
    for load in loads:
        load.wait()
    local.wait()

    def absorb(first_place, first=False):
        cols = pl.ds(first_place * width, 4 * width)
        scale = gain[:, cols]

        def one(i, carry):
            part = pl.ds(pl.multiple_of(i * step, step), step)
            spread = jnp.broadcast_to(squares[0, pl.ds(i, 1), :], (128, step))
            column = jnp.transpose(spread)[:, 0:1]
            values = xs[part, cols].astype(jnp.float32)
            normed = (values * column * scale).astype(jnp.bfloat16)
            gate_part = jnp.dot(normed, w_gate[cols, :], preferred_element_type=jnp.float32)
            up_part = jnp.dot(normed, w_up[cols, :], preferred_element_type=jnp.float32)
            if first:
                acc_gate[part, :] = gate_part
                acc_up[part, :] = up_part
            else:
                acc_gate[part, :] += gate_part
                acc_up[part, :] += up_part
            return carry

        lax.fori_loop(0, slots // step, one, 0)

    absorb(0, first=True)
    for h in (0, 1):
        arrive(3, 4, h)
        sent.append(send(11, 4, 12, me, sister, h))
        arrive(4, 5, h)
        sent += [send(6, 5, 7, down, core, h), send(12, 5, 13, me, sister, h)]
        arrive(5, 6, h)
        sent.append(send(13, 6, 14, me, sister, h))
        arrive(6, 7, h)
        sent.append(send(14, 7, 15, me, sister, h))
    absorb(4)
    for tag in range(7, 11):
        for h in (0, 1):
            arrive(tag, tag + 1, h)
    absorb(8)
    for tag in range(11, 15):
        for h in (0, 1):
            arrive(tag, tag + 1, h)
    absorb(12)

    def finish(i, carry):
        part = pl.ds(pl.multiple_of(i * step, step), step)
        gate_values = acc_gate[part, :]
        silu = gate_values / (1.0 + jnp.exp(-gate_values))
        hidden[part, :] = (silu * acc_up[part, :]).astype(hidden.dtype)
        return carry

    lax.fori_loop(0, slots // step, finish, 0)
    for copy in sent + square_copies + comes:
        copy.wait_send()


def far(chip):
    return lax.rem(chip + 4, 8)


def expert_in(packed, norm_gain, w_gate, w_up, chips):
    rows, depth, width = packed.shape
    slots = rows * depth
    blocks = chips * 2
    features = blocks * width
    hidden_units = w_gate.shape[1]
    return pl.pallas_call(
        functools.partial(expert_in_kernel, width),
        out_shape=jax.ShapeDtypeStruct((slots, hidden_units), jnp.bfloat16),
        in_specs=[pl.BlockSpec(memory_space=pltpu.VMEM)] * 2
        + [pl.BlockSpec(memory_space=pl.ANY)] * 2,
        out_specs=pl.BlockSpec(memory_space=pltpu.VMEM),
        scratch_shapes=[
            pltpu.VMEM((slots, width), packed.dtype),
            pltpu.VMEM((slots // 256, 256), jnp.float32),
            pltpu.VMEM((slots, features), jnp.bfloat16),
            pltpu.VMEM(w_gate.shape, w_gate.dtype),
            pltpu.VMEM(w_up.shape, w_up.dtype),
            pltpu.VMEM((1, features), jnp.float32),
            pltpu.VMEM((slots, hidden_units), jnp.float32),
            pltpu.VMEM((slots, hidden_units), jnp.float32),
            pltpu.VMEM((blocks, slots // 256, 256), jnp.float32),
            pltpu.SemaphoreType.DMA((15, 2)),
            pltpu.SemaphoreType.DMA((15, 2)),
            pltpu.SemaphoreType.DMA(()),
            pltpu.SemaphoreType.DMA((2, blocks)),
            pltpu.SemaphoreType.DMA((blocks,)),
            pltpu.SemaphoreType.DMA((blocks,)),
            pltpu.SemaphoreType.DMA((rows,)),
            pltpu.SemaphoreType.DMA((rows,)),
        ],
        compiler_params=pltpu.CompilerParams(
            collective_id=0, has_side_effects=True, vmem_limit_bytes=60 * 1024 * 1024
        ),
    )(packed, norm_gain.reshape(1, features), w_gate, w_up)


def project(dst, hidden, weights, start):
    rows = dst.shape[0]
    step = 256
    cols = pl.ds(pl.multiple_of(start, 256), dst.shape[1])

    def one(i, carry):
        part = pl.ds(pl.multiple_of(i * step, step), step)
        dst[part, :] = jnp.dot(hidden[part, :], weights[:, cols], preferred_element_type=jnp.float32)
        return carry

    lax.fori_loop(0, rows // step, one, 0)


def add_blocks(dst, *sources):
    rows = dst.shape[0]
    step = 128

    def one(i, carry):
        part = pl.ds(pl.multiple_of(i * step, step), step)
        total = sources[0][part, :].astype(jnp.float32)
        for source in sources[1:]:
            total = total + source[part, :].astype(jnp.float32)
        dst[part, :] = total.astype(dst.dtype)
        return carry

    lax.fori_loop(0, rows // step, one, 0)


def scatter_kernel(width, hidden, weights_hbm, returned, weights, out, mine, theirs, outgoing,
                   sending, landed, weight_sem, sister_send, sister_recv, send_sem, recv_sem,
                   back_send, back_recv):
    row, me, core = lax.axis_index("row"), lax.axis_index("chip"), lax.axis_index("core")
    sister = 1 - core
    side, y = me // 4, me % 4
    partner = lax.rem(me + 4, 8)
    up = side * 4 + lax.rem(y + 1, 4)
    down = side * 4 + lax.rem(y + 3, 4)
    across = side * 4 + lax.rem(y + 2, 4)

    def far(chip):
        return lax.rem(chip + 4, 8)

    rows = returned.shape[0]
    order = (far(down), across, up, far(across), down, far(up), partner, me)
    loads = {}
    for slot, chip in enumerate(order):
        for index, half in enumerate((sister, core)):
            cols = pl.ds(pl.multiple_of((chip * 2 + half) * width, width), width)
            load = pltpu.make_async_copy(weights_hbm.at[:, cols], weights.at[:, cols],
                                         weight_sem.at[index, slot])
            load.start()
            loads[(slot, index)] = load
    barrier = pltpu.get_barrier_semaphore()
    for chip, half in ((partner, core), (up, core), (down, core), (me, sister)):
        pl.semaphore_signal(barrier, inc=1, device_id=(row, chip, half), device_id_type=MESH)
    for d in range(1, rows):
        pl.semaphore_signal(barrier, inc=1, device_id=(lax.rem(row + d, rows), me, core),
                            device_id_type=MESH)
    pl.semaphore_wait(barrier, 4 + rows - 1)

    swaps = []

    def produce(slots, own=True):
        for slot in slots:
            loads[(slot, 0)].wait()
            project(outgoing.at[slot], hidden, weights, (order[slot] * 2 + sister) * width)
            swap = pltpu.make_async_remote_copy(
                src_ref=outgoing.at[slot], dst_ref=theirs.at[slot], send_sem=sister_send.at[slot],
                recv_sem=sister_recv.at[slot], device_id=(row, me, sister), device_id_type=MESH,
            )
            swap.start()
            swaps.append(swap)
        if own:
            for slot in slots:
                own_block(slot)

    def own_block(slot):
        loads[(slot, 1)].wait()
        project(mine.at[slot], hidden, weights, (order[slot] * 2 + core) * width)

    produce(range(4), own=False)

    def ready(slot):
        swaps[slot].wait_recv()
        return (mine.at[slot], theirs.at[slot])

    def send(tag, chip):
        copy = pltpu.make_async_remote_copy(
            src_ref=sending.at[tag], dst_ref=landed.at[tag], send_sem=send_sem.at[tag],
            recv_sem=recv_sem.at[tag], device_id=(row, chip, core), device_id_type=MESH,
        )
        copy.start()
        return copy

    def arrive(tag):
        pltpu.make_async_remote_copy(
            src_ref=sending.at[tag], dst_ref=landed.at[tag], send_sem=send_sem.at[tag],
            recv_sem=recv_sem.at[tag], device_id=(row, me, core), device_id_type=MESH,
        ).wait_recv()

    sent = []
    for tag, chip in ((0, down), (1, down), (2, up), (3, up)):
        own_block(tag)
        add_blocks(sending.at[tag], *ready(tag))
        sent.append(send(tag, chip))
    produce(range(4, 8))
    arrive(1)
    add_blocks(sending.at[4], *ready(4), landed.at[1])
    sent.append(send(4, down))
    arrive(3)
    add_blocks(sending.at[5], *ready(5), landed.at[3])
    sent.append(send(5, up))
    arrive(0)
    arrive(5)
    add_blocks(sending.at[6], *ready(6), landed.at[0], landed.at[5])
    sent.append(send(6, partner))
    arrive(2)
    arrive(4)
    add_blocks(out, *ready(7), landed.at[2], landed.at[4])
    arrive(6)
    add_blocks(out, out, landed.at[6])
    depth = returned.shape[1]
    returned[row] = out[pl.ds(pl.multiple_of(row * depth, depth), depth), :]
    backs = []
    for d in range(1, rows):
        source = lax.rem(row + d, rows)
        back = pltpu.make_async_remote_copy(
            src_ref=out.at[pl.ds(pl.multiple_of(source * depth, depth), depth), :],
            dst_ref=returned.at[row], send_sem=back_send.at[d], recv_sem=back_recv.at[d],
            device_id=(source, me, core), device_id_type=MESH,
        )
        back.start()
        backs.append(back)
    for copy in sent + swaps:
        copy.wait_send()
    for back in backs:
        back.wait()


def scatter_cols(hidden, weights, width, rows):
    slots = hidden.shape[0]
    return pl.pallas_call(
        functools.partial(scatter_kernel, width),
        out_shape=jax.ShapeDtypeStruct((rows, slots // rows, width), jnp.float32),
        in_specs=[pl.BlockSpec(memory_space=pltpu.VMEM), pl.BlockSpec(memory_space=pl.ANY)],
        out_specs=pl.BlockSpec(memory_space=pltpu.VMEM),
        scratch_shapes=[
            pltpu.VMEM(weights.shape, weights.dtype),
            pltpu.VMEM((slots, width), jnp.float32),
            pltpu.VMEM((8, slots, width), jnp.float32),
            pltpu.VMEM((8, slots, width), jnp.float32),
            pltpu.VMEM((8, slots, width), jnp.float32),
            pltpu.VMEM((7, slots, width), jnp.bfloat16),
            pltpu.VMEM((7, slots, width), jnp.bfloat16),
            pltpu.SemaphoreType.DMA((2, 8)),
            pltpu.SemaphoreType.DMA((8,)),
            pltpu.SemaphoreType.DMA((8,)),
            pltpu.SemaphoreType.DMA((7,)),
            pltpu.SemaphoreType.DMA((7,)),
            pltpu.SemaphoreType.DMA((rows,)),
            pltpu.SemaphoreType.DMA((rows,)),
        ],
        compiler_params=pltpu.CompilerParams(
            collective_id=1, has_side_effects=True, vmem_limit_bytes=60 * 1024 * 1024
        ),
    )(hidden, weights)


def body(tokens, norm_gain, expert_ids, gate_weights, w_gate, w_up, w_down):
    chips = lax.psum(1, "chip")
    width = tokens.shape[1]
    core = lax.axis_index("core")

    picker, slot_index = route_tables(expert_ids, EXPERTS, CAP)
    packed = jnp.einsum("ts,td->sd", picker, tokens, preferred_element_type=jnp.float32).astype(
        jnp.bfloat16
    )
    packed = packed.reshape(EXPERTS, CAP, width)
    hidden = expert_in(packed, norm_gain, w_gate[0], w_up[0], chips)
    returned = scatter_cols(hidden, w_down[0], width, EXPERTS)
    mixed = combine_rows(returned.reshape(-1, width), slot_index, gate_weights)
    return (tokens.astype(jnp.float32) + mixed).astype(jnp.bfloat16)


def solution(mesh):
    rows, cols = mesh.devices.shape
    split_mesh = Mesh(mesh.devices.reshape(rows, cols // 2, 2), ("row", "chip", "core"))
    placed = (
        P("row", COL),
        P(),
        P("row", None),
        P("row", None),
        P("row", None, COL),
        P("row", None, COL),
        P("row", COL, None),
    )
    return jax.shard_map(
        body, mesh=split_mesh, in_specs=placed, out_specs=P("row", COL), check_vma=False
    )
```

```python
import functools

import jax
import jax.numpy as jnp
from jax import lax
from jax.experimental import pallas as pl
from jax.experimental.pallas import tpu as pltpu
from jax.sharding import Mesh
from jax.sharding import PartitionSpec as P

EXPERTS = 8
CAP = 128
COL = ("chip", "core")
MESH = pl.DeviceIdType.MESH


def normalize(rows, norm_gain):
    values = rows.astype(jnp.float32)
    inverse_norm = lax.rsqrt(jnp.mean(values * values, axis=-1, keepdims=True) + 1e-05)
    return (values * inverse_norm * norm_gain).astype(jnp.bfloat16)


def route_tables(expert_ids, expert_count, capacity):
    token_count = expert_ids.shape[0]
    flat_ids = expert_ids.reshape(-1)
    expert_range = jnp.arange(expert_count, dtype=jnp.int32)
    expert_hits = (flat_ids[:, None] == expert_range[None, :]).astype(jnp.int32)
    earlier = jnp.cumsum(expert_hits, axis=0) - expert_hits
    ranks = jnp.sum(earlier * expert_hits, axis=1)
    slot_index = (flat_ids * capacity + ranks).reshape(token_count, -1)
    slot_ids = jnp.arange(expert_count * capacity, dtype=jnp.int32)
    matches = (slot_index[:, :, None] == slot_ids[None, None, :]).astype(jnp.float32)
    picker = jnp.sum(matches, axis=1)
    return (picker.astype(jnp.bfloat16), slot_index)


def combine_rows(slot_rows, slot_index, gate_weights):
    picked = slot_rows[slot_index]
    return jnp.sum(picked * gate_weights[:, :, None], axis=1)


def expert_in_kernel(width, packed, gain_in, w_gate_hbm, w_up_hbm, hidden, src, squares_part, xs,
                     w_gate, w_up, gain, acc_gate, acc_up, squares, send_sem, recv_sem, local_sem,
                     weight_sem, square_send, square_recv, come_send, come_recv):
    row, me, core = lax.axis_index("row"), lax.axis_index("chip"), lax.axis_index("core")
    side, y = me // 4, me % 4
    partner = lax.rem(me + 4, 8)
    up = side * 4 + lax.rem(y + 1, 4)
    down = side * 4 + lax.rem(y + 3, 4)
    across = side * 4 + lax.rem(y + 2, 4)
    sister = 1 - core
    slots = xs.shape[0]
    step = 256
    blocks = squares.shape[0]
    mine = me * 2 + core
    chips = (me, partner, down, up, far(down), far(up), across, far(across))
    features = [(chip * 2 + core) * width for chip in chips]
    features += [(chip * 2 + sister) * width for chip in chips]

    loads = []
    for place, start in enumerate(features):
        rows = pl.ds(pl.multiple_of(start, width), width)
        for index, (source, target) in enumerate(((w_gate_hbm, w_gate), (w_up_hbm, w_up))):
            load = pltpu.make_async_copy(source.at[rows, :], target.at[pl.ds(place * width, width), :],
                                         weight_sem.at[index, place])
            load.start()
            loads.append(load)
        gain[:, pl.ds(place * width, width)] = gain_in[:, rows]

    rows, depth = packed.shape[0], packed.shape[1]
    barrier = pltpu.get_barrier_semaphore()
    for d in range(1, blocks):
        other = lax.rem(mine + d, blocks)
        pl.semaphore_signal(barrier, inc=1, device_id=(row, other // 2, other % 2),
                            device_id_type=MESH)
    for d in range(1, rows):
        pl.semaphore_signal(barrier, inc=1, device_id=(lax.rem(row + d, rows), me, core),
                            device_id_type=MESH)
    pl.semaphore_wait(barrier, blocks - 1 + rows - 1)

    def rows_of(r):
        return pl.ds(pl.multiple_of(r * depth, depth), depth)

    comes = []
    for d in range(1, rows):
        target = lax.rem(row + d, rows)
        come = pltpu.make_async_remote_copy(
            src_ref=packed.at[target], dst_ref=src.at[rows_of(row), :],
            send_sem=come_send.at[d], recv_sem=come_recv.at[d],
            device_id=(target, me, core), device_id_type=MESH,
        )
        come.start()
        comes.append(come)
    src[rows_of(row), :] = packed[row]
    for come in comes:
        come.wait_recv()

    def sum_squares(i, carry):
        part = pl.ds(pl.multiple_of(i * step, step), step)
        values = src[part, :].astype(jnp.float32)
        total = jnp.sum(values * values, axis=1, keepdims=True)
        squares_part[pl.ds(i, 1), :] = jnp.transpose(jnp.broadcast_to(total, (step, 128)))[0:1, :]
        return carry

    lax.fori_loop(0, slots // step, sum_squares, 0)

    square_copies = []
    for d in range(1, blocks):
        other = lax.rem(mine + d, blocks)
        copy = pltpu.make_async_remote_copy(
            src_ref=squares_part, dst_ref=squares.at[mine], send_sem=square_send.at[d],
            recv_sem=square_recv.at[d], device_id=(row, other // 2, other % 2),
            device_id_type=MESH,
        )
        copy.start()
        square_copies.append(copy)

    half_rows = slots // 2

    def rows_half(h):
        return pl.ds(h * half_rows, half_rows)

    def place(p, h=None):
        if h is None:
            return xs.at[:, pl.ds(p * width, width)]
        return xs.at[rows_half(h), pl.ds(p * width, width)]

    def send(tag, source, target, chip, half, h):
        origin = src.at[rows_half(h), :] if source is None else place(source, h)
        copy = pltpu.make_async_remote_copy(
            src_ref=origin, dst_ref=place(target, h), send_sem=send_sem.at[tag, h],
            recv_sem=recv_sem.at[tag, h], device_id=(row, chip, half), device_id_type=MESH,
        )
        copy.start()
        return copy

    def arrive(tag, target, h):
        pltpu.make_async_remote_copy(
            src_ref=place(target, h), dst_ref=place(target, h), send_sem=send_sem.at[tag, h],
            recv_sem=recv_sem.at[tag, h], device_id=(row, me, sister), device_id_type=MESH,
        ).wait_recv()

    sent = []
    for h in (0, 1):
        sent += [send(0, None, 1, partner, core, h), send(1, None, 2, up, core, h),
                 send(2, None, 3, down, core, h), send(7, None, 8, me, sister, h)]
    local = pltpu.make_async_copy(src, place(0), local_sem)
    local.start()
    squares[mine] = squares_part[...]
    for copy in square_copies:
        copy.wait_recv()
    total = squares[0]
    for b in range(1, blocks):
        total = total + squares[b]
    squares[0] = lax.rsqrt(total / (blocks * width) + 1e-05)

    for h in (0, 1):
        arrive(0, 1, h)
        sent += [send(3, 1, 4, up, core, h), send(4, 1, 5, down, core, h),
                 send(8, 1, 9, me, sister, h)]
        arrive(1, 2, h)
        sent += [send(5, 2, 6, up, core, h), send(9, 2, 10, me, sister, h)]
        arrive(2, 3, h)
        sent.append(send(10, 3, 11, me, sister, h))
    for load in loads:
        load.wait()
    local.wait()

    def absorb(first_place, first=False):
        cols = pl.ds(first_place * width, 4 * width)
        scale = gain[:, cols]

        def one(i, carry):
            part = pl.ds(pl.multiple_of(i * step, step), step)
            spread = jnp.broadcast_to(squares[0, pl.ds(i, 1), :], (128, step))
            column = jnp.transpose(spread)[:, 0:1]
            values = xs[part, cols].astype(jnp.float32)
            normed = (values * column * scale).astype(jnp.bfloat16)
            gate_part = jnp.dot(normed, w_gate[cols, :], preferred_element_type=jnp.float32)
            up_part = jnp.dot(normed, w_up[cols, :], preferred_element_type=jnp.float32)
            if first:
                acc_gate[part, :] = gate_part
                acc_up[part, :] = up_part
            else:
                acc_gate[part, :] += gate_part
                acc_up[part, :] += up_part
            return carry

        lax.fori_loop(0, slots // step, one, 0)

    absorb(0, first=True)
    for h in (0, 1):
        arrive(3, 4, h)
        sent.append(send(11, 4, 12, me, sister, h))
        arrive(4, 5, h)
        sent += [send(6, 5, 7, down, core, h), send(12, 5, 13, me, sister, h)]
        arrive(5, 6, h)
        sent.append(send(13, 6, 14, me, sister, h))
        arrive(6, 7, h)
        sent.append(send(14, 7, 15, me, sister, h))
    absorb(4)
    for tag in range(7, 11):
        for h in (0, 1):
            arrive(tag, tag + 1, h)
    absorb(8)
    for tag in range(11, 15):
        for h in (0, 1):
            arrive(tag, tag + 1, h)
    absorb(12)

    def finish(i, carry):
        part = pl.ds(pl.multiple_of(i * step, step), step)
        gate_values = acc_gate[part, :]
        silu = gate_values / (1.0 + jnp.exp(-gate_values))
        hidden[part, :] = (silu * acc_up[part, :]).astype(hidden.dtype)
        return carry

    lax.fori_loop(0, slots // step, finish, 0)
    for copy in sent + square_copies + comes:
        copy.wait_send()


def far(chip):
    return lax.rem(chip + 4, 8)


def expert_in(packed, norm_gain, w_gate, w_up, chips):
    rows, depth, width = packed.shape
    slots = rows * depth
    blocks = chips * 2
    features = blocks * width
    hidden_units = w_gate.shape[1]
    return pl.pallas_call(
        functools.partial(expert_in_kernel, width),
        out_shape=jax.ShapeDtypeStruct((slots, hidden_units), jnp.bfloat16),
        in_specs=[pl.BlockSpec(memory_space=pltpu.VMEM)] * 2
        + [pl.BlockSpec(memory_space=pl.ANY)] * 2,
        out_specs=pl.BlockSpec(memory_space=pltpu.VMEM),
        scratch_shapes=[
            pltpu.VMEM((slots, width), packed.dtype),
            pltpu.VMEM((slots // 256, 256), jnp.float32),
            pltpu.VMEM((slots, features), jnp.bfloat16),
            pltpu.VMEM(w_gate.shape, w_gate.dtype),
            pltpu.VMEM(w_up.shape, w_up.dtype),
            pltpu.VMEM((1, features), jnp.float32),
            pltpu.VMEM((slots, hidden_units), jnp.float32),
            pltpu.VMEM((slots, hidden_units), jnp.float32),
            pltpu.VMEM((blocks, slots // 256, 256), jnp.float32),
            pltpu.SemaphoreType.DMA((15, 2)),
            pltpu.SemaphoreType.DMA((15, 2)),
            pltpu.SemaphoreType.DMA(()),
            pltpu.SemaphoreType.DMA((2, blocks)),
            pltpu.SemaphoreType.DMA((blocks,)),
            pltpu.SemaphoreType.DMA((blocks,)),
            pltpu.SemaphoreType.DMA((rows,)),
            pltpu.SemaphoreType.DMA((rows,)),
        ],
        compiler_params=pltpu.CompilerParams(
            collective_id=0, has_side_effects=True, vmem_limit_bytes=60 * 1024 * 1024
        ),
    )(packed, norm_gain.reshape(1, features), w_gate, w_up)


def project(dst, hidden, weights, start):
    rows = dst.shape[0]
    step = 256
    cols = pl.ds(pl.multiple_of(start, 256), dst.shape[1])

    def one(i, carry):
        part = pl.ds(pl.multiple_of(i * step, step), step)
        dst[part, :] = jnp.dot(hidden[part, :], weights[:, cols], preferred_element_type=jnp.float32)
        return carry

    lax.fori_loop(0, rows // step, one, 0)


def add_blocks(dst, *sources):
    rows = dst.shape[0]
    step = 128

    def one(i, carry):
        part = pl.ds(pl.multiple_of(i * step, step), step)
        total = sources[0][part, :].astype(jnp.float32)
        for source in sources[1:]:
            total = total + source[part, :].astype(jnp.float32)
        dst[part, :] = total.astype(dst.dtype)
        return carry

    lax.fori_loop(0, rows // step, one, 0)


def scatter_kernel(width, hidden, weights_hbm, returned, weights, out, mine, theirs, outgoing,
                   sending, landed, weight_sem, sister_send, sister_recv, send_sem, recv_sem,
                   back_send, back_recv):
    row, me, core = lax.axis_index("row"), lax.axis_index("chip"), lax.axis_index("core")
    sister = 1 - core
    side, y = me // 4, me % 4
    partner = lax.rem(me + 4, 8)
    up = side * 4 + lax.rem(y + 1, 4)
    down = side * 4 + lax.rem(y + 3, 4)
    across = side * 4 + lax.rem(y + 2, 4)

    def far(chip):
        return lax.rem(chip + 4, 8)

    rows = returned.shape[0]
    order = (far(down), across, up, far(across), down, far(up), partner, me)
    loads = {}
    for slot, chip in enumerate(order):
        for index, half in enumerate((sister, core)):
            cols = pl.ds(pl.multiple_of((chip * 2 + half) * width, width), width)
            load = pltpu.make_async_copy(weights_hbm.at[:, cols], weights.at[:, cols],
                                         weight_sem.at[index, slot])
            load.start()
            loads[(slot, index)] = load
    barrier = pltpu.get_barrier_semaphore()
    for chip, half in ((partner, core), (up, core), (down, core), (me, sister)):
        pl.semaphore_signal(barrier, inc=1, device_id=(row, chip, half), device_id_type=MESH)
    for d in range(1, rows):
        pl.semaphore_signal(barrier, inc=1, device_id=(lax.rem(row + d, rows), me, core),
                            device_id_type=MESH)
    pl.semaphore_wait(barrier, 4 + rows - 1)

    swaps = []

    def produce(slots, own=True):
        for slot in slots:
            loads[(slot, 0)].wait()
            project(outgoing.at[slot], hidden, weights, (order[slot] * 2 + sister) * width)
            swap = pltpu.make_async_remote_copy(
                src_ref=outgoing.at[slot], dst_ref=theirs.at[slot], send_sem=sister_send.at[slot],
                recv_sem=sister_recv.at[slot], device_id=(row, me, sister), device_id_type=MESH,
            )
            swap.start()
            swaps.append(swap)
        if own:
            for slot in slots:
                own_block(slot)

    def own_block(slot):
        loads[(slot, 1)].wait()
        project(mine.at[slot], hidden, weights, (order[slot] * 2 + core) * width)

    produce(range(4), own=False)

    def ready(slot):
        swaps[slot].wait_recv()
        return (mine.at[slot], theirs.at[slot])

    half_rows = mine.shape[1] // 2

    def cut(ref, h):
        return ref.at[pl.ds(h * half_rows, half_rows), :]

    def send(tag, chip, h):
        copy = pltpu.make_async_remote_copy(
            src_ref=cut(sending.at[tag], h), dst_ref=cut(landed.at[tag], h),
            send_sem=send_sem.at[tag, h], recv_sem=recv_sem.at[tag, h],
            device_id=(row, chip, core), device_id_type=MESH,
        )
        copy.start()
        return copy

    def arrive(tag, h):
        pltpu.make_async_remote_copy(
            src_ref=cut(sending.at[tag], h), dst_ref=cut(landed.at[tag], h),
            send_sem=send_sem.at[tag, h], recv_sem=recv_sem.at[tag, h],
            device_id=(row, me, core), device_id_type=MESH,
        ).wait_recv()

    def combine(dst, h, *sources):
        add_blocks(cut(dst, h), *[cut(source, h) for source in sources])

    sent = []
    for tag, chip in ((0, down), (1, down), (2, up), (3, up)):
        own_block(tag)
        pair = ready(tag)
        for h in (0, 1):
            combine(sending.at[tag], h, *pair)
            sent.append(send(tag, chip, h))
    produce(range(4, 8))
    pairs = [ready(slot) for slot in range(4, 8)]
    for h in (0, 1):
        arrive(1, h)
        combine(sending.at[4], h, *pairs[0], landed.at[1])
        sent.append(send(4, down, h))
        arrive(3, h)
        combine(sending.at[5], h, *pairs[1], landed.at[3])
        sent.append(send(5, up, h))
    for h in (0, 1):
        arrive(0, h)
        arrive(5, h)
        combine(sending.at[6], h, *pairs[2], landed.at[0], landed.at[5])
        sent.append(send(6, partner, h))
    for h in (0, 1):
        arrive(2, h)
        arrive(4, h)
        combine(out, h, *pairs[3], landed.at[2], landed.at[4])
    for h in (0, 1):
        arrive(6, h)
        combine(out, h, out, landed.at[6])
    depth = returned.shape[1]
    returned[row] = out[pl.ds(pl.multiple_of(row * depth, depth), depth), :]
    backs = []
    for d in range(1, rows):
        source = lax.rem(row + d, rows)
        back = pltpu.make_async_remote_copy(
            src_ref=out.at[pl.ds(pl.multiple_of(source * depth, depth), depth), :],
            dst_ref=returned.at[row], send_sem=back_send.at[d], recv_sem=back_recv.at[d],
            device_id=(source, me, core), device_id_type=MESH,
        )
        back.start()
        backs.append(back)
    for copy in sent + swaps:
        copy.wait_send()
    for back in backs:
        back.wait()


def scatter_cols(hidden, weights, width, rows):
    slots = hidden.shape[0]
    return pl.pallas_call(
        functools.partial(scatter_kernel, width),
        out_shape=jax.ShapeDtypeStruct((rows, slots // rows, width), jnp.float32),
        in_specs=[pl.BlockSpec(memory_space=pltpu.VMEM), pl.BlockSpec(memory_space=pl.ANY)],
        out_specs=pl.BlockSpec(memory_space=pltpu.VMEM),
        scratch_shapes=[
            pltpu.VMEM(weights.shape, weights.dtype),
            pltpu.VMEM((slots, width), jnp.float32),
            pltpu.VMEM((8, slots, width), jnp.float32),
            pltpu.VMEM((8, slots, width), jnp.float32),
            pltpu.VMEM((8, slots, width), jnp.float32),
            pltpu.VMEM((7, slots, width), jnp.bfloat16),
            pltpu.VMEM((7, slots, width), jnp.bfloat16),
            pltpu.SemaphoreType.DMA((2, 8)),
            pltpu.SemaphoreType.DMA((8,)),
            pltpu.SemaphoreType.DMA((8,)),
            pltpu.SemaphoreType.DMA((7, 2)),
            pltpu.SemaphoreType.DMA((7, 2)),
            pltpu.SemaphoreType.DMA((rows,)),
            pltpu.SemaphoreType.DMA((rows,)),
        ],
        compiler_params=pltpu.CompilerParams(
            collective_id=1, has_side_effects=True, vmem_limit_bytes=60 * 1024 * 1024
        ),
    )(hidden, weights)


def body(tokens, norm_gain, expert_ids, gate_weights, w_gate, w_up, w_down):
    chips = lax.psum(1, "chip")
    width = tokens.shape[1]
    core = lax.axis_index("core")

    picker, slot_index = route_tables(expert_ids, EXPERTS, CAP)
    packed = jnp.einsum("ts,td->sd", picker, tokens, preferred_element_type=jnp.float32).astype(
        jnp.bfloat16
    )
    packed = packed.reshape(EXPERTS, CAP, width)
    hidden = expert_in(packed, norm_gain, w_gate[0], w_up[0], chips)
    returned = scatter_cols(hidden, w_down[0], width, EXPERTS)
    mixed = combine_rows(returned.reshape(-1, width), slot_index, gate_weights)
    return (tokens.astype(jnp.float32) + mixed).astype(jnp.bfloat16)


def solution(mesh):
    rows, cols = mesh.devices.shape
    split_mesh = Mesh(mesh.devices.reshape(rows, cols // 2, 2), ("row", "chip", "core"))
    placed = (
        P("row", COL),
        P(),
        P("row", None),
        P("row", None),
        P("row", None, COL),
        P("row", None, COL),
        P("row", COL, None),
    )
    return jax.shard_map(
        body, mesh=split_mesh, in_specs=placed, out_specs=P("row", COL), check_vma=False
    )
```

```python
import functools

import jax
import jax.numpy as jnp
from jax import lax
from jax.experimental import pallas as pl
from jax.experimental.pallas import tpu as pltpu
from jax.sharding import Mesh
from jax.sharding import PartitionSpec as P

EXPERTS = 8
CAP = 128
COL = ("chip", "core")
MESH = pl.DeviceIdType.MESH


def normalize(rows, norm_gain):
    values = rows.astype(jnp.float32)
    inverse_norm = lax.rsqrt(jnp.mean(values * values, axis=-1, keepdims=True) + 1e-05)
    return (values * inverse_norm * norm_gain).astype(jnp.bfloat16)


def route_tables(expert_ids, expert_count, capacity):
    token_count = expert_ids.shape[0]
    flat_ids = expert_ids.reshape(-1)
    expert_range = jnp.arange(expert_count, dtype=jnp.int32)
    expert_hits = (flat_ids[:, None] == expert_range[None, :]).astype(jnp.int32)
    earlier = jnp.cumsum(expert_hits, axis=0) - expert_hits
    ranks = jnp.sum(earlier * expert_hits, axis=1)
    slot_index = (flat_ids * capacity + ranks).reshape(token_count, -1)
    slot_ids = jnp.arange(expert_count * capacity, dtype=jnp.int32)
    matches = (slot_index[:, :, None] == slot_ids[None, None, :]).astype(jnp.float32)
    picker = jnp.sum(matches, axis=1)
    return (picker.astype(jnp.bfloat16), slot_index)


def combine_rows(slot_rows, slot_index, gate_weights):
    picked = slot_rows[slot_index]
    return jnp.sum(picked * gate_weights[:, :, None], axis=1)


def expert_in_kernel(width, packed, gain_in, w_gate_hbm, w_up_hbm, hidden, src, squares_part, xs,
                     w_gate, w_up, gain, acc_gate, acc_up, squares, send_sem, recv_sem, local_sem,
                     weight_sem, square_send, square_recv, come_send, come_recv):
    row, me, core = lax.axis_index("row"), lax.axis_index("chip"), lax.axis_index("core")
    side, y = me // 4, me % 4
    partner = lax.rem(me + 4, 8)
    up = side * 4 + lax.rem(y + 1, 4)
    down = side * 4 + lax.rem(y + 3, 4)
    across = side * 4 + lax.rem(y + 2, 4)
    sister = 1 - core
    slots = xs.shape[0]
    step = 256
    blocks = squares.shape[0]
    mine = me * 2 + core
    chips = (me, partner, down, up, far(down), far(up), across, far(across))
    features = [(chip * 2 + core) * width for chip in chips]
    features += [(chip * 2 + sister) * width for chip in chips]

    loads = []
    for place, start in enumerate(features):
        rows = pl.ds(pl.multiple_of(start, width), width)
        for index, (source, target) in enumerate(((w_gate_hbm, w_gate), (w_up_hbm, w_up))):
            load = pltpu.make_async_copy(source.at[rows, :], target.at[pl.ds(place * width, width), :],
                                         weight_sem.at[index, place])
            load.start()
            loads.append(load)
        gain[:, pl.ds(place * width, width)] = gain_in[:, rows]

    rows, depth = packed.shape[0], packed.shape[1]
    barrier = pltpu.get_barrier_semaphore()
    for d in range(1, blocks):
        other = lax.rem(mine + d, blocks)
        pl.semaphore_signal(barrier, inc=1, device_id=(row, other // 2, other % 2),
                            device_id_type=MESH)
    for d in range(1, rows):
        pl.semaphore_signal(barrier, inc=1, device_id=(lax.rem(row + d, rows), me, core),
                            device_id_type=MESH)
    pl.semaphore_wait(barrier, blocks - 1 + rows - 1)

    def rows_of(r):
        return pl.ds(pl.multiple_of(r * depth, depth), depth)

    comes = []
    for d in range(1, rows):
        target = lax.rem(row + d, rows)
        come = pltpu.make_async_remote_copy(
            src_ref=packed.at[target], dst_ref=src.at[rows_of(row), :],
            send_sem=come_send.at[d], recv_sem=come_recv.at[d],
            device_id=(target, me, core), device_id_type=MESH,
        )
        come.start()
        comes.append(come)
    src[rows_of(row), :] = packed[row]
    for come in comes:
        come.wait_recv()

    def sum_squares(i, carry):
        part = pl.ds(pl.multiple_of(i * step, step), step)
        values = src[part, :].astype(jnp.float32)
        total = jnp.sum(values * values, axis=1, keepdims=True)
        squares_part[pl.ds(i, 1), :] = jnp.transpose(jnp.broadcast_to(total, (step, 128)))[0:1, :]
        return carry

    lax.fori_loop(0, slots // step, sum_squares, 0)

    square_copies = []
    for d in range(1, blocks):
        other = lax.rem(mine + d, blocks)
        copy = pltpu.make_async_remote_copy(
            src_ref=squares_part, dst_ref=squares.at[mine], send_sem=square_send.at[d],
            recv_sem=square_recv.at[d], device_id=(row, other // 2, other % 2),
            device_id_type=MESH,
        )
        copy.start()
        square_copies.append(copy)

    half_rows = slots // 2

    def rows_half(h):
        return pl.ds(h * half_rows, half_rows)

    def place(p, h=None):
        if h is None:
            return xs.at[:, pl.ds(p * width, width)]
        return xs.at[rows_half(h), pl.ds(p * width, width)]

    def send(tag, source, target, chip, half, h):
        origin = src.at[rows_half(h), :] if source is None else place(source, h)
        copy = pltpu.make_async_remote_copy(
            src_ref=origin, dst_ref=place(target, h), send_sem=send_sem.at[tag, h],
            recv_sem=recv_sem.at[tag, h], device_id=(row, chip, half), device_id_type=MESH,
        )
        copy.start()
        return copy

    def arrive(tag, target, h):
        pltpu.make_async_remote_copy(
            src_ref=place(target, h), dst_ref=place(target, h), send_sem=send_sem.at[tag, h],
            recv_sem=recv_sem.at[tag, h], device_id=(row, me, sister), device_id_type=MESH,
        ).wait_recv()

    sent = []
    for h in (0, 1):
        sent += [send(0, None, 1, partner, core, h), send(1, None, 2, up, core, h),
                 send(2, None, 3, down, core, h), send(7, None, 8, me, sister, h)]
    local = pltpu.make_async_copy(src, place(0), local_sem)
    local.start()
    squares[mine] = squares_part[...]
    for copy in square_copies:
        copy.wait_recv()
    total = squares[0]
    for b in range(1, blocks):
        total = total + squares[b]
    squares[0] = lax.rsqrt(total / (blocks * width) + 1e-05)

    for h in (0, 1):
        arrive(0, 1, h)
        sent += [send(3, 1, 4, up, core, h), send(4, 1, 5, down, core, h),
                 send(8, 1, 9, me, sister, h)]
        arrive(1, 2, h)
        sent += [send(5, 2, 6, up, core, h), send(9, 2, 10, me, sister, h)]
        arrive(2, 3, h)
        sent.append(send(10, 3, 11, me, sister, h))
    for load in loads:
        load.wait()
    local.wait()

    def absorb(first_place, first=False, rows_part=None):
        cols = pl.ds(first_place * width, 4 * width)
        scale = gain[:, cols]

        def one(i, carry):
            part = pl.ds(pl.multiple_of(i * step, step), step)
            spread = jnp.broadcast_to(squares[0, pl.ds(i, 1), :], (128, step))
            column = jnp.transpose(spread)[:, 0:1]
            values = xs[part, cols].astype(jnp.float32)
            normed = (values * column * scale).astype(jnp.bfloat16)
            gate_part = jnp.dot(normed, w_gate[cols, :], preferred_element_type=jnp.float32)
            up_part = jnp.dot(normed, w_up[cols, :], preferred_element_type=jnp.float32)
            if first:
                acc_gate[part, :] = gate_part
                acc_up[part, :] = up_part
            else:
                acc_gate[part, :] += gate_part
                acc_up[part, :] += up_part
            return carry

        chunks = slots // step
        if rows_part is None:
            lax.fori_loop(0, chunks, one, 0)
        else:
            lax.fori_loop(rows_part * chunks // 2, (rows_part + 1) * chunks // 2, one, 0)

    absorb(0, first=True)
    for h in (0, 1):
        arrive(3, 4, h)
        sent.append(send(11, 4, 12, me, sister, h))
        arrive(4, 5, h)
        sent += [send(6, 5, 7, down, core, h), send(12, 5, 13, me, sister, h)]
        arrive(5, 6, h)
        sent.append(send(13, 6, 14, me, sister, h))
        arrive(6, 7, h)
        sent.append(send(14, 7, 15, me, sister, h))
    absorb(4)
    for first_place in (8, 12):
        for h in (0, 1):
            for tag in range(first_place - 1, first_place + 3):
                arrive(tag, tag + 1, h)
            absorb(first_place, rows_part=h)

    def finish(i, carry):
        part = pl.ds(pl.multiple_of(i * step, step), step)
        gate_values = acc_gate[part, :]
        silu = gate_values / (1.0 + jnp.exp(-gate_values))
        hidden[part, :] = (silu * acc_up[part, :]).astype(hidden.dtype)
        return carry

    lax.fori_loop(0, slots // step, finish, 0)
    for copy in sent + square_copies + comes:
        copy.wait_send()


def far(chip):
    return lax.rem(chip + 4, 8)


def expert_in(packed, norm_gain, w_gate, w_up, chips):
    rows, depth, width = packed.shape
    slots = rows * depth
    blocks = chips * 2
    features = blocks * width
    hidden_units = w_gate.shape[1]
    return pl.pallas_call(
        functools.partial(expert_in_kernel, width),
        out_shape=jax.ShapeDtypeStruct((slots, hidden_units), jnp.bfloat16),
        in_specs=[pl.BlockSpec(memory_space=pltpu.VMEM)] * 2
        + [pl.BlockSpec(memory_space=pl.ANY)] * 2,
        out_specs=pl.BlockSpec(memory_space=pltpu.VMEM),
        scratch_shapes=[
            pltpu.VMEM((slots, width), packed.dtype),
            pltpu.VMEM((slots // 256, 256), jnp.float32),
            pltpu.VMEM((slots, features), jnp.bfloat16),
            pltpu.VMEM(w_gate.shape, w_gate.dtype),
            pltpu.VMEM(w_up.shape, w_up.dtype),
            pltpu.VMEM((1, features), jnp.float32),
            pltpu.VMEM((slots, hidden_units), jnp.float32),
            pltpu.VMEM((slots, hidden_units), jnp.float32),
            pltpu.VMEM((blocks, slots // 256, 256), jnp.float32),
            pltpu.SemaphoreType.DMA((15, 2)),
            pltpu.SemaphoreType.DMA((15, 2)),
            pltpu.SemaphoreType.DMA(()),
            pltpu.SemaphoreType.DMA((2, blocks)),
            pltpu.SemaphoreType.DMA((blocks,)),
            pltpu.SemaphoreType.DMA((blocks,)),
            pltpu.SemaphoreType.DMA((rows,)),
            pltpu.SemaphoreType.DMA((rows,)),
        ],
        compiler_params=pltpu.CompilerParams(
            collective_id=0, has_side_effects=True, vmem_limit_bytes=60 * 1024 * 1024
        ),
    )(packed, norm_gain.reshape(1, features), w_gate, w_up)


def project(dst, hidden, weights, start):
    rows = dst.shape[0]
    step = 256
    cols = pl.ds(pl.multiple_of(start, 256), dst.shape[1])

    def one(i, carry):
        part = pl.ds(pl.multiple_of(i * step, step), step)
        dst[part, :] = jnp.dot(hidden[part, :], weights[:, cols], preferred_element_type=jnp.float32)
        return carry

    lax.fori_loop(0, rows // step, one, 0)


def add_blocks(dst, *sources):
    rows = dst.shape[0]
    step = 128

    def one(i, carry):
        part = pl.ds(pl.multiple_of(i * step, step), step)
        total = sources[0][part, :].astype(jnp.float32)
        for source in sources[1:]:
            total = total + source[part, :].astype(jnp.float32)
        dst[part, :] = total.astype(dst.dtype)
        return carry

    lax.fori_loop(0, rows // step, one, 0)


def scatter_kernel(width, hidden, weights_hbm, returned, weights, out, mine, theirs, outgoing,
                   sending, landed, weight_sem, sister_send, sister_recv, send_sem, recv_sem,
                   back_send, back_recv):
    row, me, core = lax.axis_index("row"), lax.axis_index("chip"), lax.axis_index("core")
    sister = 1 - core
    side, y = me // 4, me % 4
    partner = lax.rem(me + 4, 8)
    up = side * 4 + lax.rem(y + 1, 4)
    down = side * 4 + lax.rem(y + 3, 4)
    across = side * 4 + lax.rem(y + 2, 4)

    def far(chip):
        return lax.rem(chip + 4, 8)

    rows = returned.shape[0]
    order = (far(down), across, up, far(across), down, far(up), partner, me)
    loads = {}
    for slot, chip in enumerate(order):
        for index, half in enumerate((sister, core)):
            cols = pl.ds(pl.multiple_of((chip * 2 + half) * width, width), width)
            load = pltpu.make_async_copy(weights_hbm.at[:, cols], weights.at[:, cols],
                                         weight_sem.at[index, slot])
            load.start()
            loads[(slot, index)] = load
    barrier = pltpu.get_barrier_semaphore()
    for chip, half in ((partner, core), (up, core), (down, core), (me, sister)):
        pl.semaphore_signal(barrier, inc=1, device_id=(row, chip, half), device_id_type=MESH)
    for d in range(1, rows):
        pl.semaphore_signal(barrier, inc=1, device_id=(lax.rem(row + d, rows), me, core),
                            device_id_type=MESH)
    pl.semaphore_wait(barrier, 4 + rows - 1)

    swaps = []

    def produce(slots, own=True):
        for slot in slots:
            loads[(slot, 0)].wait()
            project(outgoing.at[slot], hidden, weights, (order[slot] * 2 + sister) * width)
            swap = pltpu.make_async_remote_copy(
                src_ref=outgoing.at[slot], dst_ref=theirs.at[slot], send_sem=sister_send.at[slot],
                recv_sem=sister_recv.at[slot], device_id=(row, me, sister), device_id_type=MESH,
            )
            swap.start()
            swaps.append(swap)
        if own:
            for slot in slots:
                own_block(slot)

    def own_block(slot):
        loads[(slot, 1)].wait()
        project(mine.at[slot], hidden, weights, (order[slot] * 2 + core) * width)

    produce(range(4), own=False)

    def ready(slot):
        swaps[slot].wait_recv()
        return (mine.at[slot], theirs.at[slot])

    half_rows = mine.shape[1] // 2

    def cut(ref, h):
        return ref.at[pl.ds(h * half_rows, half_rows), :]

    def send(tag, chip, h):
        copy = pltpu.make_async_remote_copy(
            src_ref=cut(sending.at[tag], h), dst_ref=cut(landed.at[tag], h),
            send_sem=send_sem.at[tag, h], recv_sem=recv_sem.at[tag, h],
            device_id=(row, chip, core), device_id_type=MESH,
        )
        copy.start()
        return copy

    def arrive(tag, h):
        pltpu.make_async_remote_copy(
            src_ref=cut(sending.at[tag], h), dst_ref=cut(landed.at[tag], h),
            send_sem=send_sem.at[tag, h], recv_sem=recv_sem.at[tag, h],
            device_id=(row, me, core), device_id_type=MESH,
        ).wait_recv()

    def combine(dst, h, *sources):
        add_blocks(cut(dst, h), *[cut(source, h) for source in sources])

    sent = []
    for tag, chip in ((0, down), (1, down), (2, up), (3, up)):
        own_block(tag)
        pair = ready(tag)
        for h in (0, 1):
            combine(sending.at[tag], h, *pair)
            sent.append(send(tag, chip, h))
    produce(range(4, 8))
    pairs = [ready(slot) for slot in range(4, 8)]
    for h in (0, 1):
        arrive(1, h)
        combine(sending.at[4], h, *pairs[0], landed.at[1])
        sent.append(send(4, down, h))
        arrive(3, h)
        combine(sending.at[5], h, *pairs[1], landed.at[3])
        sent.append(send(5, up, h))
    for h in (0, 1):
        arrive(0, h)
        arrive(5, h)
        combine(sending.at[6], h, *pairs[2], landed.at[0], landed.at[5])
        sent.append(send(6, partner, h))
    for h in (0, 1):
        arrive(2, h)
        arrive(4, h)
        combine(out, h, *pairs[3], landed.at[2], landed.at[4])
    for h in (0, 1):
        arrive(6, h)
        combine(out, h, out, landed.at[6])
    depth = returned.shape[1]
    returned[row] = out[pl.ds(pl.multiple_of(row * depth, depth), depth), :]
    backs = []
    for d in range(1, rows):
        source = lax.rem(row + d, rows)
        back = pltpu.make_async_remote_copy(
            src_ref=out.at[pl.ds(pl.multiple_of(source * depth, depth), depth), :],
            dst_ref=returned.at[row], send_sem=back_send.at[d], recv_sem=back_recv.at[d],
            device_id=(source, me, core), device_id_type=MESH,
        )
        back.start()
        backs.append(back)
    for copy in sent + swaps:
        copy.wait_send()
    for back in backs:
        back.wait()


def scatter_cols(hidden, weights, width, rows):
    slots = hidden.shape[0]
    return pl.pallas_call(
        functools.partial(scatter_kernel, width),
        out_shape=jax.ShapeDtypeStruct((rows, slots // rows, width), jnp.float32),
        in_specs=[pl.BlockSpec(memory_space=pltpu.VMEM), pl.BlockSpec(memory_space=pl.ANY)],
        out_specs=pl.BlockSpec(memory_space=pltpu.VMEM),
        scratch_shapes=[
            pltpu.VMEM(weights.shape, weights.dtype),
            pltpu.VMEM((slots, width), jnp.float32),
            pltpu.VMEM((8, slots, width), jnp.float32),
            pltpu.VMEM((8, slots, width), jnp.float32),
            pltpu.VMEM((8, slots, width), jnp.float32),
            pltpu.VMEM((7, slots, width), jnp.bfloat16),
            pltpu.VMEM((7, slots, width), jnp.bfloat16),
            pltpu.SemaphoreType.DMA((2, 8)),
            pltpu.SemaphoreType.DMA((8,)),
            pltpu.SemaphoreType.DMA((8,)),
            pltpu.SemaphoreType.DMA((7, 2)),
            pltpu.SemaphoreType.DMA((7, 2)),
            pltpu.SemaphoreType.DMA((rows,)),
            pltpu.SemaphoreType.DMA((rows,)),
        ],
        compiler_params=pltpu.CompilerParams(
            collective_id=1, has_side_effects=True, vmem_limit_bytes=60 * 1024 * 1024
        ),
    )(hidden, weights)


def body(tokens, norm_gain, expert_ids, gate_weights, w_gate, w_up, w_down):
    chips = lax.psum(1, "chip")
    width = tokens.shape[1]
    core = lax.axis_index("core")

    picker, slot_index = route_tables(expert_ids, EXPERTS, CAP)
    packed = jnp.einsum("ts,td->sd", picker, tokens, preferred_element_type=jnp.float32).astype(
        jnp.bfloat16
    )
    packed = packed.reshape(EXPERTS, CAP, width)
    hidden = expert_in(packed, norm_gain, w_gate[0], w_up[0], chips)
    returned = scatter_cols(hidden, w_down[0], width, EXPERTS)
    mixed = combine_rows(returned.reshape(-1, width), slot_index, gate_weights)
    return (tokens.astype(jnp.float32) + mixed).astype(jnp.bfloat16)


def solution(mesh):
    rows, cols = mesh.devices.shape
    split_mesh = Mesh(mesh.devices.reshape(rows, cols // 2, 2), ("row", "chip", "core"))
    placed = (
        P("row", COL),
        P(),
        P("row", None),
        P("row", None),
        P("row", None, COL),
        P("row", None, COL),
        P("row", COL, None),
    )
    return jax.shard_map(
        body, mesh=split_mesh, in_specs=placed, out_specs=P("row", COL), check_vma=False
    )
```

```python
import functools

import jax
import jax.numpy as jnp
from jax import lax
from jax.experimental import pallas as pl
from jax.experimental.pallas import tpu as pltpu
from jax.sharding import Mesh
from jax.sharding import PartitionSpec as P

EXPERTS = 8
CAP = 128
COL = ("chip", "core")
MESH = pl.DeviceIdType.MESH


def normalize(rows, norm_gain):
    values = rows.astype(jnp.float32)
    inverse_norm = lax.rsqrt(jnp.mean(values * values, axis=-1, keepdims=True) + 1e-05)
    return (values * inverse_norm * norm_gain).astype(jnp.bfloat16)


def route_tables(expert_ids, expert_count, capacity):
    token_count = expert_ids.shape[0]
    flat_ids = expert_ids.reshape(-1)
    expert_range = jnp.arange(expert_count, dtype=jnp.int32)
    expert_hits = (flat_ids[:, None] == expert_range[None, :]).astype(jnp.int32)
    earlier = jnp.cumsum(expert_hits, axis=0) - expert_hits
    ranks = jnp.sum(earlier * expert_hits, axis=1)
    slot_index = (flat_ids * capacity + ranks).reshape(token_count, -1)
    slot_ids = jnp.arange(expert_count * capacity, dtype=jnp.int32)
    matches = (slot_index[:, :, None] == slot_ids[None, None, :]).astype(jnp.float32)
    picker = jnp.sum(matches, axis=1)
    return (picker.astype(jnp.bfloat16), slot_index)


def combine_rows(slot_rows, slot_index, gate_weights):
    picked = slot_rows[slot_index]
    return jnp.sum(picked * gate_weights[:, :, None], axis=1)


def expert_in_kernel(width, packed, gain_in, w_gate_hbm, w_up_hbm, hidden, src, squares_part, xs,
                     w_gate, w_up, gain, acc_gate, acc_up, squares, send_sem, recv_sem, local_sem,
                     weight_sem, square_send, square_recv, come_send, come_recv):
    row, me, core = lax.axis_index("row"), lax.axis_index("chip"), lax.axis_index("core")
    side, y = me // 4, me % 4
    partner = lax.rem(me + 4, 8)
    up = side * 4 + lax.rem(y + 1, 4)
    down = side * 4 + lax.rem(y + 3, 4)
    across = side * 4 + lax.rem(y + 2, 4)
    sister = 1 - core
    slots = xs.shape[0]
    step = 256
    blocks = squares.shape[0]
    mine = me * 2 + core
    chips = (me, partner, down, up, far(down), far(up), across, far(across))
    features = [(chip * 2 + core) * width for chip in chips]
    features += [(chip * 2 + sister) * width for chip in chips]

    loads = []
    for place, start in enumerate(features):
        rows = pl.ds(pl.multiple_of(start, width), width)
        for index, (source, target) in enumerate(((w_gate_hbm, w_gate), (w_up_hbm, w_up))):
            load = pltpu.make_async_copy(source.at[rows, :], target.at[pl.ds(place * width, width), :],
                                         weight_sem.at[index, place])
            load.start()
            loads.append(load)
        gain[:, pl.ds(place * width, width)] = gain_in[:, rows]

    rows, depth = packed.shape[0], packed.shape[1]
    barrier = pltpu.get_barrier_semaphore()
    for d in range(1, blocks):
        other = lax.rem(mine + d, blocks)
        pl.semaphore_signal(barrier, inc=1, device_id=(row, other // 2, other % 2),
                            device_id_type=MESH)
    for d in range(1, rows):
        pl.semaphore_signal(barrier, inc=1, device_id=(lax.rem(row + d, rows), me, core),
                            device_id_type=MESH)
    pl.semaphore_wait(barrier, blocks - 1 + rows - 1)

    def rows_of(r):
        return pl.ds(pl.multiple_of(r * depth, depth), depth)

    comes = []
    for d in range(1, rows):
        target = lax.rem(row + d, rows)
        come = pltpu.make_async_remote_copy(
            src_ref=packed.at[target], dst_ref=src.at[rows_of(row), :],
            send_sem=come_send.at[d], recv_sem=come_recv.at[d],
            device_id=(target, me, core), device_id_type=MESH,
        )
        come.start()
        comes.append(come)
    src[rows_of(row), :] = packed[row]
    for come in comes:
        come.wait_recv()

    def sum_squares(i, carry):
        part = pl.ds(pl.multiple_of(i * step, step), step)
        values = src[part, :].astype(jnp.float32)
        total = jnp.sum(values * values, axis=1, keepdims=True)
        squares_part[pl.ds(i, 1), :] = jnp.transpose(jnp.broadcast_to(total, (step, 128)))[0:1, :]
        return carry

    lax.fori_loop(0, slots // step, sum_squares, 0)

    square_copies = []
    for d in range(1, blocks):
        other = lax.rem(mine + d, blocks)
        copy = pltpu.make_async_remote_copy(
            src_ref=squares_part, dst_ref=squares.at[mine], send_sem=square_send.at[d],
            recv_sem=square_recv.at[d], device_id=(row, other // 2, other % 2),
            device_id_type=MESH,
        )
        copy.start()
        square_copies.append(copy)

    half_rows = slots // 2

    def rows_half(h):
        return pl.ds(h * half_rows, half_rows)

    def place(p, h=None):
        if h is None:
            return xs.at[:, pl.ds(p * width, width)]
        return xs.at[rows_half(h), pl.ds(p * width, width)]

    def send(tag, source, target, chip, half, h):
        origin = src.at[rows_half(h), :] if source is None else place(source, h)
        copy = pltpu.make_async_remote_copy(
            src_ref=origin, dst_ref=place(target, h), send_sem=send_sem.at[tag, h],
            recv_sem=recv_sem.at[tag, h], device_id=(row, chip, half), device_id_type=MESH,
        )
        copy.start()
        return copy

    def arrive(tag, target, h):
        pltpu.make_async_remote_copy(
            src_ref=place(target, h), dst_ref=place(target, h), send_sem=send_sem.at[tag, h],
            recv_sem=recv_sem.at[tag, h], device_id=(row, me, sister), device_id_type=MESH,
        ).wait_recv()

    sent = []
    for h in (0, 1):
        sent += [send(0, None, 1, partner, core, h), send(1, None, 2, up, core, h),
                 send(2, None, 3, down, core, h), send(7, None, 8, me, sister, h)]
    local = pltpu.make_async_copy(src, place(0), local_sem)
    local.start()
    squares[mine] = squares_part[...]
    for copy in square_copies:
        copy.wait_recv()
    total = squares[0]
    for b in range(1, blocks):
        total = total + squares[b]
    squares[0] = lax.rsqrt(total / (blocks * width) + 1e-05)

    for h in (0, 1):
        arrive(0, 1, h)
        sent += [send(3, 1, 4, up, core, h), send(4, 1, 5, down, core, h),
                 send(8, 1, 9, me, sister, h)]
        arrive(1, 2, h)
        sent += [send(5, 2, 6, up, core, h), send(9, 2, 10, me, sister, h)]
        arrive(2, 3, h)
        sent.append(send(10, 3, 11, me, sister, h))
    for load in loads:
        load.wait()
    local.wait()

    def absorb(first_place, first=False, rows_part=None):
        cols = pl.ds(first_place * width, 4 * width)
        scale = gain[:, cols]

        def one(i, carry):
            part = pl.ds(pl.multiple_of(i * step, step), step)
            spread = jnp.broadcast_to(squares[0, pl.ds(i, 1), :], (128, step))
            column = jnp.transpose(spread)[:, 0:1]
            values = xs[part, cols].astype(jnp.float32)
            normed = (values * column * scale).astype(jnp.bfloat16)
            gate_part = jnp.dot(normed, w_gate[cols, :], preferred_element_type=jnp.float32)
            up_part = jnp.dot(normed, w_up[cols, :], preferred_element_type=jnp.float32)
            if first:
                acc_gate[part, :] = gate_part
                acc_up[part, :] = up_part
            else:
                acc_gate[part, :] += gate_part
                acc_up[part, :] += up_part
            return carry

        chunks = slots // step
        if rows_part is None:
            lax.fori_loop(0, chunks, one, 0)
        else:
            lax.fori_loop(rows_part * chunks // 2, (rows_part + 1) * chunks // 2, one, 0)

    absorb(0, first=True)
    for h in (0, 1):
        arrive(3, 4, h)
        sent.append(send(11, 4, 12, me, sister, h))
        arrive(4, 5, h)
        sent += [send(6, 5, 7, down, core, h), send(12, 5, 13, me, sister, h)]
        arrive(5, 6, h)
        sent.append(send(13, 6, 14, me, sister, h))
        arrive(6, 7, h)
        sent.append(send(14, 7, 15, me, sister, h))
    absorb(4)
    for first_place in (8, 12):
        for h in (0, 1):
            for tag in range(first_place - 1, first_place + 3):
                arrive(tag, tag + 1, h)
            absorb(first_place, rows_part=h)

    def finish(i, carry):
        part = pl.ds(pl.multiple_of(i * step, step), step)
        gate_values = acc_gate[part, :]
        silu = gate_values / (1.0 + jnp.exp(-gate_values))
        hidden[part, :] = (silu * acc_up[part, :]).astype(hidden.dtype)
        return carry

    lax.fori_loop(0, slots // step, finish, 0)
    for copy in sent + square_copies + comes:
        copy.wait_send()


def far(chip):
    return lax.rem(chip + 4, 8)


def expert_in(packed, norm_gain, w_gate, w_up, chips):
    rows, depth, width = packed.shape
    slots = rows * depth
    blocks = chips * 2
    features = blocks * width
    hidden_units = w_gate.shape[1]
    return pl.pallas_call(
        functools.partial(expert_in_kernel, width),
        out_shape=jax.ShapeDtypeStruct((slots, hidden_units), jnp.bfloat16),
        in_specs=[pl.BlockSpec(memory_space=pltpu.VMEM)] * 2
        + [pl.BlockSpec(memory_space=pl.ANY)] * 2,
        out_specs=pl.BlockSpec(memory_space=pltpu.VMEM),
        scratch_shapes=[
            pltpu.VMEM((slots, width), packed.dtype),
            pltpu.VMEM((slots // 256, 256), jnp.float32),
            pltpu.VMEM((slots, features), jnp.bfloat16),
            pltpu.VMEM(w_gate.shape, w_gate.dtype),
            pltpu.VMEM(w_up.shape, w_up.dtype),
            pltpu.VMEM((1, features), jnp.float32),
            pltpu.VMEM((slots, hidden_units), jnp.float32),
            pltpu.VMEM((slots, hidden_units), jnp.float32),
            pltpu.VMEM((blocks, slots // 256, 256), jnp.float32),
            pltpu.SemaphoreType.DMA((15, 2)),
            pltpu.SemaphoreType.DMA((15, 2)),
            pltpu.SemaphoreType.DMA(()),
            pltpu.SemaphoreType.DMA((2, blocks)),
            pltpu.SemaphoreType.DMA((blocks,)),
            pltpu.SemaphoreType.DMA((blocks,)),
            pltpu.SemaphoreType.DMA((rows,)),
            pltpu.SemaphoreType.DMA((rows,)),
        ],
        compiler_params=pltpu.CompilerParams(
            collective_id=0, has_side_effects=True, vmem_limit_bytes=60 * 1024 * 1024
        ),
    )(packed, norm_gain.reshape(1, features), w_gate, w_up)


def project(dst, hidden, weights, start):
    rows = dst.shape[0]
    step = 256
    cols = pl.ds(pl.multiple_of(start, 256), dst.shape[1])

    def one(i, carry):
        part = pl.ds(pl.multiple_of(i * step, step), step)
        dst[part, :] = jnp.dot(hidden[part, :], weights[:, cols], preferred_element_type=jnp.float32)
        return carry

    lax.fori_loop(0, rows // step, one, 0)


def add_blocks(dst, *sources):
    rows = dst.shape[0]
    step = 128

    def one(i, carry):
        part = pl.ds(pl.multiple_of(i * step, step), step)
        total = sources[0][part, :].astype(jnp.float32)
        for source in sources[1:]:
            total = total + source[part, :].astype(jnp.float32)
        dst[part, :] = total.astype(dst.dtype)
        return carry

    lax.fori_loop(0, rows // step, one, 0)


def scatter_kernel(width, hidden, weights_hbm, returned, weights, out, mine, theirs, outgoing,
                   sending, landed, weight_sem, sister_send, sister_recv, send_sem, recv_sem,
                   back_send, back_recv):
    row, me, core = lax.axis_index("row"), lax.axis_index("chip"), lax.axis_index("core")
    sister = 1 - core
    side, y = me // 4, me % 4
    partner = lax.rem(me + 4, 8)
    up = side * 4 + lax.rem(y + 1, 4)
    down = side * 4 + lax.rem(y + 3, 4)
    across = side * 4 + lax.rem(y + 2, 4)

    def far(chip):
        return lax.rem(chip + 4, 8)

    rows = returned.shape[0]
    order = (far(down), across, up, far(across), down, far(up), partner, me)
    loads = {}
    for slot, chip in enumerate(order):
        for index, half in enumerate((sister, core)):
            cols = pl.ds(pl.multiple_of((chip * 2 + half) * width, width), width)
            load = pltpu.make_async_copy(weights_hbm.at[:, cols], weights.at[:, cols],
                                         weight_sem.at[index, slot])
            load.start()
            loads[(slot, index)] = load
    barrier = pltpu.get_barrier_semaphore()
    for chip, half in ((partner, core), (up, core), (down, core), (me, sister)):
        pl.semaphore_signal(barrier, inc=1, device_id=(row, chip, half), device_id_type=MESH)
    for d in range(1, rows):
        pl.semaphore_signal(barrier, inc=1, device_id=(lax.rem(row + d, rows), me, core),
                            device_id_type=MESH)
    pl.semaphore_wait(barrier, 4 + rows - 1)

    swaps = {}

    def produce(slots, own=True):
        for slot in slots:
            loads[(slot, 0)].wait()
            project(outgoing.at[slot], hidden, weights, (order[slot] * 2 + sister) * width)
            for h in (0, 1):
                rows_h = pl.ds(h * (hidden.shape[0] // 2), hidden.shape[0] // 2)
                swap = pltpu.make_async_remote_copy(
                    src_ref=outgoing.at[slot, rows_h, :], dst_ref=theirs.at[slot, rows_h, :],
                    send_sem=sister_send.at[slot, h], recv_sem=sister_recv.at[slot, h],
                    device_id=(row, me, sister), device_id_type=MESH,
                )
                swap.start()
                swaps[(slot, h)] = swap
        if own:
            for slot in slots:
                own_block(slot)

    def own_block(slot):
        loads[(slot, 1)].wait()
        project(mine.at[slot], hidden, weights, (order[slot] * 2 + core) * width)

    produce(range(4), own=False)

    def ready(slot, h):
        swaps[(slot, h)].wait_recv()
        return (mine.at[slot], theirs.at[slot])

    half_rows = mine.shape[1] // 2

    def cut(ref, h):
        return ref.at[pl.ds(h * half_rows, half_rows), :]

    def send(tag, chip, h):
        copy = pltpu.make_async_remote_copy(
            src_ref=cut(sending.at[tag], h), dst_ref=cut(landed.at[tag], h),
            send_sem=send_sem.at[tag, h], recv_sem=recv_sem.at[tag, h],
            device_id=(row, chip, core), device_id_type=MESH,
        )
        copy.start()
        return copy

    def arrive(tag, h):
        pltpu.make_async_remote_copy(
            src_ref=cut(sending.at[tag], h), dst_ref=cut(landed.at[tag], h),
            send_sem=send_sem.at[tag, h], recv_sem=recv_sem.at[tag, h],
            device_id=(row, me, core), device_id_type=MESH,
        ).wait_recv()

    def combine(dst, h, *sources):
        add_blocks(cut(dst, h), *[cut(source, h) for source in sources])

    sent = []
    for tag, chip in ((0, down), (1, down), (2, up), (3, up)):
        own_block(tag)
        for h in (0, 1):
            combine(sending.at[tag], h, *ready(tag, h))
            sent.append(send(tag, chip, h))
    produce(range(4, 8))
    for h in (0, 1):
        arrive(1, h)
        combine(sending.at[4], h, *ready(4, h), landed.at[1])
        sent.append(send(4, down, h))
        arrive(3, h)
        combine(sending.at[5], h, *ready(5, h), landed.at[3])
        sent.append(send(5, up, h))
    for h in (0, 1):
        arrive(0, h)
        arrive(5, h)
        combine(sending.at[6], h, *ready(6, h), landed.at[0], landed.at[5])
        sent.append(send(6, partner, h))
    for h in (0, 1):
        arrive(2, h)
        arrive(4, h)
        combine(out, h, *ready(7, h), landed.at[2], landed.at[4])
    for h in (0, 1):
        arrive(6, h)
        combine(out, h, out, landed.at[6])
    depth = returned.shape[1]
    returned[row] = out[pl.ds(pl.multiple_of(row * depth, depth), depth), :]
    backs = []
    for d in range(1, rows):
        source = lax.rem(row + d, rows)
        back = pltpu.make_async_remote_copy(
            src_ref=out.at[pl.ds(pl.multiple_of(source * depth, depth), depth), :],
            dst_ref=returned.at[row], send_sem=back_send.at[d], recv_sem=back_recv.at[d],
            device_id=(source, me, core), device_id_type=MESH,
        )
        back.start()
        backs.append(back)
    for copy in sent + list(swaps.values()):
        copy.wait_send()
    for back in backs:
        back.wait()


def scatter_cols(hidden, weights, width, rows):
    slots = hidden.shape[0]
    return pl.pallas_call(
        functools.partial(scatter_kernel, width),
        out_shape=jax.ShapeDtypeStruct((rows, slots // rows, width), jnp.float32),
        in_specs=[pl.BlockSpec(memory_space=pltpu.VMEM), pl.BlockSpec(memory_space=pl.ANY)],
        out_specs=pl.BlockSpec(memory_space=pltpu.VMEM),
        scratch_shapes=[
            pltpu.VMEM(weights.shape, weights.dtype),
            pltpu.VMEM((slots, width), jnp.float32),
            pltpu.VMEM((8, slots, width), jnp.float32),
            pltpu.VMEM((8, slots, width), jnp.float32),
            pltpu.VMEM((8, slots, width), jnp.float32),
            pltpu.VMEM((7, slots, width), jnp.bfloat16),
            pltpu.VMEM((7, slots, width), jnp.bfloat16),
            pltpu.SemaphoreType.DMA((2, 8)),
            pltpu.SemaphoreType.DMA((8, 2)),
            pltpu.SemaphoreType.DMA((8, 2)),
            pltpu.SemaphoreType.DMA((7, 2)),
            pltpu.SemaphoreType.DMA((7, 2)),
            pltpu.SemaphoreType.DMA((rows,)),
            pltpu.SemaphoreType.DMA((rows,)),
        ],
        compiler_params=pltpu.CompilerParams(
            collective_id=1, has_side_effects=True, vmem_limit_bytes=60 * 1024 * 1024
        ),
    )(hidden, weights)


def body(tokens, norm_gain, expert_ids, gate_weights, w_gate, w_up, w_down):
    chips = lax.psum(1, "chip")
    width = tokens.shape[1]
    core = lax.axis_index("core")

    picker, slot_index = route_tables(expert_ids, EXPERTS, CAP)
    packed = jnp.einsum("ts,td->sd", picker, tokens, preferred_element_type=jnp.float32).astype(
        jnp.bfloat16
    )
    packed = packed.reshape(EXPERTS, CAP, width)
    hidden = expert_in(packed, norm_gain, w_gate[0], w_up[0], chips)
    returned = scatter_cols(hidden, w_down[0], width, EXPERTS)
    mixed = combine_rows(returned.reshape(-1, width), slot_index, gate_weights)
    return (tokens.astype(jnp.float32) + mixed).astype(jnp.bfloat16)


def solution(mesh):
    rows, cols = mesh.devices.shape
    split_mesh = Mesh(mesh.devices.reshape(rows, cols // 2, 2), ("row", "chip", "core"))
    placed = (
        P("row", COL),
        P(),
        P("row", None),
        P("row", None),
        P("row", None, COL),
        P("row", None, COL),
        P("row", COL, None),
    )
    return jax.shard_map(
        body, mesh=split_mesh, in_specs=placed, out_specs=P("row", COL), check_vma=False
    )
```

```python
import functools

import jax
import jax.numpy as jnp
from jax import lax
from jax.experimental import pallas as pl
from jax.experimental.pallas import tpu as pltpu
from jax.sharding import Mesh
from jax.sharding import PartitionSpec as P

EXPERTS = 8
CAP = 128
COL = ("chip", "core")
MESH = pl.DeviceIdType.MESH
PIECES = 4


def normalize(rows, norm_gain):
    values = rows.astype(jnp.float32)
    inverse_norm = lax.rsqrt(jnp.mean(values * values, axis=-1, keepdims=True) + 1e-05)
    return (values * inverse_norm * norm_gain).astype(jnp.bfloat16)


def route_tables(expert_ids, expert_count, capacity):
    token_count = expert_ids.shape[0]
    flat_ids = expert_ids.reshape(-1)
    expert_range = jnp.arange(expert_count, dtype=jnp.int32)
    expert_hits = (flat_ids[:, None] == expert_range[None, :]).astype(jnp.int32)
    earlier = jnp.cumsum(expert_hits, axis=0) - expert_hits
    ranks = jnp.sum(earlier * expert_hits, axis=1)
    slot_index = (flat_ids * capacity + ranks).reshape(token_count, -1)
    slot_ids = jnp.arange(expert_count * capacity, dtype=jnp.int32)
    matches = (slot_index[:, :, None] == slot_ids[None, None, :]).astype(jnp.float32)
    picker = jnp.sum(matches, axis=1)
    return (picker.astype(jnp.bfloat16), slot_index)


def combine_rows(slot_rows, slot_index, gate_weights):
    picked = slot_rows[slot_index]
    return jnp.sum(picked * gate_weights[:, :, None], axis=1)


def expert_in_kernel(width, packed, gain_in, w_gate_hbm, w_up_hbm, hidden, src, squares_part, xs,
                     w_gate, w_up, gain, acc_gate, acc_up, squares, send_sem, recv_sem, local_sem,
                     weight_sem, square_send, square_recv, come_send, come_recv):
    row, me, core = lax.axis_index("row"), lax.axis_index("chip"), lax.axis_index("core")
    side, y = me // 4, me % 4
    partner = lax.rem(me + 4, 8)
    up = side * 4 + lax.rem(y + 1, 4)
    down = side * 4 + lax.rem(y + 3, 4)
    across = side * 4 + lax.rem(y + 2, 4)
    sister = 1 - core
    slots = xs.shape[0]
    step = 256
    blocks = squares.shape[0]
    mine = me * 2 + core
    chips = (me, partner, down, up, far(down), far(up), across, far(across))
    features = [(chip * 2 + core) * width for chip in chips]
    features += [(chip * 2 + sister) * width for chip in chips]

    loads = []
    for place, start in enumerate(features):
        rows = pl.ds(pl.multiple_of(start, width), width)
        for index, (source, target) in enumerate(((w_gate_hbm, w_gate), (w_up_hbm, w_up))):
            load = pltpu.make_async_copy(source.at[rows, :], target.at[pl.ds(place * width, width), :],
                                         weight_sem.at[index, place])
            load.start()
            loads.append(load)
        gain[:, pl.ds(place * width, width)] = gain_in[:, rows]

    rows, depth = packed.shape[0], packed.shape[1]
    barrier = pltpu.get_barrier_semaphore()
    for d in range(1, blocks):
        other = lax.rem(mine + d, blocks)
        pl.semaphore_signal(barrier, inc=1, device_id=(row, other // 2, other % 2),
                            device_id_type=MESH)
    for d in range(1, rows):
        pl.semaphore_signal(barrier, inc=1, device_id=(lax.rem(row + d, rows), me, core),
                            device_id_type=MESH)
    pl.semaphore_wait(barrier, blocks - 1 + rows - 1)

    def rows_of(r):
        return pl.ds(pl.multiple_of(r * depth, depth), depth)

    comes = []
    for d in range(1, rows):
        target = lax.rem(row + d, rows)
        come = pltpu.make_async_remote_copy(
            src_ref=packed.at[target], dst_ref=src.at[rows_of(row), :],
            send_sem=come_send.at[d], recv_sem=come_recv.at[d],
            device_id=(target, me, core), device_id_type=MESH,
        )
        come.start()
        comes.append(come)
    src[rows_of(row), :] = packed[row]
    for come in comes:
        come.wait_recv()

    def sum_squares(i, carry):
        part = pl.ds(pl.multiple_of(i * step, step), step)
        values = src[part, :].astype(jnp.float32)
        total = jnp.sum(values * values, axis=1, keepdims=True)
        squares_part[pl.ds(i, 1), :] = jnp.transpose(jnp.broadcast_to(total, (step, 128)))[0:1, :]
        return carry

    lax.fori_loop(0, slots // step, sum_squares, 0)

    square_copies = []
    for d in range(1, blocks):
        other = lax.rem(mine + d, blocks)
        copy = pltpu.make_async_remote_copy(
            src_ref=squares_part, dst_ref=squares.at[mine], send_sem=square_send.at[d],
            recv_sem=square_recv.at[d], device_id=(row, other // 2, other % 2),
            device_id_type=MESH,
        )
        copy.start()
        square_copies.append(copy)

    half_rows = slots // PIECES

    def rows_half(h):
        return pl.ds(h * half_rows, half_rows)

    def place(p, h=None):
        if h is None:
            return xs.at[:, pl.ds(p * width, width)]
        return xs.at[rows_half(h), pl.ds(p * width, width)]

    def send(tag, source, target, chip, half, h):
        origin = src.at[rows_half(h), :] if source is None else place(source, h)
        copy = pltpu.make_async_remote_copy(
            src_ref=origin, dst_ref=place(target, h), send_sem=send_sem.at[tag, h],
            recv_sem=recv_sem.at[tag, h], device_id=(row, chip, half), device_id_type=MESH,
        )
        copy.start()
        return copy

    def arrive(tag, target, h):
        pltpu.make_async_remote_copy(
            src_ref=place(target, h), dst_ref=place(target, h), send_sem=send_sem.at[tag, h],
            recv_sem=recv_sem.at[tag, h], device_id=(row, me, sister), device_id_type=MESH,
        ).wait_recv()

    sent = []
    for h in range(PIECES):
        sent += [send(0, None, 1, partner, core, h), send(1, None, 2, up, core, h),
                 send(2, None, 3, down, core, h), send(7, None, 8, me, sister, h)]
    local = pltpu.make_async_copy(src, place(0), local_sem)
    local.start()
    squares[mine] = squares_part[...]
    for copy in square_copies:
        copy.wait_recv()
    total = squares[0]
    for b in range(1, blocks):
        total = total + squares[b]
    squares[0] = lax.rsqrt(total / (blocks * width) + 1e-05)

    for h in range(PIECES):
        arrive(0, 1, h)
        sent += [send(3, 1, 4, up, core, h), send(4, 1, 5, down, core, h),
                 send(8, 1, 9, me, sister, h)]
        arrive(1, 2, h)
        sent += [send(5, 2, 6, up, core, h), send(9, 2, 10, me, sister, h)]
        arrive(2, 3, h)
        sent.append(send(10, 3, 11, me, sister, h))
    for load in loads:
        load.wait()
    local.wait()

    def absorb(first_place, first=False, rows_part=None):
        cols = pl.ds(first_place * width, 4 * width)
        scale = gain[:, cols]

        def one(i, carry):
            part = pl.ds(pl.multiple_of(i * step, step), step)
            spread = jnp.broadcast_to(squares[0, pl.ds(i, 1), :], (128, step))
            column = jnp.transpose(spread)[:, 0:1]
            values = xs[part, cols].astype(jnp.float32)
            normed = (values * column * scale).astype(jnp.bfloat16)
            gate_part = jnp.dot(normed, w_gate[cols, :], preferred_element_type=jnp.float32)
            up_part = jnp.dot(normed, w_up[cols, :], preferred_element_type=jnp.float32)
            if first:
                acc_gate[part, :] = gate_part
                acc_up[part, :] = up_part
            else:
                acc_gate[part, :] += gate_part
                acc_up[part, :] += up_part
            return carry

        chunks = slots // step
        if rows_part is None:
            lax.fori_loop(0, chunks, one, 0)
        else:
            lax.fori_loop(rows_part * chunks // PIECES, (rows_part + 1) * chunks // PIECES, one, 0)

    absorb(0, first=True)
    for h in range(PIECES):
        arrive(3, 4, h)
        sent.append(send(11, 4, 12, me, sister, h))
        arrive(4, 5, h)
        sent += [send(6, 5, 7, down, core, h), send(12, 5, 13, me, sister, h)]
        arrive(5, 6, h)
        sent.append(send(13, 6, 14, me, sister, h))
        arrive(6, 7, h)
        sent.append(send(14, 7, 15, me, sister, h))
    absorb(4)
    for first_place in (8, 12):
        for h in range(PIECES):
            for tag in range(first_place - 1, first_place + 3):
                arrive(tag, tag + 1, h)
            absorb(first_place, rows_part=h)

    def finish(i, carry):
        part = pl.ds(pl.multiple_of(i * step, step), step)
        gate_values = acc_gate[part, :]
        silu = gate_values / (1.0 + jnp.exp(-gate_values))
        hidden[part, :] = (silu * acc_up[part, :]).astype(hidden.dtype)
        return carry

    lax.fori_loop(0, slots // step, finish, 0)
    for copy in sent + square_copies + comes:
        copy.wait_send()


def far(chip):
    return lax.rem(chip + 4, 8)


def expert_in(packed, norm_gain, w_gate, w_up, chips):
    rows, depth, width = packed.shape
    slots = rows * depth
    blocks = chips * 2
    features = blocks * width
    hidden_units = w_gate.shape[1]
    return pl.pallas_call(
        functools.partial(expert_in_kernel, width),
        out_shape=jax.ShapeDtypeStruct((slots, hidden_units), jnp.bfloat16),
        in_specs=[pl.BlockSpec(memory_space=pltpu.VMEM)] * 2
        + [pl.BlockSpec(memory_space=pl.ANY)] * 2,
        out_specs=pl.BlockSpec(memory_space=pltpu.VMEM),
        scratch_shapes=[
            pltpu.VMEM((slots, width), packed.dtype),
            pltpu.VMEM((slots // 256, 256), jnp.float32),
            pltpu.VMEM((slots, features), jnp.bfloat16),
            pltpu.VMEM(w_gate.shape, w_gate.dtype),
            pltpu.VMEM(w_up.shape, w_up.dtype),
            pltpu.VMEM((1, features), jnp.float32),
            pltpu.VMEM((slots, hidden_units), jnp.float32),
            pltpu.VMEM((slots, hidden_units), jnp.float32),
            pltpu.VMEM((blocks, slots // 256, 256), jnp.float32),
            pltpu.SemaphoreType.DMA((15, PIECES)),
            pltpu.SemaphoreType.DMA((15, PIECES)),
            pltpu.SemaphoreType.DMA(()),
            pltpu.SemaphoreType.DMA((2, blocks)),
            pltpu.SemaphoreType.DMA((blocks,)),
            pltpu.SemaphoreType.DMA((blocks,)),
            pltpu.SemaphoreType.DMA((rows,)),
            pltpu.SemaphoreType.DMA((rows,)),
        ],
        compiler_params=pltpu.CompilerParams(
            collective_id=0, has_side_effects=True, vmem_limit_bytes=60 * 1024 * 1024
        ),
    )(packed, norm_gain.reshape(1, features), w_gate, w_up)


def project(dst, hidden, weights, start):
    rows = dst.shape[0]
    step = 256
    cols = pl.ds(pl.multiple_of(start, 256), dst.shape[1])

    def one(i, carry):
        part = pl.ds(pl.multiple_of(i * step, step), step)
        dst[part, :] = jnp.dot(hidden[part, :], weights[:, cols], preferred_element_type=jnp.float32)
        return carry

    lax.fori_loop(0, rows // step, one, 0)


def add_blocks(dst, *sources):
    rows = dst.shape[0]
    step = 128

    def one(i, carry):
        part = pl.ds(pl.multiple_of(i * step, step), step)
        total = sources[0][part, :].astype(jnp.float32)
        for source in sources[1:]:
            total = total + source[part, :].astype(jnp.float32)
        dst[part, :] = total.astype(dst.dtype)
        return carry

    lax.fori_loop(0, rows // step, one, 0)


def scatter_kernel(width, hidden, weights_hbm, returned, weights, out, mine, theirs, outgoing,
                   sending, landed, weight_sem, sister_send, sister_recv, send_sem, recv_sem,
                   back_send, back_recv):
    row, me, core = lax.axis_index("row"), lax.axis_index("chip"), lax.axis_index("core")
    sister = 1 - core
    side, y = me // 4, me % 4
    partner = lax.rem(me + 4, 8)
    up = side * 4 + lax.rem(y + 1, 4)
    down = side * 4 + lax.rem(y + 3, 4)
    across = side * 4 + lax.rem(y + 2, 4)

    def far(chip):
        return lax.rem(chip + 4, 8)

    rows = returned.shape[0]
    order = (far(down), across, up, far(across), down, far(up), partner, me)
    loads = {}
    for slot, chip in enumerate(order):
        for index, half in enumerate((sister, core)):
            cols = pl.ds(pl.multiple_of((chip * 2 + half) * width, width), width)
            load = pltpu.make_async_copy(weights_hbm.at[:, cols], weights.at[:, cols],
                                         weight_sem.at[index, slot])
            load.start()
            loads[(slot, index)] = load
    barrier = pltpu.get_barrier_semaphore()
    for chip, half in ((partner, core), (up, core), (down, core), (me, sister)):
        pl.semaphore_signal(barrier, inc=1, device_id=(row, chip, half), device_id_type=MESH)
    for d in range(1, rows):
        pl.semaphore_signal(barrier, inc=1, device_id=(lax.rem(row + d, rows), me, core),
                            device_id_type=MESH)
    pl.semaphore_wait(barrier, 4 + rows - 1)

    swaps = []

    def produce(slots, own=True):
        for slot in slots:
            loads[(slot, 0)].wait()
            project(outgoing.at[slot], hidden, weights, (order[slot] * 2 + sister) * width)
            swap = pltpu.make_async_remote_copy(
                src_ref=outgoing.at[slot], dst_ref=theirs.at[slot], send_sem=sister_send.at[slot],
                recv_sem=sister_recv.at[slot], device_id=(row, me, sister), device_id_type=MESH,
            )
            swap.start()
            swaps.append(swap)
        if own:
            for slot in slots:
                own_block(slot)

    def own_block(slot):
        loads[(slot, 1)].wait()
        project(mine.at[slot], hidden, weights, (order[slot] * 2 + core) * width)

    produce(range(4), own=False)

    def ready(slot):
        swaps[slot].wait_recv()
        return (mine.at[slot], theirs.at[slot])

    half_rows = mine.shape[1] // 2

    def cut(ref, h):
        return ref.at[pl.ds(h * half_rows, half_rows), :]

    def send(tag, chip, h):
        copy = pltpu.make_async_remote_copy(
            src_ref=cut(sending.at[tag], h), dst_ref=cut(landed.at[tag], h),
            send_sem=send_sem.at[tag, h], recv_sem=recv_sem.at[tag, h],
            device_id=(row, chip, core), device_id_type=MESH,
        )
        copy.start()
        return copy

    def arrive(tag, h):
        pltpu.make_async_remote_copy(
            src_ref=cut(sending.at[tag], h), dst_ref=cut(landed.at[tag], h),
            send_sem=send_sem.at[tag, h], recv_sem=recv_sem.at[tag, h],
            device_id=(row, me, core), device_id_type=MESH,
        ).wait_recv()

    def combine(dst, h, *sources):
        add_blocks(cut(dst, h), *[cut(source, h) for source in sources])

    sent = []
    for tag, chip in ((0, down), (1, down), (2, up), (3, up)):
        own_block(tag)
        pair = ready(tag)
        for h in (0, 1):
            combine(sending.at[tag], h, *pair)
            sent.append(send(tag, chip, h))
    produce(range(4, 8))
    pairs = [ready(slot) for slot in range(4, 8)]
    for h in (0, 1):
        arrive(1, h)
        combine(sending.at[4], h, *pairs[0], landed.at[1])
        sent.append(send(4, down, h))
        arrive(3, h)
        combine(sending.at[5], h, *pairs[1], landed.at[3])
        sent.append(send(5, up, h))
    for h in (0, 1):
        arrive(0, h)
        arrive(5, h)
        combine(sending.at[6], h, *pairs[2], landed.at[0], landed.at[5])
        sent.append(send(6, partner, h))
    for h in (0, 1):
        arrive(2, h)
        arrive(4, h)
        combine(out, h, *pairs[3], landed.at[2], landed.at[4])
    for h in (0, 1):
        arrive(6, h)
        combine(out, h, out, landed.at[6])
    depth = returned.shape[1]
    returned[row] = out[pl.ds(pl.multiple_of(row * depth, depth), depth), :]
    backs = []
    for d in range(1, rows):
        source = lax.rem(row + d, rows)
        back = pltpu.make_async_remote_copy(
            src_ref=out.at[pl.ds(pl.multiple_of(source * depth, depth), depth), :],
            dst_ref=returned.at[row], send_sem=back_send.at[d], recv_sem=back_recv.at[d],
            device_id=(source, me, core), device_id_type=MESH,
        )
        back.start()
        backs.append(back)
    for copy in sent + swaps:
        copy.wait_send()
    for back in backs:
        back.wait()


def scatter_cols(hidden, weights, width, rows):
    slots = hidden.shape[0]
    return pl.pallas_call(
        functools.partial(scatter_kernel, width),
        out_shape=jax.ShapeDtypeStruct((rows, slots // rows, width), jnp.float32),
        in_specs=[pl.BlockSpec(memory_space=pltpu.VMEM), pl.BlockSpec(memory_space=pl.ANY)],
        out_specs=pl.BlockSpec(memory_space=pltpu.VMEM),
        scratch_shapes=[
            pltpu.VMEM(weights.shape, weights.dtype),
            pltpu.VMEM((slots, width), jnp.float32),
            pltpu.VMEM((8, slots, width), jnp.float32),
            pltpu.VMEM((8, slots, width), jnp.float32),
            pltpu.VMEM((8, slots, width), jnp.float32),
            pltpu.VMEM((7, slots, width), jnp.bfloat16),
            pltpu.VMEM((7, slots, width), jnp.bfloat16),
            pltpu.SemaphoreType.DMA((2, 8)),
            pltpu.SemaphoreType.DMA((8,)),
            pltpu.SemaphoreType.DMA((8,)),
            pltpu.SemaphoreType.DMA((7, 2)),
            pltpu.SemaphoreType.DMA((7, 2)),
            pltpu.SemaphoreType.DMA((rows,)),
            pltpu.SemaphoreType.DMA((rows,)),
        ],
        compiler_params=pltpu.CompilerParams(
            collective_id=1, has_side_effects=True, vmem_limit_bytes=60 * 1024 * 1024
        ),
    )(hidden, weights)


def body(tokens, norm_gain, expert_ids, gate_weights, w_gate, w_up, w_down):
    chips = lax.psum(1, "chip")
    width = tokens.shape[1]
    core = lax.axis_index("core")

    picker, slot_index = route_tables(expert_ids, EXPERTS, CAP)
    packed = jnp.einsum("ts,td->sd", picker, tokens, preferred_element_type=jnp.float32).astype(
        jnp.bfloat16
    )
    packed = packed.reshape(EXPERTS, CAP, width)
    hidden = expert_in(packed, norm_gain, w_gate[0], w_up[0], chips)
    returned = scatter_cols(hidden, w_down[0], width, EXPERTS)
    mixed = combine_rows(returned.reshape(-1, width), slot_index, gate_weights)
    return (tokens.astype(jnp.float32) + mixed).astype(jnp.bfloat16)


def solution(mesh):
    rows, cols = mesh.devices.shape
    split_mesh = Mesh(mesh.devices.reshape(rows, cols // 2, 2), ("row", "chip", "core"))
    placed = (
        P("row", COL),
        P(),
        P("row", None),
        P("row", None),
        P("row", None, COL),
        P("row", None, COL),
        P("row", COL, None),
    )
    return jax.shard_map(
        body, mesh=split_mesh, in_specs=placed, out_specs=P("row", COL), check_vma=False
    )
```
